32 devices in a mesh: batch: 8 (over z, y), doc: 4 (over x, core).
Axes of the slice: x: 2, y: 2, z: 4, core: 2. Of those that a mesh axis runs over, the one named last changes fastest.
Arguments:
- hidden_in: bfloat16 [8, 4, 288, 768], P('batch', 'doc'), may hold values from -6 to 6
- segments: int32 [8, 4, 288], P('batch', 'doc'), may hold values from 0 to 3, as said below
- mask_pos: int32 [8, 4, 4, 8], P('batch', 'doc'), may hold values from 0 to 287, as said below
- target_ids: int32 [8, 4, 8], replicated, may hold values from 0 to 8191
- query_emb: float32 [8, 4, 128], P('batch', None, 'doc'), may hold values from -6 to 6
- doc_emb: float32 [8, 4, 4, 128], P('batch', 'doc'), may hold values from -0.9 to 0.9
- qkv_weight: bfloat16 [768, 2304], replicated, may hold values from -0.21875 to 0.21875
- query_bias: float32 [768], replicated, may hold values from -3 to 3
- value_bias: float32 [768], replicated, may hold values from -3 to 3
- out_weight: bfloat16 [768, 768], replicated, may hold values from -1.25 to 1.25
- out_bias: float32 [768], replicated, may hold values from -3 to 3
- gain_one: float32 [768], replicated, may hold values from 0.5 to 1.5
- shift_one: float32 [768], replicated, may hold values from -2 to 2
- up_weight: bfloat16 [768, 3072], replicated, may hold values from -0.21875 to 0.21875
- up_bias: float32 [3072], replicated, may hold values from -3 to 3
- down_weight: bfloat16 [3072, 768], replicated, may hold values from -0.21875 to 0.21875
- down_bias: float32 [768], replicated, may hold values from -3 to 3
- gain_two: float32 [768], replicated, may hold values from 0.5 to 1.5
- shift_two: float32 [768], replicated, may hold values from -2 to 2
- vocab: bfloat16 [8192, 768], P('batch'), may hold values from -0.4375 to 0.4375
Outputs:
- block_out: bfloat16 [8, 4, 288, 768], P('batch', 'doc')
- loss: float32 [8, 4], P('batch')
- grad_in: bfloat16 [8, 4, 288, 768], P('batch', 'doc')
- grad_query: float32 [8, 4, 128], P('batch', None, 'doc')
- grad_qkv_weight: float32 [768, 2304], P('batch')
- grad_query_bias: float32 [768], P('batch')
- grad_value_bias: float32 [768], P('batch')
- grad_out_weight: float32 [768, 768], P('batch')
- grad_out_bias: float32 [768], P('batch')
- grad_gain_one: float32 [768], P('batch')
- grad_shift_one: float32 [768], P('batch')
- grad_up_weight: float32 [768, 3072], P('batch')
- grad_up_bias: float32 [3072], P('batch')
- grad_down_weight: float32 [3072, 768], P('batch')
- grad_down_bias: float32 [768], P('batch')
- grad_gain_two: float32 [768], P('batch')
- grad_shift_two: float32 [768], P('batch')
The draws below stay inside these ranges and needn't reach their ends.
Inputs may be any that keep to these rules, and one draw needn't show every extreme that they name: `segments`: in each sequence the segment numbers never fall and every one of 0 to 3 occurs; segment q holds pair q. `mask_pos`: the 8 positions of pair q rise strictly and lie in segment q of their sequence.
All inputs are finite; a program needn't handle non-finite values.
Results may differ from the reference program's by a relative error of at most 0.025.
Values may be sent and summed in bfloat16 or wider, within the bound.
A program may use at most 128 MiB of HBM per device.

```python
import jax
import jax.numpy as jnp
from jax import lax

D = 768
HEADS = 12
HEAD_DIM = 64
FF = 3072
PROJ = 128
LEN = 288
Q_SEQ = 4
M_Q = 8
SEQS = 8
DOCS = 4
VOCAB = 8192


def pair_layout(key):
    base_len = LEN // Q_SEQ
    reach = base_len // 4
    halves = jax.random.randint(jax.random.fold_in(key, 11), (SEQS, DOCS, Q_SEQ // 2), -reach, reach + 1)
    lengths = base_len + jnp.stack([halves, -halves], -1).reshape(SEQS, DOCS, Q_SEQ)
    lengths = lengths.at[..., Q_SEQ - 1].add(LEN - base_len * Q_SEQ)
    starts = jnp.cumsum(lengths, -1) - lengths
    return (lengths.astype(jnp.int32), starts.astype(jnp.int32))


def draw_segments(key, part):
    lengths, starts = pair_layout(key)
    spots = jnp.arange(LEN, dtype=jnp.int32)
    after = (spots[None, None, None, :] >= starts[..., None]).astype(jnp.int32)
    return (jnp.sum(after, axis=2) - 1).astype(jnp.int32)


def draw_mask_pos(key, part):
    lengths, starts = pair_layout(key)
    widths = lengths // M_Q
    raw_bits = jax.random.randint(jax.random.fold_in(key, 13), (SEQS, DOCS, Q_SEQ, M_Q), 0, 1 << 20)
    offsets = raw_bits % widths[..., None]
    slots = jnp.arange(M_Q, dtype=jnp.int32)
    return (starts[..., None] + slots * widths[..., None] + offsets).astype(jnp.int32)


def plant(entries, key, least, largest):
    place = [jax.random.randint(jax.random.fold_in(key, axis), (), 0, length) for axis, length in enumerate(entries.shape)]
    main_axis = entries.shape.index(max(entries.shape))
    next_to = place[:main_axis] + [(place[main_axis] + 1) % entries.shape[main_axis]] + place[main_axis + 1:]
    return entries.at[tuple(place)].set(least).at[tuple(next_to)].set(largest)


def levels(key, extent, pieces, least, largest):
    def one(axis_at, shards_of):
        draws = jax.random.uniform(jax.random.fold_in(jax.random.fold_in(key, 6), axis_at), (shards_of,), jnp.float32, least / len(pieces), largest / len(pieces))
        return jnp.repeat(jnp.exp(draws), extent[axis_at] // shards_of).reshape((-1,) + (1,) * (len(extent) - axis_at - 1))

    loudness = one(*pieces[0])
    for cut in pieces[1:]:
        loudness = loudness * one(*cut)
    return loudness


def scatter_about(stream_key, dims, width, bound, pieces=(), held_as=jnp.bfloat16):
    drawn = width * jax.random.normal(stream_key, dims, jnp.float32)
    if pieces:
        drawn = drawn * levels(stream_key, dims, pieces, -0.22, 0.18)
    return jnp.clip(drawn, -bound, bound).astype(held_as)


def setup_inputs(seed: int = 0) -> dict:
    streams_of = jax.random.split(jax.random.key(seed), 21)
    return {
        "hidden_in": scatter_about(streams_of[0], (SEQS, DOCS, LEN, D), 1.0, 6.0, ((0, 8), (1, 4))),
        "segments": draw_segments(jax.random.fold_in(streams_of[20], 71), 0),
        "mask_pos": draw_mask_pos(jax.random.fold_in(streams_of[20], 71), 0),
        "target_ids": plant(jax.random.randint(streams_of[3], (SEQS, Q_SEQ, M_Q), 0, VOCAB), jax.random.fold_in(streams_of[3], 1), 0, VOCAB - 1).astype(jnp.int32),
        "query_emb": scatter_about(streams_of[4], (SEQS, Q_SEQ, PROJ), 1.0, 6.0, ((0, 8), (2, 4)), jnp.float32),
        "doc_emb": scatter_about(streams_of[5], (SEQS, DOCS, Q_SEQ, PROJ), 0.15, 0.9, ((0, 8), (1, 4)), jnp.float32),
        "qkv_weight": scatter_about(streams_of[6], (D, 3 * D), D ** -0.5, 0.21875),
        "query_bias": scatter_about(streams_of[7], (D,), 0.5, 3.0, (), jnp.float32),
        "value_bias": scatter_about(streams_of[8], (D,), 0.5, 3.0, (), jnp.float32),
        "out_weight": scatter_about(streams_of[9], (D, D), (D // 32) ** -0.5, 1.25),
        "out_bias": scatter_about(streams_of[10], (D,), 0.5, 3.0, (), jnp.float32),
        "gain_one": jnp.clip(1.0 + 0.1 * jax.random.normal(streams_of[11], (D,), jnp.float32), 0.5, 1.5),
        "shift_one": scatter_about(streams_of[12], (D,), 0.3, 2.0, (), jnp.float32),
        "up_weight": scatter_about(streams_of[13], (D, FF), D ** -0.5, 0.21875),
        "up_bias": scatter_about(streams_of[14], (FF,), 0.5, 3.0, (), jnp.float32),
        "down_weight": scatter_about(streams_of[15], (FF, D), (FF // 4) ** -0.5, 0.21875),
        "down_bias": scatter_about(streams_of[16], (D,), 0.5, 3.0, (), jnp.float32),
        "gain_two": jnp.clip(1.0 + 0.1 * jax.random.normal(streams_of[17], (D,), jnp.float32), 0.5, 1.5),
        "shift_two": scatter_about(streams_of[18], (D,), 0.3, 2.0, (), jnp.float32),
        "vocab": scatter_about(streams_of[19], (VOCAB, D), (D // 4) ** -0.5, 0.4375, ((0, 8),)),
    }


@jax.custom_vjp
def low(v):
    return lax.optimization_barrier(v.astype(jnp.bfloat16)).astype(jnp.float32)

@jax.custom_vjp
def low_back(v):
    return v

def low_keep(v):
    return (low(v), None)

def low_pass(kept, grad):
    return (grad,)

def back_keep(v):
    return (v, None)

def back_low(kept, grad):
    return (low(grad),)
low.defvjp(low_keep, low_pass)
low_back.defvjp(back_keep, back_low)
highest = lax.Precision.HIGHEST

def norm_rows(values, gain, shift):
    centre = lax.optimization_barrier(jnp.mean(values, -1, keepdims=True))
    centred = values - centre
    spread = lax.optimization_barrier(jnp.mean(centred * centred, -1, keepdims=True))
    return centred * lax.rsqrt(spread + 1e-06) * gain + shift

def encode(hidden, segs, params):
    qkv_weight, query_bias, value_bias, out_weight, out_bias, gain_one, shift_one, up_weight, up_bias, down_weight, down_bias, gain_two, shift_two = params
    model_width = hidden.shape[-1]
    split_shape = hidden.shape[:2] + (HEADS, HEAD_DIM)
    packed = low_back(jnp.einsum('bld,de->ble', hidden, qkv_weight, precision=highest))
    queries = low(packed[..., :model_width] + query_bias).reshape(split_shape)
    key_rows = low(packed[..., model_width:2 * model_width]).reshape(split_shape)
    value_rows = low(packed[..., 2 * model_width:] + value_bias).reshape(split_shape)
    raw_scores = low_back(jnp.einsum('blhe,bmhe->bhlm', queries, key_rows, precision=highest))
    same_seg = (segs[:, :, None] == segs[:, None, :])[:, None]
    scaled = jnp.where(same_seg, raw_scores * (1.0 / jnp.sqrt(jnp.float32(HEAD_DIM))), -1e+30)
    probs = low(jax.nn.softmax(scaled, axis=-1))
    mixed_heads = jnp.einsum('bhlm,bmhe->blhe', probs, value_rows, precision=highest).reshape(hidden.shape)
    mixed_heads = low(low_back(mixed_heads))
    attended = low_back(jnp.einsum('bld,de->ble', mixed_heads, out_weight, precision=highest)) + out_bias
    first_norm = norm_rows(hidden + attended, gain_one, shift_one)
    inner_act = low_back(jnp.einsum('bld,df->blf', low(first_norm), up_weight, precision=highest)) + up_bias
    active = low(jax.nn.gelu(inner_act, approximate=False))
    second = low_back(jnp.einsum('blf,fd->bld', active, down_weight, precision=highest)) + down_bias
    return norm_rows(first_norm + second, gain_two, shift_two)

def score_group(hidden, segs, places, targets, query_rows, doc_rows, params, vocab_rows):
    final_rows = encode(hidden, segs, params)
    flat_places = places.reshape(DOCS, Q_SEQ * M_Q)
    picked = low(jnp.take_along_axis(final_rows, flat_places[:, :, None], axis=1))
    logits = low_back(jnp.einsum('brd,vd->brv', picked, vocab_rows, precision=highest))
    totals = jax.nn.logsumexp(logits, axis=-1)
    target_index = jnp.broadcast_to(targets.reshape(1, Q_SEQ * M_Q, 1), (DOCS, Q_SEQ * M_Q, 1))
    chosen = jnp.take_along_axis(logits, target_index, axis=2)[..., 0]
    reader = lax.optimization_barrier(jnp.mean((chosen - totals).reshape(DOCS, Q_SEQ, M_Q), -1))
    score = lax.optimization_barrier(jnp.sum(query_rows[None] * doc_rows, -1))
    loss = jax.nn.logsumexp(score, axis=0) - jax.nn.logsumexp(score + reader, axis=0)
    return (final_rows, loss)

def reference(hidden_in, segments, mask_pos, target_ids, query_emb, doc_emb, qkv_weight, query_bias, value_bias, out_weight, out_bias, gain_one, shift_one, up_weight, up_bias, down_weight, down_bias, gain_two, shift_two, vocab):
    params = (qkv_weight.astype(jnp.float32), query_bias, value_bias, out_weight.astype(jnp.float32), out_bias, gain_one, shift_one, up_weight.astype(jnp.float32), up_bias, down_weight.astype(jnp.float32), down_bias, gain_two, shift_two)
    vocab_rows = vocab.astype(jnp.float32)
    hidden = hidden_in.astype(jnp.float32)

    def objective(hidden_all, query_all, weights):

        def group(member):
            hid, segs, places, targets, query_rows, doc_rows = member
            return jax.checkpoint(score_group)(hid, segs, places, targets, query_rows, doc_rows, weights, vocab_rows)
        final_all, losses = lax.map(group, (hidden_all, segments, mask_pos, target_ids, query_all, doc_emb))
        return (jnp.sum(losses), (final_all, losses))
    total, backward, extra = jax.vjp(objective, hidden, query_emb, params, has_aux=True)
    final_all, losses = extra
    grad_hidden, grad_query, grad_params = backward(jnp.ones_like(total))
    return (final_all.astype(jnp.bfloat16), losses, grad_hidden.astype(jnp.bfloat16), grad_query, grad_params[0], grad_params[1], grad_params[2], grad_params[3], grad_params[4], grad_params[5], grad_params[6], grad_params[7], grad_params[8], grad_params[9], grad_params[10], grad_params[11], grad_params[12])
```

```python
from functools import partial
import itertools
import math

import jax
import jax.numpy as jnp
from jax import lax
from jax.experimental import pallas as pl
from jax.experimental.pallas import tpu as pltpu
from jax.sharding import PartitionSpec as P

HEAD_DIM = 64
MESH = pl.DeviceIdType.MESH
VMEM_BYTES = 64000000


class Spot:
    def __init__(self):
        self.at = {"batch": lax.axis_index("batch"), "doc": lax.axis_index("doc")}

    def mine(self, key):
        axis, k = key
        return lax.rem(self.at[axis] // (1 << k), 2)

    def peer(self, key):
        axis, k = key
        moved = dict(self.at)
        moved[axis] = self.at[axis] + (1 - 2 * self.mine(key)) * (1 << k)
        return (moved["batch"], moved["doc"])


def mesh_keys(nb, nd):
    batch = [("batch", k) for k in range(nb.bit_length() - 1)]
    doc = [("doc", k) for k in range(nd.bit_length() - 1)]
    return batch, doc


class Piece:
    def __init__(self, mat, col, rows, cols, lead, halve, both, spread):
        self.mat, self.col, self.rows, self.cols = mat, col, rows, cols
        self.lead, self.halve, self.both, self.spread = lead, halve, both, spread
        self.tile = (rows, cols)
        self.steps = (
            [("halve", key) for key in halve]
            + [("both", key) for key in both]
            + [("spread", key) for key in spread]
            + [("twin", ("doc", 0))]
        )
        self.width = cols * 2 ** len(spread)

    def buffers(self):
        two = [(2,) * (len(self.lead) - i - 1) + self.tile for i in range(len(self.halve))]
        two += [self.tile] * len(self.both)
        wide = (2,) * len(self.spread) + self.tile
        return [(2,) * len(self.lead) + self.tile] + two + [wide, wide]

    def bytes(self, i):
        kind, key = self.steps[i]
        unit = self.rows * self.cols * 2
        if kind == "halve":
            return unit * 2 ** (len(self.lead) - i - 1)
        return unit * (2 if kind == "twin" and self.spread else 1)


def plan_pieces(nb, nd, mats):
    batch, doc = mesh_keys(nb, nd)
    across = doc[1:]
    pieces = []
    for m, (rows, cols) in enumerate(mats):
        first = across[:1] if len(across) == 1 else []
        col = 0
        if first and cols % 256 == 0 and m == 0 or first and cols > 1024:
            wide = cols // 2 // 256 * 256 if m else 256
            chunk = 256 if wide % 512 else 512
            for _ in range(wide // chunk):
                pieces.append(
                    Piece(m, col, rows, chunk // 2, first + batch[::-1], first + batch, [], first)
                )
                col += chunk
        while col < cols:
            chunk = min(cols - col, 512)
            pieces.append(Piece(m, col, rows, chunk, batch[::-1], batch, across, []))
            col += chunk
    return pieces


def exchange_order(pieces, ready, topology):
    free = {}
    clock = [(ready[i], i, 0) for i in range(len(pieces))]
    done = []
    while clock:
        clock.sort()
        at, i, step = clock.pop(0)
        key = pieces[i].steps[step][1]
        link, weight, rate = topology[key]
        start = max(at, free.get(link, 0.0))
        end = start + pieces[i].bytes(step) * weight / rate
        free[link] = end
        done.append((end + 1.5, i, step))
        if step + 1 < len(pieces[i].steps):
            clock.append((end + 2.0, i, step + 1))
    return [(i, step) for _, i, step in sorted(done)]


class Flow:
    def __init__(self, piece, bufs, send, recv, base, spot):
        self.p, self.bufs, self.send, self.recv, self.base, self.spot = piece, bufs, send, recv, base, spot
        self.live = {}
        self.copies = []

    @property
    def grad(self):
        return self.bufs[0]

    def index(self, fixed):
        return tuple(fixed.get(key, slice(None)) for key in self.p.lead)

    def start(self, step):
        kind, key = self.p.steps[step]
        mine = self.spot.mine(key)
        n = len(self.p.halve) + len(self.p.both)
        if kind == "halve":
            src = self.bufs[0].at[self.index({**self.live, key: 1 - mine})]
            dst = self.bufs[1 + step]
        elif kind == "both":
            src = self.bufs[0].at[self.index(self.live)]
            dst = self.bufs[1 + step]
        elif kind == "spread":
            src = self.bufs[n + 1].at[mine]
            dst = self.bufs[n + 1].at[mine]
        else:
            src = self.bufs[n + 1]
            dst = self.bufs[n + 2]
        copy = pltpu.make_async_remote_copy(
            src_ref=src,
            dst_ref=dst,
            send_sem=self.send.at[self.base + step],
            recv_sem=self.recv.at[self.base + step],
            device_id=self.spot.peer(key),
            device_id_type=MESH,
        )
        copy.start()
        self.copies.append(copy)

    def finish(self, step):
        kind, key = self.p.steps[step]
        copy = self.copies[step]
        if kind == "both":
            copy.wait()
        else:
            copy.wait_recv()
        n = len(self.p.halve) + len(self.p.both)
        if kind in ("halve", "both"):
            if kind == "halve":
                self.live[key] = self.spot.mine(key)
            got = self.bufs[1 + step]
            free = [k for k in self.p.lead if k not in self.live]
            last = step + 1 == n
            for pick in itertools.product(range(2), repeat=len(free)):
                at = self.index({**self.live, **dict(zip(free, pick))})
                total = self.bufs[0][at] + got[pick]
                if last:
                    self.bufs[n + 1][tuple(self.spot.mine(k) for k in self.p.spread)] = total
                else:
                    self.bufs[0][at] = total

    def drain(self):
        for step, copy in enumerate(self.copies):
            if self.p.steps[step][0] != "both":
                copy.wait_send()


def link_table(nb, nd):
    batch, doc = mesh_keys(nb, nd)
    table = {key: (key, 2.0, 91e3) for key in batch + doc}
    table[("doc", 0)] = ("twin", 1.0, 450e3)
    if (nb, nd) == (8, 4):
        table[("batch", 1)] = ("z", 2.0, 91e3)
        table[("batch", 2)] = ("z", 4.0, 91e3)
    return table


def reduce_kernel(pieces, halves, order, n_mats, *refs):
    mats, refs = refs[:n_mats], refs[n_mats:]
    vec, refs = refs[0], refs[1:]
    outs, refs = refs[:n_mats], refs[n_mats:]
    vec_out, refs = refs[0], refs[1:]
    spot = Spot()
    nb, nd = lax.axis_size("batch"), lax.axis_size("doc")
    batch, doc = mesh_keys(nb, nd)
    keys = batch + doc
    bufs = []
    for p in pieces:
        k = len(p.buffers())
        bufs.append(refs[:k])
        refs = refs[k:]
    vec_send, vec_recv = refs[:2]
    send, recv, twin_send, twin_recv, vs, vr = refs[2:]

    barrier = pltpu.get_barrier_semaphore()
    for key in keys:
        pl.semaphore_signal(barrier, inc=1, device_id=spot.peer(key), device_id_type=MESH)
    pl.semaphore_wait(barrier, len(keys))

    core = spot.mine(("doc", 0))
    twin = spot.peer(("doc", 0))
    flows = []
    base = 0
    twins = []
    for i, p in enumerate(pieces):
        flow = Flow(p, bufs[i], send, recv, base, spot)
        base += len(p.steps)
        flows.append(flow)
        half = halves[p.mat]
        copies = []
        for j in range(2 ** len(p.spread)):
            cols = pl.ds(pl.multiple_of((1 - core) * half + p.col + j * p.cols, 128), p.cols)
            dst = flow.grad.at[j] if p.spread else flow.grad
            lead = (slice(None),) * len(batch)
            copy = pltpu.make_async_remote_copy(
                src_ref=mats[p.mat].at[lead + (slice(None), cols)],
                dst_ref=dst,
                send_sem=twin_send.at[2 * i + j],
                recv_sem=twin_recv.at[2 * i + j],
                device_id=twin,
                device_id_type=MESH,
            )
            copy.start()
            copies.append(copy)
        twins.append(copies)

    vec_now = vec[...]
    vec_copies = []

    def vec_step(i):
        vec_send[i] = vec_now.astype(jnp.bfloat16)
        copy = pltpu.make_async_remote_copy(
            src_ref=vec_send.at[i],
            dst_ref=vec_recv.at[i],
            send_sem=vs.at[i],
            recv_sem=vr.at[i],
            device_id=spot.peer(keys[i]),
            device_id_type=MESH,
        )
        copy.start()
        vec_copies.append(copy)

    vec_step(0)
    for i, p in enumerate(pieces):
        half = halves[p.mat]
        for j, copy in enumerate(twins[i]):
            copy.wait()
            cols = pl.ds(pl.multiple_of(core * half + p.col + j * p.cols, 128), p.cols)
            for pick in itertools.product(range(2), repeat=len(batch)):
                at = ((j,) if p.spread else ()) + pick
                flows[i].grad[at] = flows[i].grad[at] + mats[p.mat][pick + (slice(None), cols)]
        flows[i].start(0)
        if i + 1 < len(keys):
            vec_copies[i].wait()
            vec_now = vec_now + vec_recv[i].astype(jnp.float32)
            vec_step(i + 1)
    for i in range(len(vec_copies), len(keys) + 1):
        vec_copies[i - 1].wait()
        vec_now = vec_now + vec_recv[i - 1].astype(jnp.float32)
        if i < len(keys):
            vec_step(i)
    vec_out[...] = vec_now

    for i, step in order:
        flows[i].finish(step)
        p = pieces[i]
        if step + 1 < len(p.steps):
            flows[i].start(step + 1)
        else:
            half = halves[p.mat]
            for side, buf in ((core, bufs[i][-2]), (1 - core, bufs[i][-1])):
                for j in range(2 ** len(p.spread)):
                    cols = pl.ds(pl.multiple_of(side * half + p.col + j * p.cols, 128), p.cols)
                    outs[p.mat][:, cols] = buf[j] if p.spread else buf[...]
    for flow in flows:
        flow.drain()


def reduce_params(mats, vectors, nb, nd):
    batch, doc = mesh_keys(nb, nd)
    shares = [(m.shape[0] // nb, m.shape[1]) for m in mats]
    halves = [c // 2 for _, c in shares]
    pieces = plan_pieces(nb, nd, [(r, c // 2) for r, c in shares])
    order = exchange_order(pieces, [3.0 * i for i in range(len(pieces))], link_table(nb, nd))
    keys = batch + doc
    scratch = []
    for p in pieces:
        scratch += [pltpu.VMEM(shape, jnp.bfloat16) for shape in p.buffers()]
    scratch += [pltpu.VMEM((len(keys),) + vectors.shape, jnp.bfloat16)] * 2
    steps = sum(len(p.steps) for p in pieces)
    dma = pltpu.SemaphoreType.DMA
    scratch += [dma((steps,)), dma((steps,)), dma((2 * len(pieces),)), dma((2 * len(pieces),))]
    scratch += [dma((len(keys),)), dma((len(keys),))]
    vm = pl.BlockSpec(memory_space=pltpu.VMEM)
    return pl.pallas_call(
        partial(reduce_kernel, pieces, halves, order, len(mats)),
        out_shape=[jax.ShapeDtypeStruct(s, jnp.bfloat16) for s in shares]
        + [jax.ShapeDtypeStruct(vectors.shape, jnp.float32)],
        in_specs=[vm] * (len(mats) + 1),
        out_specs=[vm] * (len(mats) + 1),
        scratch_shapes=scratch,
        compiler_params=pltpu.CompilerParams(
            collective_id=0, has_side_effects=True, vmem_limit_bytes=VMEM_BYTES
        ),
    )(*[m.reshape((2,) * len(batch) + (m.shape[0] // nb, m.shape[1])) for m in mats], vectors)


def combined_all(x, axis, combine):
    everything = jax.tree.map(lambda part: lax.all_gather(part, axis), x)
    leading = jax.tree.map(lambda part: part[0], everything)

    def hop(k, so_far):
        return combine(so_far, jax.tree.map(lambda part: part[k], everything))

    return lax.fori_loop(1, lax.axis_size(axis), hop, leading)


def norm_rows(values, gain, shift):
    centre = jnp.mean(values, -1, keepdims=True)
    centred = values - centre
    spread = jnp.mean(centred * centred, -1, keepdims=True)
    return centred * lax.rsqrt(spread + 1e-06) * gain + shift


def lse_pair(earlier, later):
    maxima = jnp.maximum(earlier[0], later[0])
    totals = earlier[1] * jnp.exp(earlier[0] - maxima) + later[1] * jnp.exp(later[0] - maxima)
    return (maxima, totals)


def vocab_pair(earlier, later):
    return lse_pair(earlier[:2], later[:2]) + (earlier[2] + later[2],)


def place_rows(places, grads, seq_len):
    return jnp.zeros((seq_len, grads.shape[-1]), jnp.float32).at[places].add(grads)


def local(
    hidden_in,
    segments,
    mask_pos,
    target_ids,
    query_emb,
    doc_emb,
    qkv_weight,
    query_bias,
    value_bias,
    out_weight,
    out_bias,
    gain_one,
    shift_one,
    up_weight,
    up_bias,
    down_weight,
    down_bias,
    gain_two,
    shift_two,
    vocab,
):
    f32 = jnp.float32
    bf16 = jnp.bfloat16
    seq_count, _, seq_len, model_width = hidden_in.shape
    pair_count = mask_pos.shape[2]
    mask_count = mask_pos.shape[3]
    head_count = model_width // HEAD_DIM
    score_scale = 1.0 / math.sqrt(HEAD_DIM)
    split_shape = (seq_count, seq_len, head_count, HEAD_DIM)
    tokens = hidden_in.reshape(seq_count, seq_len, model_width)
    segs = segments.reshape(seq_count, seq_len)
    packed = jnp.einsum("nld,de->nle", tokens, qkv_weight, preferred_element_type=f32)
    queries = (packed[..., :model_width] + query_bias).astype(bf16).reshape(split_shape)
    key_rows = packed[..., model_width : 2 * model_width].astype(bf16).reshape(split_shape)
    value_rows = (packed[..., 2 * model_width :] + value_bias).astype(bf16).reshape(split_shape)
    same_seg = (segs[:, :, None] == segs[:, None, :])[:, None]
    raw_scores = jnp.einsum("nlhe,nmhe->nhlm", queries, key_rows, preferred_element_type=f32)

    def attend(scores_in):
        return jax.nn.softmax(jnp.where(same_seg, scores_in * score_scale, -1e30), axis=-1)

    probs, soft_back = jax.vjp(attend, raw_scores)
    probs_low = probs.astype(bf16)
    mixed_heads = jnp.einsum("nhlm,nmhe->nlhe", probs_low, value_rows, preferred_element_type=f32)
    mixed_low = mixed_heads.reshape(seq_count, seq_len, model_width).astype(bf16)
    attended = (
        jnp.einsum("nld,de->nle", mixed_low, out_weight, preferred_element_type=f32) + out_bias
    )
    first_norm, norm_back_one = jax.vjp(
        norm_rows, tokens.astype(f32) + attended, gain_one, shift_one
    )
    first_low = first_norm.astype(bf16)
    inner_act = (
        jnp.einsum("nld,df->nlf", first_low, up_weight, preferred_element_type=f32) + up_bias
    )
    active, gelu_back = jax.vjp(partial(jax.nn.gelu, approximate=False), inner_act)
    active_low = active.astype(bf16)
    second = (
        jnp.einsum("nlf,fd->nld", active_low, down_weight, preferred_element_type=f32) + down_bias
    )
    final_rows, norm_back_two = jax.vjp(norm_rows, first_norm + second, gain_two, shift_two)
    per_seq = pair_count * mask_count
    rows_dev = seq_count * per_seq
    flat_places = mask_pos.reshape(seq_count, per_seq)
    picked = jnp.take_along_axis(final_rows, flat_places[:, :, None], axis=1)
    picked_low = picked.reshape(rows_dev, model_width).astype(bf16)
    logits = lax.dot_general(
        lax.all_gather(picked_low, "batch", axis=0, tiled=True),
        vocab,
        (((1,), (1,)), ((), ())),
        preferred_element_type=f32,
    )
    shard_size = vocab.shape[0]
    vocab_ids = lax.axis_index("batch") * shard_size + lax.iota(jnp.int32, shard_size)
    is_target = target_ids.reshape(-1)[:, None] == vocab_ids[None, :]
    maxima = jnp.max(logits, 1)
    totals = jnp.sum(jnp.exp(logits - maxima[:, None]), 1)
    chosen = jnp.sum(jnp.where(is_target, logits, 0.0), 1)
    maxima, totals, chosen = combined_all((maxima, totals, chosen), "batch", vocab_pair)
    log_total = maxima + jnp.log(totals)
    first_own = lax.axis_index("batch") * rows_dev
    own_logp = lax.dynamic_slice_in_dim(chosen - log_total, first_own, rows_dev)
    reader = jnp.mean(own_logp.reshape(seq_count, pair_count, mask_count), -1)
    gathered_query = lax.all_gather(query_emb, "doc", axis=2, tiled=True)
    doc_rows = doc_emb.reshape(seq_count, pair_count, doc_emb.shape[-1])
    score = jnp.sum(gathered_query * doc_rows, -1)
    joint = score + reader
    unit_terms = jnp.ones_like(score)
    score_top, score_sum = combined_all((score, unit_terms), "doc", lse_pair)
    score_total = score_top + jnp.log(score_sum)
    shifted = joint - score_total
    joint_top, joint_sum = combined_all((shifted, unit_terms), "doc", lse_pair)
    joint_total = joint_top + jnp.log(joint_sum)
    loss = -joint_total
    weight_joint = jnp.exp(shifted - joint_total)
    weight_score = jnp.exp(score - score_total)
    score_grad = weight_score - weight_joint
    grad_query = lax.psum_scatter(
        score_grad[..., None] * doc_rows, "doc", scatter_dimension=2, tiled=True
    )
    row_scale = jnp.broadcast_to(
        (weight_joint / mask_count)[..., None], (seq_count, pair_count, mask_count)
    ).reshape(rows_dev)
    all_scale = lax.all_gather(row_scale, "batch", axis=0, tiled=True)
    vocab_probs = jnp.exp(logits - log_total[:, None])
    logit_grad = (all_scale[:, None] * (vocab_probs - is_target.astype(f32))).astype(bf16)
    picked_grad = lax.psum_scatter(
        jnp.dot(logit_grad, vocab, preferred_element_type=f32).astype(jnp.bfloat16),
        "batch",
        scatter_dimension=0,
        tiled=True,
    ).astype(jnp.float32)
    final_grad = jax.vmap(partial(place_rows, seq_len=seq_len))(
        flat_places, picked_grad.reshape(seq_count, per_seq, model_width)
    )
    sum_grad, grad_gain_two, grad_shift_two = norm_back_two(final_grad)
    grad_down_bias = jnp.sum(sum_grad, (0, 1))
    second_low = sum_grad.astype(bf16)
    grad_down_weight = jnp.einsum("nlf,nld->fd", active_low, second_low, preferred_element_type=f32)
    active_grad = jnp.einsum("nld,fd->nlf", second_low, down_weight, preferred_element_type=f32)
    (inner_grad,) = gelu_back(active_grad)
    grad_up_bias = jnp.sum(inner_grad, (0, 1))
    inner_low = inner_grad.astype(bf16)
    grad_up_weight = jnp.einsum("nld,nlf->df", first_low, inner_low, preferred_element_type=f32)
    first_grad = sum_grad + jnp.einsum(
        "nlf,df->nld", inner_low, up_weight, preferred_element_type=f32
    )
    resid_grad, grad_gain_one, grad_shift_one = norm_back_one(first_grad)
    grad_out_bias = jnp.sum(resid_grad, (0, 1))
    resid_low = resid_grad.astype(bf16)
    grad_out_weight = jnp.einsum("nld,nle->de", mixed_low, resid_low, preferred_element_type=f32)
    mixed_grad = (
        jnp.einsum("nle,de->nld", resid_low, out_weight, preferred_element_type=f32)
        .astype(bf16)
        .reshape(split_shape)
    )
    value_grad = jnp.einsum("nhlm,nlhe->nmhe", probs_low, mixed_grad, preferred_element_type=f32)
    prob_grad = jnp.einsum("nlhe,nmhe->nhlm", mixed_grad, value_rows, preferred_element_type=f32)
    (score_back,) = soft_back(prob_grad)
    score_low = score_back.astype(bf16)
    query_grad = jnp.einsum("nhlm,nmhe->nlhe", score_low, key_rows, preferred_element_type=f32)
    key_grad = jnp.einsum("nhlm,nlhe->nmhe", score_low, queries, preferred_element_type=f32)
    flat_shape = (seq_count, seq_len, model_width)
    query_grad = query_grad.reshape(flat_shape)
    key_grad = key_grad.reshape(flat_shape)
    value_grad = value_grad.reshape(flat_shape)
    grad_query_bias = jnp.sum(query_grad, (0, 1))
    grad_value_bias = jnp.sum(value_grad, (0, 1))
    packed_grad = jnp.concatenate([query_grad, key_grad, value_grad], -1).astype(bf16)
    grad_qkv_weight = jnp.einsum("nld,nle->de", tokens, packed_grad, preferred_element_type=f32)
    input_grad = resid_grad + jnp.einsum(
        "nle,de->nld", packed_grad, qkv_weight, preferred_element_type=f32
    )
    vectors = jnp.concatenate(
        [
            jnp.stack(
                [
                    grad_query_bias,
                    grad_value_bias,
                    grad_out_bias,
                    grad_gain_one,
                    grad_shift_one,
                    grad_down_bias,
                    grad_gain_two,
                    grad_shift_two,
                ]
            ),
            grad_up_bias.reshape(-1, model_width),
        ]
    )
    vectors = jnp.pad(vectors, ((0, -vectors.shape[0] % 16), (0, 0)))
    mats = (grad_down_weight, grad_up_weight, grad_out_weight, grad_qkv_weight)
    down_sum, up_sum, out_sum, qkv_sum, vector_sum = reduce_params(
        [m.astype(bf16) for m in mats], vectors, lax.axis_size("batch"), lax.axis_size("doc")
    )
    nb = lax.axis_size("batch")
    slot = lax.axis_index("batch")

    def share(v):
        return lax.dynamic_slice_in_dim(v, slot * (v.shape[0] // nb), v.shape[0] // nb)

    up_bias_sum = vector_sum[8 : 8 + grad_up_bias.shape[0] // model_width].reshape(-1)
    results = (
        qkv_sum.astype(f32),
        share(vector_sum[0]),
        share(vector_sum[1]),
        out_sum.astype(f32),
        share(vector_sum[2]),
        share(vector_sum[3]),
        share(vector_sum[4]),
        up_sum.astype(f32),
        share(up_bias_sum),
        down_sum.astype(f32),
        share(vector_sum[5]),
        share(vector_sum[6]),
        share(vector_sum[7]),
    )
    block_out = final_rows.astype(bf16).reshape(hidden_in.shape)
    grad_in = input_grad.astype(bf16).reshape(hidden_in.shape)
    return (
        block_out,
        loss,
        grad_in,
        grad_query,
        results[0],
        results[1],
        results[2],
        results[3],
        results[4],
        results[5],
        results[6],
        results[7],
        results[8],
        results[9],
        results[10],
        results[11],
        results[12],
    )


def solution(mesh):
    in_specs = (
        P("batch", "doc", None, None),
        P("batch", "doc", None),
        P("batch", "doc", None, None),
        P(),
        P("batch", None, "doc"),
        P("batch", "doc", None, None),
        P(),
        P(),
        P(),
        P(),
        P(),
        P(),
        P(),
        P(),
        P(),
        P(),
        P(),
        P(),
        P(),
        P("batch", None),
    )
    out_specs = (
        P("batch", "doc", None, None),
        P("batch", None),
        P("batch", "doc", None, None),
        P("batch", None, "doc"),
        P("batch", None),
        P("batch"),
        P("batch"),
        P("batch", None),
        P("batch"),
        P("batch"),
        P("batch"),
        P("batch", None),
        P("batch"),
        P("batch", None),
        P("batch"),
        P("batch"),
        P("batch"),
    )
    return jax.shard_map(local, mesh=mesh, in_specs=in_specs, out_specs=out_specs, check_vma=False)
```

```python
from functools import partial
import itertools
import math

import jax
import jax.numpy as jnp
from jax import lax
from jax.experimental import pallas as pl
from jax.experimental.pallas import tpu as pltpu
from jax.sharding import PartitionSpec as P

HEAD_DIM = 64
MESH = pl.DeviceIdType.MESH
VMEM_BYTES = 64000000


class Spot:
    def __init__(self):
        self.at = {"batch": lax.axis_index("batch"), "doc": lax.axis_index("doc")}

    def mine(self, key):
        axis, k = key
        return lax.rem(self.at[axis] // (1 << k), 2)

    def peer(self, key):
        axis, k = key
        moved = dict(self.at)
        moved[axis] = self.at[axis] + (1 - 2 * self.mine(key)) * (1 << k)
        return (moved["batch"], moved["doc"])


def mesh_keys(nb, nd):
    batch = [("batch", k) for k in range(nb.bit_length() - 1)]
    doc = [("doc", k) for k in range(nd.bit_length() - 1)]
    return batch, doc


class Piece:
    def __init__(self, mat, col, rows, cols, lead, halve, both, spread):
        self.mat, self.col, self.rows, self.cols = mat, col, rows, cols
        self.lead, self.halve, self.both, self.spread = lead, halve, both, spread
        self.tile = (rows, cols)
        self.steps = (
            [("halve", key) for key in halve]
            + [("both", key) for key in both]
            + [("spread", key) for key in spread]
            + [("twin", ("doc", 0))]
        )
        self.width = cols * 2 ** len(spread)

    def buffers(self):
        two = [(2,) * (len(self.lead) - i - 1) + self.tile for i in range(len(self.halve))]
        two += [self.tile] * len(self.both)
        wide = (2,) * len(self.spread) + self.tile
        return [(2,) * len(self.lead) + self.tile] + two + [wide, wide]

    def bytes(self, i):
        kind, key = self.steps[i]
        unit = self.rows * self.cols * 2
        if kind == "halve":
            return unit * 2 ** (len(self.lead) - i - 1)
        return unit * (2 if kind == "twin" and self.spread else 1)


def plan_pieces(nb, nd, mats):
    batch, doc = mesh_keys(nb, nd)
    across = doc[1:]
    pieces = []
    for m, (rows, cols) in enumerate(mats):
        first = across[:1] if len(across) == 1 else []
        col = 0
        if first and cols % 256 == 0 and m == 0 or first and cols > 1024:
            wide = cols // 2 // 256 * 256 if m else 256
            chunk = 256 if wide % 512 else 512
            for _ in range(wide // chunk):
                pieces.append(
                    Piece(m, col, rows, chunk // 2, first + batch[::-1], first + batch, [], first)
                )
                col += chunk
        while col < cols:
            chunk = min(cols - col, 512)
            pieces.append(Piece(m, col, rows, chunk, batch[::-1], batch, across, []))
            col += chunk
    return pieces


def exchange_order(pieces, ready, topology):
    free = {}
    clock = [(ready[i], i, 0) for i in range(len(pieces))]
    done = []
    while clock:
        clock.sort()
        at, i, step = clock.pop(0)
        key = pieces[i].steps[step][1]
        link, weight, rate = topology[key]
        start = max(at, free.get(link, 0.0))
        end = start + pieces[i].bytes(step) * weight / rate
        free[link] = end
        done.append((end + 1.5, i, step))
        if step + 1 < len(pieces[i].steps):
            clock.append((end + 2.0, i, step + 1))
    return [(i, step) for _, i, step in sorted(done)]


class Flow:
    def __init__(self, piece, bufs, send, recv, base, spot):
        self.p, self.bufs, self.send, self.recv, self.base, self.spot = piece, bufs, send, recv, base, spot
        self.live = {}
        self.copies = []

    @property
    def grad(self):
        return self.bufs[0]

    def index(self, fixed):
        return tuple(fixed.get(key, slice(None)) for key in self.p.lead)

    def start(self, step):
        kind, key = self.p.steps[step]
        mine = self.spot.mine(key)
        n = len(self.p.halve) + len(self.p.both)
        if kind == "halve":
            src = self.bufs[0].at[self.index({**self.live, key: 1 - mine})]
            dst = self.bufs[1 + step]
        elif kind == "both":
            src = self.bufs[0].at[self.index(self.live)]
            dst = self.bufs[1 + step]
        elif kind == "spread":
            src = self.bufs[n + 1].at[mine]
            dst = self.bufs[n + 1].at[mine]
        else:
            src = self.bufs[n + 1]
            dst = self.bufs[n + 2]
        copy = pltpu.make_async_remote_copy(
            src_ref=src,
            dst_ref=dst,
            send_sem=self.send.at[self.base + step],
            recv_sem=self.recv.at[self.base + step],
            device_id=self.spot.peer(key),
            device_id_type=MESH,
        )
        copy.start()
        self.copies.append(copy)

    def finish(self, step):
        kind, key = self.p.steps[step]
        copy = self.copies[step]
        if kind == "both":
            copy.wait()
        else:
            copy.wait_recv()
        n = len(self.p.halve) + len(self.p.both)
        if kind in ("halve", "both"):
            if kind == "halve":
                self.live[key] = self.spot.mine(key)
            got = self.bufs[1 + step]
            free = [k for k in self.p.lead if k not in self.live]
            last = step + 1 == n
            for pick in itertools.product(range(2), repeat=len(free)):
                at = self.index({**self.live, **dict(zip(free, pick))})
                total = self.bufs[0][at] + got[pick]
                if last:
                    self.bufs[n + 1][tuple(self.spot.mine(k) for k in self.p.spread)] = total
                else:
                    self.bufs[0][at] = total

    def drain(self):
        for step, copy in enumerate(self.copies):
            if self.p.steps[step][0] != "both":
                copy.wait_send()


def link_table(nb, nd):
    batch, doc = mesh_keys(nb, nd)
    table = {key: (key, 2.0, 91e3) for key in batch + doc}
    table[("doc", 0)] = ("twin", 1.0, 450e3)
    if (nb, nd) == (8, 4):
        table[("batch", 1)] = ("z", 2.0, 91e3)
        table[("batch", 2)] = ("z", 4.0, 91e3)
    return table


def reduce_kernel(pieces, halves, order, n_mats, *refs):
    mats, refs = refs[:n_mats], refs[n_mats:]
    vec, refs = refs[0], refs[1:]
    outs, refs = refs[:n_mats], refs[n_mats:]
    vec_out, refs = refs[0], refs[1:]
    spot = Spot()
    nb, nd = lax.axis_size("batch"), lax.axis_size("doc")
    batch, doc = mesh_keys(nb, nd)
    keys = batch + doc
    bufs = []
    for p in pieces:
        k = len(p.buffers())
        bufs.append(refs[:k])
        refs = refs[k:]
    vec_send, vec_recv = refs[:2]
    send, recv, twin_send, twin_recv, vs, vr = refs[2:]

    barrier = pltpu.get_barrier_semaphore()
    for key in keys:
        pl.semaphore_signal(barrier, inc=1, device_id=spot.peer(key), device_id_type=MESH)
    pl.semaphore_wait(barrier, len(keys))

    core = spot.mine(("doc", 0))
    twin = spot.peer(("doc", 0))
    flows = []
    base = 0
    twins = []
    for i, p in enumerate(pieces):
        flow = Flow(p, bufs[i], send, recv, base, spot)
        base += len(p.steps)
        flows.append(flow)
        half = halves[p.mat]
        copies = []
        for j in range(2 ** len(p.spread)):
            cols = pl.ds(pl.multiple_of((1 - core) * half + p.col + j * p.cols, 128), p.cols)
            dst = flow.grad.at[j] if p.spread else flow.grad
            lead = (slice(None),) * len(batch)
            copy = pltpu.make_async_remote_copy(
                src_ref=mats[p.mat].at[lead + (slice(None), cols)],
                dst_ref=dst,
                send_sem=twin_send.at[2 * i + j],
                recv_sem=twin_recv.at[2 * i + j],
                device_id=twin,
                device_id_type=MESH,
            )
            copy.start()
            copies.append(copy)
        twins.append(copies)

    vec_now = vec[...]
    vec_copies = []

    def vec_step(i):
        vec_send[i] = vec_now.astype(jnp.bfloat16)
        copy = pltpu.make_async_remote_copy(
            src_ref=vec_send.at[i],
            dst_ref=vec_recv.at[i],
            send_sem=vs.at[i],
            recv_sem=vr.at[i],
            device_id=spot.peer(keys[i]),
            device_id_type=MESH,
        )
        copy.start()
        vec_copies.append(copy)

    vec_step(0)
    for i, p in enumerate(pieces):
        half = halves[p.mat]
        for j, copy in enumerate(twins[i]):
            copy.wait()
            cols = pl.ds(pl.multiple_of(core * half + p.col + j * p.cols, 128), p.cols)
            for pick in itertools.product(range(2), repeat=len(batch)):
                at = ((j,) if p.spread else ()) + pick
                flows[i].grad[at] = flows[i].grad[at] + mats[p.mat][pick + (slice(None), cols)]
        flows[i].start(0)
        if i + 1 < len(keys):
            vec_copies[i].wait()
            vec_now = vec_now + vec_recv[i].astype(jnp.float32)
            vec_step(i + 1)
    for i in range(len(vec_copies), len(keys) + 1):
        vec_copies[i - 1].wait()
        vec_now = vec_now + vec_recv[i - 1].astype(jnp.float32)
        if i < len(keys):
            vec_step(i)
    vec_out[...] = vec_now

    for i, step in order:
        flows[i].finish(step)
        p = pieces[i]
        if step + 1 < len(p.steps):
            flows[i].start(step + 1)
        else:
            half = halves[p.mat]
            for side, buf in ((core, bufs[i][-2]), (1 - core, bufs[i][-1])):
                for j in range(2 ** len(p.spread)):
                    cols = pl.ds(pl.multiple_of(side * half + p.col + j * p.cols, 128), p.cols)
                    outs[p.mat][:, cols] = buf[j] if p.spread else buf[...]
    for flow in flows:
        flow.drain()


def reduce_params(mats, vectors, nb, nd):
    batch, doc = mesh_keys(nb, nd)
    shares = [(m.shape[0] // nb, m.shape[1]) for m in mats]
    halves = [c // 2 for _, c in shares]
    pieces = plan_pieces(nb, nd, [(r, c // 2) for r, c in shares])
    order = exchange_order(pieces, [3.0 * i for i in range(len(pieces))], link_table(nb, nd))
    keys = batch + doc
    scratch = []
    for p in pieces:
        scratch += [pltpu.VMEM(shape, jnp.bfloat16) for shape in p.buffers()]
    scratch += [pltpu.VMEM((len(keys),) + vectors.shape, jnp.bfloat16)] * 2
    steps = sum(len(p.steps) for p in pieces)
    dma = pltpu.SemaphoreType.DMA
    scratch += [dma((steps,)), dma((steps,)), dma((2 * len(pieces),)), dma((2 * len(pieces),))]
    scratch += [dma((len(keys),)), dma((len(keys),))]
    vm = pl.BlockSpec(memory_space=pltpu.VMEM)
    return pl.pallas_call(
        partial(reduce_kernel, pieces, halves, order, len(mats)),
        out_shape=[jax.ShapeDtypeStruct(s, jnp.bfloat16) for s in shares]
        + [jax.ShapeDtypeStruct(vectors.shape, jnp.float32)],
        in_specs=[vm] * (len(mats) + 1),
        out_specs=[vm] * (len(mats) + 1),
        scratch_shapes=scratch,
        compiler_params=pltpu.CompilerParams(
            collective_id=0, has_side_effects=True, vmem_limit_bytes=VMEM_BYTES
        ),
    )(*[m.reshape((2,) * len(batch) + (m.shape[0] // nb, m.shape[1])) for m in mats], vectors)


F32, BF16 = jnp.float32, jnp.bfloat16
NT = (((1,), (1,)), ((), ()))
TN = (((0,), (0,)), ((), ()))
EPS = 1e-06


def mm(a, b):
    return jnp.dot(a, b, preferred_element_type=F32)


def mm_nt(a, b):
    return lax.dot_general(a, b, NT, preferred_element_type=F32)


def mm_tn(a, b):
    return lax.dot_general(a, b, TN, preferred_element_type=F32)


def mm_exact(a, b, dims=(((1,), (0,)), ((), ()))):
    return lax.dot_general(a, b, dims, preferred_element_type=F32, precision=lax.Precision.HIGHEST)


def iota(shape, axis):
    return lax.broadcasted_iota(jnp.int32, shape, axis)


def normed(z):
    centred = z - jnp.mean(z, -1, keepdims=True)
    rstd = lax.rsqrt(jnp.mean(centred * centred, -1, keepdims=True) + EPS)
    return centred * rstd, rstd


def norm_back(grad, hat, rstd, gain):
    g = grad * gain
    inner = g - jnp.mean(g, -1, keepdims=True) - hat * jnp.mean(g * hat, -1, keepdims=True)
    return rstd * inner


def gelu(x):
    return 0.5 * x * (1.0 + lax.erf(x * math.sqrt(0.5)))


def gelu_slope(x):
    density = jnp.exp(-0.5 * x * x) * (1.0 / math.sqrt(2.0 * math.pi))
    return 0.5 * (1.0 + lax.erf(x * math.sqrt(0.5))) + x * density


def column_of(row_block):
    n, m = row_block.shape
    diag = iota((m, m), 0) == iota((m, m), 1)
    cols = [
        jnp.sum(jnp.where(diag, jnp.broadcast_to(row_block[i : i + 1, :], (m, m)), 0), 1, keepdims=True)
        for i in range(n)
    ]
    return jnp.concatenate(cols, 0)


class Net:
    def __init__(self, send, recv):
        self.send, self.recv, self.used, self.open = send, recv, 0, []

    def take(self, n=1):
        self.used += n
        return self.used - n

    def copy(self, src, dst, peer, send_at, recv_at):
        return pltpu.make_async_remote_copy(
            src_ref=src,
            dst_ref=dst,
            send_sem=self.send.at[send_at],
            recv_sem=self.recv.at[recv_at],
            device_id=peer,
            device_id_type=MESH,
        )

    def put(self, src, dst, peer, send_at, recv_at):
        copy = self.copy(src, dst, peer, send_at, recv_at)
        copy.start()
        self.open.append((None, copy))
        return copy

    def put_if(self, cond, src, dst, peer, send_at, recv_at):
        copy = self.copy(src, dst, peer, send_at, recv_at)
        pl.when(cond)(copy.start)
        self.open.append((cond, copy))
        return copy

    def drain(self):
        for cond, copy in self.open:
            if cond is None:
                copy.wait_send()
            else:
                pl.when(cond)(copy.wait_send)
        self.open = []


class Trip:
    def __init__(self, tile, lead, halve, both, spread, twin):
        self.tile, self.lead, self.halve, self.both = tile, lead, halve, both
        self.steps = [("halve", k) for k in halve] + [("both", k) for k in both]
        self.sums = len(self.steps)
        self.steps += [("spread", k) for k in spread] + ([("twin", ("doc", 0))] if twin else [])
        self.spread, self.twin = spread, twin

    def buffers(self):
        shapes = [(2,) * len(self.lead) + self.tile]
        shapes += [(2,) * (len(self.lead) - i - 1) + self.tile for i in range(len(self.halve))]
        shapes += [self.tile] * len(self.both)
        return shapes + [(2,) * (self.twin + len(self.spread)) + self.tile]

    def bytes(self, i):
        kind, key = self.steps[i]
        unit = 2 * math.prod(self.tile)
        if kind == "halve":
            return unit * 2 ** (len(self.lead) - i - 1)
        return unit * (2 ** len(self.spread) if kind == "twin" else 1)


class TripRun:
    def __init__(self, trip, bufs, net, spot):
        self.t, self.bufs, self.net, self.spot = trip, bufs, net, spot
        self.base = net.take(len(trip.steps))
        self.live, self.copies = {}, []

    @property
    def final(self):
        return self.bufs[-1]

    def at(self, fixed):
        return tuple(fixed.get(key, slice(None)) for key in self.t.lead)

    def place(self):
        return ((self.spot.mine(("doc", 0)),) if self.t.twin else ()) + tuple(
            self.spot.mine(k) for k in self.t.spread
        )

    def start(self, step):
        kind, key = self.t.steps[step]
        if kind == "halve":
            src = self.bufs[0].at[self.at({**self.live, key: 1 - self.spot.mine(key)})]
            dst = self.bufs[1 + step]
        elif kind == "both":
            src, dst = self.bufs[0].at[self.at(self.live)], self.bufs[1 + step]
        elif kind == "spread":
            src = dst = self.final.at[self.place()]
        else:
            src = dst = self.final.at[self.spot.mine(key)]
        at = self.base + step
        copy = self.net.copy(src, dst, self.spot.peer(key), at, at)
        copy.start()
        self.copies.append(copy)

    def finish(self, step):
        kind, key = self.t.steps[step]
        copy = self.copies[step]
        copy.wait_recv()
        if kind == "both":
            copy.wait_send()
        else:
            self.net.open.append((None, copy))
        if step < self.t.sums:
            if kind == "halve":
                self.live[key] = self.spot.mine(key)
            got = self.bufs[1 + step]
            free = [k for k in self.t.lead if k not in self.live]
            for pick in itertools.product(range(2), repeat=len(free)):
                at = self.at({**self.live, **dict(zip(free, pick))})
                total = self.bufs[0][at] + got[pick]
                if step + 1 == self.t.sums:
                    self.final[self.place()] = total
                else:
                    self.bufs[0][at] = total


def layer_trips(share):
    y, z0, z1, x = ("batch", 0), ("batch", 1), ("batch", 2), ("doc", 1)
    block = [Trip((share, 384), [z1, y], [y, z1], [], [x], True) for _ in range(5)]
    wide = [Trip((share, 128), [x, z1, z0, y], [x, y, z0, z1], [], [x], True) for _ in range(3)]
    small = Trip((16, 768), [], [], [y, z0, z1, x, ("doc", 0)], [], False)
    return block + wide + [small]


def layer_kernel(trips, *refs):
    (
        hidden, segs, places, targets, query, doc_rows,
        bias_q, bias_v, bias_o, gain1, shift1, bias_up, bias_down, gain2, shift2,
        qkv_hbm, out_hbm, up_hbm, down_hbm, vocab_hbm,
        block_out, loss_out, grad_in, grad_query, mats_out, wide_out, vec_out,
        wqkv, wout, wup, wdown, wvoc,
        qb, kb, vb, mixed, first_norm, first_low, acc,
        x2, x2t, kvb, kv2,
        picks, tsend, trecv, usend, urecv, ssend, srecv, logits,
        qexp, probs, probs_low,
        hints, hints_in, joint, joint_in,
        a_send, a_mixed, a1, a2, at, second_b, inner_b, rest_b, g1, g2,
        vecs,
        load_sem, send, recv, *trip_bufs,
    ) = refs
    spot = Spot()
    batch, doc = spot.at["batch"], spot.at["doc"]
    nb, nd = lax.axis_size("batch"), lax.axis_size("doc")
    core, x = spot.mine(("doc", 0)), spot.mine(("doc", 1))
    z0 = spot.mine(("batch", 1))
    rows, width = hidden.shape
    pairs, slots = places.shape
    n_pick = pairs * slots
    heads = width // HEAD_DIM
    share = width // nb
    net = Net(send, recv)

    loads = [
        pltpu.make_async_copy(qkv_hbm.at[:, pl.ds(width, 2 * width)], wqkv.at[:, pl.ds(width, 2 * width)], load_sem.at[0]),
        pltpu.make_async_copy(qkv_hbm.at[:, pl.ds(0, width)], wqkv.at[:, pl.ds(0, width)], load_sem.at[1]),
        pltpu.make_async_copy(out_hbm, wout, load_sem.at[2]),
        pltpu.make_async_copy(up_hbm, wup, load_sem.at[3]),
        pltpu.make_async_copy(down_hbm, wdown, load_sem.at[4]),
        pltpu.make_async_copy(vocab_hbm, wvoc, load_sem.at[5]),
    ]
    for load in loads:
        load.start()

    batch_peers = [(lax.rem(batch + j, nb), doc) for j in range(1, nb)]
    doc_peers = [(batch, lax.rem(doc + j, nd)) for j in range(1, nd)]
    sides = [(dx, dz) for dz in range(2) for dx in range(2)]

    def side_peer(dx, dz, to_core):
        tx = lax.rem(x + dx, 2)
        tz = lax.rem(z0 + dz, 2)
        return (batch + 2 * (tz - z0), 2 * tx + to_core), tx, tz

    far = [side_peer(1, 1, core)[0], side_peer(1, 1, 1 - core)[0], side_peer(0, 1, 1 - core)[0]]
    everyone = batch_peers + doc_peers + far
    barrier = pltpu.get_barrier_semaphore()
    for peer in everyone:
        pl.semaphore_signal(barrier, inc=1, device_id=peer, device_id_type=MESH)
    pl.semaphore_wait(barrier, len(everyone))

    own_part = query.shape[1]
    spread_lanes = (iota((own_part, own_part * nd), 0) + own_part * doc == iota((own_part, own_part * nd), 1)).astype(F32)
    hints[0:pairs, :] = mm_exact(query[...], spread_lanes)
    hints[8 : 8 + pairs, :] = doc_rows[...]
    hints_in[doc, 0:pairs, :] = hints[0:pairs, :]
    hints_in[doc, 8 : 8 + pairs, :] = hints[8 : 8 + pairs, :]
    hint_at = net.take(nd)
    hint_copies = [
        net.put(hints, hints_in.at[doc], peer, hint_at + j + 1, hint_at + j + 1) for j, peer in enumerate(doc_peers)
    ]
    twin = spot.peer(("doc", 0))
    x2_at = net.take()
    x2_copy = net.put(hidden, x2.at[pl.ds(rows, rows)], twin, x2_at, x2_at)
    x2[0:rows, :] = hidden[...]

    place_col = column_of(places[...])
    pick_bool = iota((n_pick, rows), 1) == place_col
    pick = pick_bool.astype(BF16)
    pick_f32 = pick_bool.astype(F32)
    tokens = hidden[...]
    loads[0].wait()
    kb[...] = mm(tokens, wqkv[:, width : 2 * width]).astype(BF16)
    vb[...] = (mm(tokens, wqkv[:, 2 * width :]) + bias_v[...]).astype(BF16)
    tokens_p = mm(pick, tokens).astype(BF16)
    loads[1].wait()
    query_p = (mm(tokens_p, wqkv[:, 0:width]) + bias_q[...]).astype(BF16)

    tall = heads * n_pick
    own_head = iota((tall, width), 0) // n_pick == iota((tall, width), 1) // HEAD_DIM

    def expand(v):
        return jnp.where(own_head, jnp.concatenate([v] * heads, 0), jnp.zeros((), v.dtype))

    def fold(v):
        return jnp.sum(jnp.where(own_head, v, 0.0).reshape(heads, n_pick, width), 0)

    seg_row = segs[...]
    seg_pick = jnp.sum(jnp.where(pick_bool, jnp.broadcast_to(seg_row, (n_pick, rows)), 0), 1, keepdims=True)
    same_pick = seg_pick == seg_row
    scale = 1.0 / math.sqrt(HEAD_DIM)
    qexp[...] = expand(query_p)
    scores = mm_nt(qexp[...], kb[...]) * scale
    same_tall = jnp.concatenate([same_pick.astype(F32)] * heads, 0) > 0.5
    scores = jnp.where(same_tall, scores, -1e30)
    weights = jnp.exp(scores - jnp.max(scores, -1, keepdims=True))
    weights = weights / jnp.sum(weights, -1, keepdims=True)
    probs[...] = weights
    probs_low[...] = weights.astype(BF16)
    mixed_p = fold(mm(probs_low[...], vb[...])).astype(BF16)
    loads[2].wait()
    attended = mm(mixed_p, wout[...]) + bias_o[...]
    hat1, rstd1 = normed(tokens_p.astype(F32) + attended)
    first_p = hat1 * gain1[...] + shift1[...]
    first_low_p = first_p.astype(BF16)
    loads[3].wait()
    inner_p = mm(first_low_p, wup[...]) + bias_up[...]
    active_p = gelu(inner_p).astype(BF16)
    loads[4].wait()
    second_p = mm(active_p, wdown[...]) + bias_down[...]
    hat2, rstd2 = normed(first_p + second_p)
    picks[batch] = (hat2 * gain2[...] + shift2[...]).astype(BF16)
    pick_at = net.take(nb)
    pick_copies = [
        net.put(picks.at[batch], picks.at[batch], peer, pick_at + j + 1, pick_at + j + 1)
        for j, peer in enumerate(batch_peers)
    ]

    ff = wup.shape[1]
    for k in range(2):
        for half in range(2):
            start = (2 * half + k) * 2 * (ff // nb)
            a_send[k, :, half * width : (half + 1) * width] = active_p[:, start : start + width]
    a_send[2, :, 0:width] = first_low_p
    a_send[2, :, width : 2 * width] = tokens_p
    a_mixed[...] = mixed_p
    slot = 4 * z0 + doc
    a1_at, a2_at = net.take(8), net.take(8)
    a1[slot] = a_send[(1 - core) * z0 + 2 * core]
    a2[slot] = a_mixed[...]

    def send_left(k):
        dx, dz = sides[k]
        for other in range(2):
            if k == 0 and other == 0:
                continue
            to_core = core if other == 0 else 1 - core
            peer, tx, tz = side_peer(dx, dz, to_core)
            part = a_send.at[(1 - to_core) * tz + 2 * to_core]
            net.put(part, a1.at[slot], peer, a1_at + 2 * k + other, a1_at + 2 * k + other)
            net.put(a_mixed, a2.at[slot], peer, a2_at + 2 * k + other, a2_at + 2 * k + other)

    def wait_left():
        for k in range(4):
            for other in range(2):
                if k or other:
                    i = 2 * k + other
                    net.copy(a_send.at[0], a1.at[slot], twin, a1_at + i, a1_at + i).wait_recv()
                    net.copy(a_mixed, a2.at[slot], twin, a2_at + i, a2_at + i).wait_recv()

    send_left(0)
    send_left(1)

    loads[5].wait()
    entries = wvoc.shape[0]
    target_col = jnp.concatenate([column_of(targets[j]) for j in range(nb)], 0) - batch * entries
    all_rows = nb * n_pick
    is_target = iota((all_rows, entries), 1) == target_col
    tsend[...] = mm(is_target.astype(BF16), wvoc[...]).astype(BF16).reshape(nb, n_pick, width)
    trecv[batch] = tsend[batch]
    t_at = net.take(nb)
    t_copies = [
        net.put(tsend.at[peer[0]], trecv.at[batch], peer, t_at + j + 1, t_at + j + 1)
        for j, peer in enumerate(batch_peers)
    ]

    seg_col = jnp.sum(
        jnp.where(iota((rows, rows), 0) == iota((rows, rows), 1), jnp.broadcast_to(seg_row, (rows, rows)), 0),
        1,
        keepdims=True,
    )
    qb[...] = (mm(tokens, wqkv[:, 0:width]) + bias_q[...]).astype(BF16)

    def attend(i):
        lanes = pl.ds(pl.multiple_of(i * 128, 128), 128)
        q_s, k_s, v_s = qb[:, lanes], kb[:, lanes], vb[:, lanes]
        low = iota((rows, 128), 1) < HEAD_DIM
        same = seg_col == seg_row
        parts = []
        for side in (low, ~low):
            s = mm_nt(jnp.where(side, q_s, jnp.zeros((), BF16)), k_s) * scale
            s = jnp.where(same, s, -1e30)
            e = jnp.exp(s - jnp.max(s, -1, keepdims=True))
            p = (e / jnp.sum(e, -1, keepdims=True)).astype(BF16)
            parts.append(mm(p, v_s))
        mixed[:, lanes] = jnp.where(low, parts[0], parts[1]).astype(BF16)

    pl.loop(0, width // 128)(attend)

    for copy in pick_copies:
        copy.wait_recv()
    logits[...] = mm_nt(picks[...].reshape(all_rows, width), wvoc[...])
    lg = logits[...]
    top = jnp.max(lg, 1, keepdims=True)
    chosen = jnp.sum(jnp.where(is_target, lg, 0.0), 1, keepdims=True)
    others = jnp.where(is_target, 0.0, jnp.exp(lg - top))
    total = jnp.sum(others, 1, keepdims=True)
    lane = iota((all_rows, 128), 1)
    stats = jnp.where(lane == 0, top, jnp.where(lane == 1, total, chosen))
    ssend[...] = stats.reshape(nb, n_pick, 128)
    usend[...] = mm(others.astype(BF16), wvoc[...]).astype(BF16).reshape(nb, n_pick, width)
    srecv[batch] = ssend[batch]
    urecv[batch] = usend[batch]
    s_at, u_at = net.take(nb), net.take(nb)
    s_copies, u_copies = [], []
    for j, peer in enumerate(batch_peers):
        s_copies.append(net.put(ssend.at[peer[0]], srecv.at[batch], peer, s_at + j + 1, s_at + j + 1))
        u_copies.append(net.put(usend.at[peer[0]], urecv.at[batch], peer, u_at + j + 1, u_at + j + 1))

    tokens = hidden[...]
    hat, _ = normed(tokens.astype(F32) + mm(mixed[...], wout[...]) + bias_o[...])
    first_norm[...] = hat * gain1[...] + shift1[...]
    first_low[...] = first_norm[...].astype(BF16)
    acc[...] = first_norm[...] + bias_down[...]
    chunk = 512

    def feed(i):
        cols = pl.ds(pl.multiple_of(i * chunk, chunk), chunk)
        hid = mm(first_low[...], wup[:, cols]) + bias_up[:, cols]
        acc[...] += mm(gelu(hid).astype(BF16), wdown[cols, :])

    pl.loop(0, ff // chunk)(feed)
    hat, _ = normed(acc[...])
    block_out[...] = (hat * gain2[...] + shift2[...]).astype(BF16)
    x2_copy.wait_recv()
    x2t[...] = x2[...].T

    for group in (s_copies, t_copies, u_copies):
        for copy in group:
            copy.wait_recv()
    send_left(2)
    send_left(3)
    tops = [srecv[j][:, 0:1] for j in range(nb)]
    peak = tops[0]
    for t in tops[1:]:
        peak = jnp.maximum(peak, t)
    rest = jnp.zeros_like(peak)
    chosen = jnp.zeros_like(peak)
    mixture = jnp.zeros((n_pick, width), F32)
    target_rows = jnp.zeros((n_pick, width), F32)
    for j in range(nb):
        factor = jnp.exp(tops[j] - peak)
        rest += factor * srecv[j][:, 1:2]
        chosen += srecv[j][:, 2:3]
        mixture += factor * urecv[j].astype(F32)
        target_rows += trecv[j].astype(F32)
    whole = rest + jnp.exp(chosen - peak)
    logp = chosen - peak - jnp.log(whole)
    reader = jnp.sum(jnp.broadcast_to(logp, (n_pick, 128)).reshape(pairs, slots, 128), 1) / slots
    joint[0:pairs, :] = reader
    joint_in[doc, 0:pairs, :] = reader
    joint_at = net.take(nd)
    joint_copies = [
        net.put(joint, joint_in.at[doc], peer, joint_at + j + 1, joint_at + j + 1) for j, peer in enumerate(doc_peers)
    ]
    row_grad = (mixture - rest * target_rows) / whole

    for copy in hint_copies:
        copy.wait_recv()
    full_query = hints_in[0, 0:pairs, :]
    for j in range(1, nd):
        full_query += hints_in[j, 0:pairs, :]
    docs = [hints_in[j, 8 : 8 + pairs, :] for j in range(nd)]
    score = [jnp.broadcast_to(jnp.sum(full_query * d, 1, keepdims=True), (pairs, 128)) for d in docs]
    for copy in joint_copies:
        copy.wait_recv()
    both = [s + joint_in[j, 0:pairs, :] for j, s in enumerate(score)]

    def soft(vals):
        high = vals[0]
        for v in vals[1:]:
            high = jnp.maximum(high, v)
        es = [jnp.exp(v - high) for v in vals]
        tot = es[0]
        for e in es[1:]:
            tot = tot + e
        return [e / tot for e in es], high + jnp.log(tot)

    w_score, total_score = soft(score)
    w_joint, total_joint = soft(both)
    eye = iota((pairs, 128), 0) == iota((pairs, 128), 1)
    loss_out[...] = jnp.sum(jnp.where(eye, total_score - total_joint, 0.0), 0, keepdims=True)
    query_grad = (w_score[0] - w_joint[0]) * docs[0]
    for j in range(1, nd):
        query_grad += (w_score[j] - w_joint[j]) * docs[j]
    grad_query[...] = mm_exact(query_grad, spread_lanes, NT)
    mine = w_joint[0]
    for j in range(1, nd):
        mine = jnp.where(doc == j, w_joint[j], mine)
    row_weight = jnp.broadcast_to(mine.reshape(pairs, 1, 128), (pairs, slots, 128)).reshape(n_pick, 128)[:, 0:1]
    final_grad = row_grad * (row_weight / slots)

    g1_at, g2_at = net.take(8), net.take(8)
    g1_send, g2_send = net.take(8), net.take(8)
    half_w, half_f = width // 2, ff // 2

    def send_right(src, cols, dst, to_core, send_at, recv_at):
        for k, (dx, dz) in enumerate(sides):
            peer, tx, _ = side_peer(dx, dz, to_core)
            part = src.at[:, pl.ds(pl.multiple_of(tx * cols, 128), cols)]
            land = dst.at[slot, :, pl.ds(0, cols)]
            args = (part, land, peer, send_at + 2 * k + to_core, recv_at + 2 * k + core)
            if k:
                net.put(*args)
            else:
                net.put_if(core == 1 - to_core, *args)

                def keep():
                    dst[slot, :, 0:cols] = src[:, pl.ds(pl.multiple_of(x * cols, 128), cols)]

                pl.when(core == to_core)(keep)

    def wait_right(src, cols, dst, recv_at):
        part = src.at[:, pl.ds(0, cols)]
        land = dst.at[slot, :, pl.ds(0, cols)]
        for k in range(4):
            for from_core in range(2):
                i = recv_at + 2 * k + from_core
                if k:
                    net.copy(part, land, twin, i, i).wait_recv()
        i = recv_at + 1 - core
        net.copy(part, land, twin, i, i).wait_recv()

    vecs[...] = jnp.zeros_like(vecs)
    sum_grad = norm_back(final_grad, hat2, rstd2, gain2[...])
    vecs[6:7, :] = jnp.sum(final_grad * hat2, 0, keepdims=True)
    vecs[7:8, :] = jnp.sum(final_grad, 0, keepdims=True)
    vecs[5:6, :] = jnp.sum(sum_grad, 0, keepdims=True)
    second_low = sum_grad.astype(BF16)
    second_b[...] = second_low
    send_right(second_b, half_w, g1, 0, g1_send, g1_at)
    inner_grad = mm_nt(second_low, wdown[...]) * gelu_slope(inner_p)
    inner_low = inner_grad.astype(BF16)
    inner_b[...] = inner_low
    send_right(inner_b, half_f, g1, 1, g1_send, g1_at)
    up_bias_grad = jnp.sum(inner_grad, 0, keepdims=True)
    for i in range(ff // width):
        vecs[8 + i : 9 + i, :] = up_bias_grad[:, i * width : (i + 1) * width]
    first_grad = sum_grad + mm_nt(inner_low, wup[...])
    resid_grad = norm_back(first_grad, hat1, rstd1, gain1[...])
    resid_low = resid_grad.astype(BF16)
    rest_b[0] = resid_low
    send_right(rest_b.at[0], half_w, g2, 0, g2_send, g2_at)
    vecs[3:4, :] = jnp.sum(first_grad * hat1, 0, keepdims=True)
    vecs[4:5, :] = jnp.sum(first_grad, 0, keepdims=True)
    vecs[2:3, :] = jnp.sum(resid_grad, 0, keepdims=True)
    mixed_grad = expand(mm_nt(resid_low, wout[...]).astype(BF16))
    prob_grad = mm_nt(mixed_grad, vb[...])
    value_grad = mm_tn(probs_low[...], mixed_grad)
    p = probs[...]
    score_low = (p * (prob_grad - jnp.sum(prob_grad * p, -1, keepdims=True)) * scale).astype(BF16)
    key_grad = mm_tn(score_low, qexp[...])
    kvb[0] = key_grad.astype(BF16)
    kvb[1] = value_grad.astype(BF16)
    kv_at = net.take()
    kv_copy = net.put(kvb.at[1 - core], kv2.at[pl.ds(rows, rows)], twin, kv_at, kv_at)
    kv2[0:rows, :] = kvb[core]
    query_grad_p = fold(mm(score_low, kb[...]))
    rest_b[1] = query_grad_p.astype(BF16)
    send_right(rest_b.at[1], half_w, g2, 1, g2_send, g2_at)
    vecs[0:1, :] = jnp.sum(query_grad_p, 0, keepdims=True)
    vecs[1:2, :] = jnp.sum(value_grad, 0, keepdims=True)

    runs = []
    bufs = list(trip_bufs)
    for t in trips:
        k = len(t.buffers())
        runs.append(TripRun(t, bufs[:k], net, spot))
        bufs = bufs[k:]
    runs[8].bufs[0][...] = vecs[...].astype(BF16)
    runs[8].start(0)
    wait_left()
    at[0 : 2 * width, :] = a1[...].reshape(8 * n_pick, 2 * width).T
    at[2 * width : 3 * width, :] = a2[...].reshape(8 * n_pick, width).T
    quads = [(z1, y) for z1 in range(2) for y in range(2)]

    def block(i, offsets, g, col):
        left = jnp.concatenate([at[pl.ds(pl.multiple_of(o, 32), share), :] for o in offsets], 0)
        right = g[:, :, pl.ds(col, half_w)].reshape(8 * n_pick, half_w)
        out = mm(left, right).astype(BF16)
        for n, (z1, y) in enumerate(quads):
            runs[i].bufs[0][z1, y] = out[n * share : (n + 1) * share]
        runs[i].start(0)

    pl.when(core == 0)(lambda: wait_right(second_b, half_w, g1, g1_at))
    pl.when(core == 1)(lambda: wait_right(inner_b, half_f, g1, g1_at))
    for i in range(4):
        offsets = [
            (1 - core) * ((2 * z1 + y) * 4 * share + i * share) + core * (4 * z1 + 2 * z0 + y) * share
            for z1, y in quads
        ]
        block(i, offsets, g1, pl.multiple_of(core * i * half_w, 128))

    kv_copy.wait_recv()
    for j in range(3):
        right = jnp.concatenate([kv2[:, s * half_w + 128 * j : s * half_w + 128 * (j + 1)] for s in range(2)], 1)
        out = mm(x2t[...], right).astype(BF16)
        for s in range(2):
            for b in range(nb):
                runs[5 + j].bufs[0][s, b // 4, b // 2 % 2, b % 2] = out[
                    b * share : (b + 1) * share, 128 * s : 128 * (s + 1)
                ]
        runs[5 + j].start(0)
    wait_right(rest_b.at[0], half_w, g2, g2_at)
    block(4, [2 * width - width * core + (4 * z1 + 2 * z0 + y) * share for z1, y in quads], g2, 0)

    inward = mm_nt(kvb[0], wqkv[:, width : 2 * width]) + mm_nt(kvb[1], wqkv[:, 2 * width :])
    at_rows = resid_grad + mm_nt(rest_b[1], wqkv[:, 0:width])
    grad_in[...] = (inward + mm_exact(pick_f32, at_rows, TN)).astype(BF16)

    ready = [0.0, 0.4, 0.8, 1.2, 5.0, 3.0, 3.5, 4.0, 0.0]
    for i, step in exchange_order(trips, ready, link_table(8, 4)):
        runs[i].finish(step)
        if step + 1 < len(trips[i].steps):
            runs[i].start(step + 1)
        elif i < 5:
            mats_out[i] = runs[i].final[...]
        elif i < 8:
            wide_out[i - 5] = runs[i].final[...]
        else:
            vec_out[...] = runs[i].final[...]
    net.drain()


def finish_kernel(block, grad, loss, gq, mats, wide, vec, *outs):
    (o_block, o_loss, o_grad, o_gq, o_qkv, o_qb, o_vb, o_out, o_ob, o_g1, o_s1, o_up, o_ub, o_down, o_db, o_g2, o_s2) = outs
    batch = lax.axis_index("batch")
    nb = lax.axis_size("batch")
    width = vec.shape[1]
    share, half = width // nb, width // 2
    o_block[...] = block[...]
    o_grad[...] = grad[...]
    o_loss[...] = loss[:, 0 : o_loss.shape[1]]
    o_gq[...] = gq[...]
    for s in range(2):
        cols = slice(s * half, (s + 1) * half)
        o_out[:, cols] = mats[4, 0, s].astype(F32)
        o_qkv[:, cols] = mats[4, 1, s].astype(F32)
        for i in range(4):
            o_down[i * share : (i + 1) * share, cols] = mats[i, 0, s].astype(F32)
            o_up[:, (4 * s + i) * half : (4 * s + i + 1) * half] = mats[i, 1, s].astype(F32)
        for c in range(2):
            for j in range(3):
                start = (1 + c) * width + s * half + 128 * j
                o_qkv[:, start : start + 128] = wide[j, c, s].astype(F32)
    v = vec[...].astype(F32)
    take = (iota((width, share), 0) == iota((width, share), 1) + batch * share).astype(F32)
    got = mm_exact(v, take)
    for i, o in enumerate((o_qb, o_vb, o_ob, o_g1, o_s1, o_db, o_g2, o_s2)):
        o[...] = got[i : i + 1, :]
    side = jnp.where(lax.rem(batch, 2) == 0, v[8:12, 0:half], v[8:12, half:])
    o_ub[...] = jnp.sum(jnp.where(iota((4, half), 0) == batch // 2, side, 0.0), 0, keepdims=True)


def paired_local(*args):
    (
        hidden_in, segments, mask_pos, target_ids, query_emb, doc_emb,
        qkv_weight, query_bias, value_bias, out_weight, out_bias, gain_one, shift_one,
        up_weight, up_bias, down_weight, down_bias, gain_two, shift_two, vocab,
    ) = args
    rows, width = hidden_in.shape[2:]
    pairs, slots = mask_pos.shape[2:]
    n_pick = pairs * slots
    ff = up_weight.shape[1]
    entries = vocab.shape[0]
    nb, nd = lax.axis_size("batch"), lax.axis_size("doc")
    share = width // nb
    heads = width // HEAD_DIM
    trips = layer_trips(share)
    vm, hbm = pl.BlockSpec(memory_space=pltpu.VMEM), pl.BlockSpec(memory_space=pl.ANY)

    def v(shape, dtype=BF16):
        return pltpu.VMEM(shape, dtype)

    dma = pltpu.SemaphoreType.DMA
    scratch = [
        v(qkv_weight.shape), v(out_weight.shape), v(up_weight.shape), v(down_weight.shape), v(vocab.shape),
        v((rows, width)), v((rows, width)), v((rows, width)), v((rows, width)),
        v((rows, width), F32), v((rows, width)), v((rows, width), F32),
        v((2 * rows, width)), v((width, 2 * rows)), v((2, rows, width)), v((2 * rows, width)),
        v((nb, n_pick, width)), v((nb, n_pick, width)), v((nb, n_pick, width)), v((nb, n_pick, width)),
        v((nb, n_pick, width)), v((nb, n_pick, 128), F32), v((nb, n_pick, 128), F32), v((nb * n_pick, entries), F32),
        v((heads * n_pick, width)), v((heads * n_pick, rows), F32), v((heads * n_pick, rows)),
        v((16, 128), F32), v((nd, 16, 128), F32), v((8, 128), F32), v((nd, 8, 128), F32),
        v((3, n_pick, 2 * width)), v((n_pick, width)), v((8, n_pick, 2 * width)), v((8, n_pick, width)),
        v((3 * width, 8 * n_pick)), v((n_pick, width)), v((n_pick, ff)), v((2, n_pick, width)),
        v((8, n_pick, ff // 2)), v((8, n_pick, width // 2)),
        v((16, width), F32),
        dma((6,)), dma((256,)), dma((256,)),
    ]
    for t in trips:
        scratch += [v(shape) for shape in t.buffers()]
    sds = jax.ShapeDtypeStruct
    first = pl.pallas_call(
        partial(layer_kernel, trips),
        out_shape=[
            sds((rows, width), BF16),
            sds((1, 128), F32),
            sds((rows, width), BF16),
            sds((pairs, query_emb.shape[2]), F32),
            sds((5, 2, 2, share, 384), BF16),
            sds((3, 2, 2, share, 128), BF16),
            sds((16, width), BF16),
        ],
        in_specs=[vm] * 15 + [hbm] * 5,
        out_specs=[vm] * 7,
        scratch_shapes=scratch,
        compiler_params=pltpu.CompilerParams(
            collective_id=0, has_side_effects=True, vmem_limit_bytes=VMEM_BYTES
        ),
        name="layer",
    )
    biases = (query_bias, value_bias, out_bias, gain_one, shift_one, up_bias, down_bias, gain_two, shift_two)
    block, loss, grad, gq, mats, wide, vec = first(
        hidden_in.reshape(rows, width),
        segments.reshape(1, rows),
        mask_pos.reshape(pairs, slots),
        target_ids,
        query_emb.reshape(pairs, -1),
        doc_emb.reshape(pairs, -1),
        *[b.reshape(1, -1) for b in biases],
        qkv_weight,
        out_weight,
        up_weight,
        down_weight,
        vocab,
    )
    small = sds((1, share), F32)
    outs = pl.pallas_call(
        finish_kernel,
        out_shape=[
            sds((rows, width), BF16), sds((1, pairs), F32), sds((rows, width), BF16), sds(gq.shape, F32),
            sds((share, 3 * width), F32), small, small, sds((share, width), F32), small, small, small,
            sds((share, ff), F32), sds((1, ff // nb), F32), sds((ff // nb, width), F32), small, small, small,
        ],
        in_specs=[vm] * 7,
        out_specs=[vm] * 17,
        compiler_params=pltpu.CompilerParams(vmem_limit_bytes=VMEM_BYTES),
        name="finish",
    )(block, grad, loss, gq, mats, wide, vec)
    shapes = [hidden_in.shape, (1, pairs), hidden_in.shape, query_emb.shape]
    fixed = [o.reshape(s) for o, s in zip(outs[:4], shapes)]
    return tuple(fixed + [o.reshape(-1) if o.shape[0] == 1 else o for o in outs[4:]])


def combined_all(x, axis, combine):
    everything = jax.tree.map(lambda part: lax.all_gather(part, axis), x)
    leading = jax.tree.map(lambda part: part[0], everything)

    def hop(k, so_far):
        return combine(so_far, jax.tree.map(lambda part: part[k], everything))

    return lax.fori_loop(1, lax.axis_size(axis), hop, leading)


def norm_rows(values, gain, shift):
    centre = jnp.mean(values, -1, keepdims=True)
    centred = values - centre
    spread = jnp.mean(centred * centred, -1, keepdims=True)
    return centred * lax.rsqrt(spread + 1e-06) * gain + shift


def lse_pair(earlier, later):
    maxima = jnp.maximum(earlier[0], later[0])
    totals = earlier[1] * jnp.exp(earlier[0] - maxima) + later[1] * jnp.exp(later[0] - maxima)
    return (maxima, totals)


def vocab_pair(earlier, later):
    return lse_pair(earlier[:2], later[:2]) + (earlier[2] + later[2],)


def place_rows(places, grads, seq_len):
    return jnp.zeros((seq_len, grads.shape[-1]), jnp.float32).at[places].add(grads)


def local(
    hidden_in,
    segments,
    mask_pos,
    target_ids,
    query_emb,
    doc_emb,
    qkv_weight,
    query_bias,
    value_bias,
    out_weight,
    out_bias,
    gain_one,
    shift_one,
    up_weight,
    up_bias,
    down_weight,
    down_bias,
    gain_two,
    shift_two,
    vocab,
):
    f32 = jnp.float32
    bf16 = jnp.bfloat16
    seq_count, _, seq_len, model_width = hidden_in.shape
    pair_count = mask_pos.shape[2]
    mask_count = mask_pos.shape[3]
    head_count = model_width // HEAD_DIM
    score_scale = 1.0 / math.sqrt(HEAD_DIM)
    split_shape = (seq_count, seq_len, head_count, HEAD_DIM)
    tokens = hidden_in.reshape(seq_count, seq_len, model_width)
    segs = segments.reshape(seq_count, seq_len)
    packed = jnp.einsum("nld,de->nle", tokens, qkv_weight, preferred_element_type=f32)
    queries = (packed[..., :model_width] + query_bias).astype(bf16).reshape(split_shape)
    key_rows = packed[..., model_width : 2 * model_width].astype(bf16).reshape(split_shape)
    value_rows = (packed[..., 2 * model_width :] + value_bias).astype(bf16).reshape(split_shape)
    same_seg = (segs[:, :, None] == segs[:, None, :])[:, None]
    raw_scores = jnp.einsum("nlhe,nmhe->nhlm", queries, key_rows, preferred_element_type=f32)

    def attend(scores_in):
        return jax.nn.softmax(jnp.where(same_seg, scores_in * score_scale, -1e30), axis=-1)

    probs, soft_back = jax.vjp(attend, raw_scores)
    probs_low = probs.astype(bf16)
    mixed_heads = jnp.einsum("nhlm,nmhe->nlhe", probs_low, value_rows, preferred_element_type=f32)
    mixed_low = mixed_heads.reshape(seq_count, seq_len, model_width).astype(bf16)
    attended = (
        jnp.einsum("nld,de->nle", mixed_low, out_weight, preferred_element_type=f32) + out_bias
    )
    first_norm, norm_back_one = jax.vjp(
        norm_rows, tokens.astype(f32) + attended, gain_one, shift_one
    )
    first_low = first_norm.astype(bf16)
    inner_act = (
        jnp.einsum("nld,df->nlf", first_low, up_weight, preferred_element_type=f32) + up_bias
    )
    active, gelu_back = jax.vjp(partial(jax.nn.gelu, approximate=False), inner_act)
    active_low = active.astype(bf16)
    second = (
        jnp.einsum("nlf,fd->nld", active_low, down_weight, preferred_element_type=f32) + down_bias
    )
    final_rows, norm_back_two = jax.vjp(norm_rows, first_norm + second, gain_two, shift_two)
    per_seq = pair_count * mask_count
    rows_dev = seq_count * per_seq
    flat_places = mask_pos.reshape(seq_count, per_seq)
    picked = jnp.take_along_axis(final_rows, flat_places[:, :, None], axis=1)
    picked_low = picked.reshape(rows_dev, model_width).astype(bf16)
    logits = lax.dot_general(
        lax.all_gather(picked_low, "batch", axis=0, tiled=True),
        vocab,
        (((1,), (1,)), ((), ())),
        preferred_element_type=f32,
    )
    shard_size = vocab.shape[0]
    vocab_ids = lax.axis_index("batch") * shard_size + lax.iota(jnp.int32, shard_size)
    is_target = target_ids.reshape(-1)[:, None] == vocab_ids[None, :]
    maxima = jnp.max(logits, 1)
    totals = jnp.sum(jnp.exp(logits - maxima[:, None]), 1)
    chosen = jnp.sum(jnp.where(is_target, logits, 0.0), 1)
    maxima, totals, chosen = combined_all((maxima, totals, chosen), "batch", vocab_pair)
    log_total = maxima + jnp.log(totals)
    first_own = lax.axis_index("batch") * rows_dev
    own_logp = lax.dynamic_slice_in_dim(chosen - log_total, first_own, rows_dev)
    reader = jnp.mean(own_logp.reshape(seq_count, pair_count, mask_count), -1)
    gathered_query = lax.all_gather(query_emb, "doc", axis=2, tiled=True)
    doc_rows = doc_emb.reshape(seq_count, pair_count, doc_emb.shape[-1])
    score = jnp.sum(gathered_query * doc_rows, -1)
    joint = score + reader
    unit_terms = jnp.ones_like(score)
    score_top, score_sum = combined_all((score, unit_terms), "doc", lse_pair)
    score_total = score_top + jnp.log(score_sum)
    shifted = joint - score_total
    joint_top, joint_sum = combined_all((shifted, unit_terms), "doc", lse_pair)
    joint_total = joint_top + jnp.log(joint_sum)
    loss = -joint_total
    weight_joint = jnp.exp(shifted - joint_total)
    weight_score = jnp.exp(score - score_total)
    score_grad = weight_score - weight_joint
    grad_query = lax.psum_scatter(
        score_grad[..., None] * doc_rows, "doc", scatter_dimension=2, tiled=True
    )
    row_scale = jnp.broadcast_to(
        (weight_joint / mask_count)[..., None], (seq_count, pair_count, mask_count)
    ).reshape(rows_dev)
    all_scale = lax.all_gather(row_scale, "batch", axis=0, tiled=True)
    vocab_probs = jnp.exp(logits - log_total[:, None])
    logit_grad = (all_scale[:, None] * (vocab_probs - is_target.astype(f32))).astype(bf16)
    picked_grad = lax.psum_scatter(
        jnp.dot(logit_grad, vocab, preferred_element_type=f32).astype(jnp.bfloat16),
        "batch",
        scatter_dimension=0,
        tiled=True,
    ).astype(jnp.float32)
    final_grad = jax.vmap(partial(place_rows, seq_len=seq_len))(
        flat_places, picked_grad.reshape(seq_count, per_seq, model_width)
    )
    sum_grad, grad_gain_two, grad_shift_two = norm_back_two(final_grad)
    grad_down_bias = jnp.sum(sum_grad, (0, 1))
    second_low = sum_grad.astype(bf16)
    grad_down_weight = jnp.einsum("nlf,nld->fd", active_low, second_low, preferred_element_type=f32)
    active_grad = jnp.einsum("nld,fd->nlf", second_low, down_weight, preferred_element_type=f32)
    (inner_grad,) = gelu_back(active_grad)
    grad_up_bias = jnp.sum(inner_grad, (0, 1))
    inner_low = inner_grad.astype(bf16)
    grad_up_weight = jnp.einsum("nld,nlf->df", first_low, inner_low, preferred_element_type=f32)
    first_grad = sum_grad + jnp.einsum(
        "nlf,df->nld", inner_low, up_weight, preferred_element_type=f32
    )
    resid_grad, grad_gain_one, grad_shift_one = norm_back_one(first_grad)
    grad_out_bias = jnp.sum(resid_grad, (0, 1))
    resid_low = resid_grad.astype(bf16)
    grad_out_weight = jnp.einsum("nld,nle->de", mixed_low, resid_low, preferred_element_type=f32)
    mixed_grad = (
        jnp.einsum("nle,de->nld", resid_low, out_weight, preferred_element_type=f32)
        .astype(bf16)
        .reshape(split_shape)
    )
    value_grad = jnp.einsum("nhlm,nlhe->nmhe", probs_low, mixed_grad, preferred_element_type=f32)
    prob_grad = jnp.einsum("nlhe,nmhe->nhlm", mixed_grad, value_rows, preferred_element_type=f32)
    (score_back,) = soft_back(prob_grad)
    score_low = score_back.astype(bf16)
    query_grad = jnp.einsum("nhlm,nmhe->nlhe", score_low, key_rows, preferred_element_type=f32)
    key_grad = jnp.einsum("nhlm,nlhe->nmhe", score_low, queries, preferred_element_type=f32)
    flat_shape = (seq_count, seq_len, model_width)
    query_grad = query_grad.reshape(flat_shape)
    key_grad = key_grad.reshape(flat_shape)
    value_grad = value_grad.reshape(flat_shape)
    grad_query_bias = jnp.sum(query_grad, (0, 1))
    grad_value_bias = jnp.sum(value_grad, (0, 1))
    packed_grad = jnp.concatenate([query_grad, key_grad, value_grad], -1).astype(bf16)
    grad_qkv_weight = jnp.einsum("nld,nle->de", tokens, packed_grad, preferred_element_type=f32)
    input_grad = resid_grad + jnp.einsum(
        "nle,de->nld", packed_grad, qkv_weight, preferred_element_type=f32
    )
    vectors = jnp.concatenate(
        [
            jnp.stack(
                [
                    grad_query_bias,
                    grad_value_bias,
                    grad_out_bias,
                    grad_gain_one,
                    grad_shift_one,
                    grad_down_bias,
                    grad_gain_two,
                    grad_shift_two,
                ]
            ),
            grad_up_bias.reshape(-1, model_width),
        ]
    )
    vectors = jnp.pad(vectors, ((0, -vectors.shape[0] % 16), (0, 0)))
    mats = (grad_down_weight, grad_up_weight, grad_out_weight, grad_qkv_weight)
    down_sum, up_sum, out_sum, qkv_sum, vector_sum = reduce_params(
        [m.astype(bf16) for m in mats], vectors, lax.axis_size("batch"), lax.axis_size("doc")
    )
    nb = lax.axis_size("batch")
    slot = lax.axis_index("batch")

    def share(v):
        return lax.dynamic_slice_in_dim(v, slot * (v.shape[0] // nb), v.shape[0] // nb)

    up_bias_sum = vector_sum[8 : 8 + grad_up_bias.shape[0] // model_width].reshape(-1)
    results = (
        qkv_sum.astype(f32),
        share(vector_sum[0]),
        share(vector_sum[1]),
        out_sum.astype(f32),
        share(vector_sum[2]),
        share(vector_sum[3]),
        share(vector_sum[4]),
        up_sum.astype(f32),
        share(up_bias_sum),
        down_sum.astype(f32),
        share(vector_sum[5]),
        share(vector_sum[6]),
        share(vector_sum[7]),
    )
    block_out = final_rows.astype(bf16).reshape(hidden_in.shape)
    grad_in = input_grad.astype(bf16).reshape(hidden_in.shape)
    return (
        block_out,
        loss,
        grad_in,
        grad_query,
        results[0],
        results[1],
        results[2],
        results[3],
        results[4],
        results[5],
        results[6],
        results[7],
        results[8],
        results[9],
        results[10],
        results[11],
        results[12],
    )


def solution(mesh):
    in_specs = (
        P("batch", "doc", None, None),
        P("batch", "doc", None),
        P("batch", "doc", None, None),
        P(),
        P("batch", None, "doc"),
        P("batch", "doc", None, None),
        P(),
        P(),
        P(),
        P(),
        P(),
        P(),
        P(),
        P(),
        P(),
        P(),
        P(),
        P(),
        P(),
        P("batch", None),
    )
    out_specs = (
        P("batch", "doc", None, None),
        P("batch", None),
        P("batch", "doc", None, None),
        P("batch", None, "doc"),
        P("batch", None),
        P("batch"),
        P("batch"),
        P("batch", None),
        P("batch"),
        P("batch"),
        P("batch"),
        P("batch", None),
        P("batch"),
        P("batch", None),
        P("batch"),
        P("batch"),
        P("batch"),
    )
    paired = dict(mesh.shape) == {"batch": 8, "doc": 4}
    return jax.shard_map(paired_local if paired else local, mesh=mesh, in_specs=in_specs, out_specs=out_specs, check_vma=False)
```

```python
from functools import partial
import itertools
import math

import jax
import jax.numpy as jnp
from jax import lax
from jax.experimental import pallas as pl
from jax.experimental.pallas import tpu as pltpu
from jax.sharding import PartitionSpec as P

HEAD_DIM = 64
MESH = pl.DeviceIdType.MESH
VMEM_BYTES = 64000000


class Spot:
    def __init__(self):
        self.at = {"batch": lax.axis_index("batch"), "doc": lax.axis_index("doc")}

    def mine(self, key):
        axis, k = key
        return lax.rem(self.at[axis] // (1 << k), 2)

    def others(self):
        nd = lax.axis_size("doc")
        return [(self.at["batch"], lax.rem(self.at["doc"] + j, nd)) for j in range(1, nd)]

    def peer(self, key):
        axis, k = key
        moved = dict(self.at)
        moved[axis] = self.at[axis] + (1 - 2 * self.mine(key)) * (1 << k)
        return (moved["batch"], moved["doc"])


def mesh_keys(nb, nd):
    batch = [("batch", k) for k in range(nb.bit_length() - 1)]
    doc = [("doc", k) for k in range(nd.bit_length() - 1)]
    return batch, doc


class Piece:
    def __init__(self, mat, col, rows, cols, lead, halve, both, spread):
        self.mat, self.col, self.rows, self.cols = mat, col, rows, cols
        self.lead, self.halve, self.both, self.spread = lead, halve, both, spread
        self.tile = (rows, cols)
        self.steps = (
            [("halve", key) for key in halve]
            + [("both", key) for key in both]
            + [("spread", key) for key in spread]
            + [("twin", ("doc", 0))]
        )
        self.width = cols * 2 ** len(spread)

    def buffers(self):
        two = [(2,) * (len(self.lead) - i - 1) + self.tile for i in range(len(self.halve))]
        two += [self.tile] * len(self.both)
        wide = (2,) * len(self.spread) + self.tile
        return [(2,) * len(self.lead) + self.tile] + two + [wide, wide]

    def bytes(self, i):
        kind, key = self.steps[i]
        unit = self.rows * self.cols * 2
        if kind == "halve":
            return unit * 2 ** (len(self.lead) - i - 1)
        return unit * (2 if kind == "twin" and self.spread else 1)


def plan_pieces(nb, nd, mats):
    batch, doc = mesh_keys(nb, nd)
    across = doc[1:]
    pieces = []
    for m, (rows, cols) in enumerate(mats):
        first = across[:1] if len(across) == 1 else []
        col = 0
        if first and cols % 256 == 0 and m == 0 or first and cols > 1024:
            wide = cols // 2 // 256 * 256 if m else 256
            chunk = 256 if wide % 512 else 512
            for _ in range(wide // chunk):
                pieces.append(
                    Piece(m, col, rows, chunk // 2, first + batch[::-1], first + batch, [], first)
                )
                col += chunk
        while col < cols:
            chunk = min(cols - col, 512)
            pieces.append(Piece(m, col, rows, chunk, batch[::-1], batch, across, []))
            col += chunk
    return pieces


def exchange_order(pieces, ready, topology):
    free = {}
    clock = [(ready[i], i, 0) for i in range(len(pieces))]
    done = []
    while clock:
        clock.sort()
        at, i, step = clock.pop(0)
        key = pieces[i].steps[step][1]
        link, weight, rate = topology[key]
        start = max(at, free.get(link, 0.0))
        end = start + pieces[i].bytes(step) * weight / rate
        free[link] = end
        done.append((end + 1.5, i, step))
        if step + 1 < len(pieces[i].steps):
            clock.append((end + 2.0, i, step + 1))
    return [(i, step) for _, i, step in sorted(done)]


class Flow:
    def __init__(self, piece, bufs, send, recv, base, spot):
        self.p, self.bufs, self.send, self.recv, self.base, self.spot = piece, bufs, send, recv, base, spot
        self.live = {}
        self.copies = []

    @property
    def grad(self):
        return self.bufs[0]

    def index(self, fixed):
        return tuple(fixed.get(key, slice(None)) for key in self.p.lead)

    def start(self, step):
        kind, key = self.p.steps[step]
        mine = self.spot.mine(key)
        n = len(self.p.halve) + len(self.p.both)
        if kind == "halve":
            src = self.bufs[0].at[self.index({**self.live, key: 1 - mine})]
            dst = self.bufs[1 + step]
        elif kind == "both":
            src = self.bufs[0].at[self.index(self.live)]
            dst = self.bufs[1 + step]
        elif kind == "spread":
            src = self.bufs[n + 1].at[mine]
            dst = self.bufs[n + 1].at[mine]
        else:
            src = self.bufs[n + 1]
            dst = self.bufs[n + 2]
        copy = pltpu.make_async_remote_copy(
            src_ref=src,
            dst_ref=dst,
            send_sem=self.send.at[self.base + step],
            recv_sem=self.recv.at[self.base + step],
            device_id=self.spot.peer(key),
            device_id_type=MESH,
        )
        copy.start()
        self.copies.append(copy)

    def finish(self, step):
        kind, key = self.p.steps[step]
        copy = self.copies[step]
        if kind == "both":
            copy.wait()
        else:
            copy.wait_recv()
        n = len(self.p.halve) + len(self.p.both)
        if kind in ("halve", "both"):
            if kind == "halve":
                self.live[key] = self.spot.mine(key)
            got = self.bufs[1 + step]
            free = [k for k in self.p.lead if k not in self.live]
            last = step + 1 == n
            for pick in itertools.product(range(2), repeat=len(free)):
                at = self.index({**self.live, **dict(zip(free, pick))})
                total = self.bufs[0][at] + got[pick]
                if last:
                    self.bufs[n + 1][tuple(self.spot.mine(k) for k in self.p.spread)] = total
                else:
                    self.bufs[0][at] = total

    def drain(self):
        for step, copy in enumerate(self.copies):
            if self.p.steps[step][0] != "both":
                copy.wait_send()


def link_table(nb, nd):
    batch, doc = mesh_keys(nb, nd)
    table = {key: (key, 2.0, 91e3) for key in batch + doc}
    table[("doc", 0)] = ("twin", 1.0, 450e3)
    if (nb, nd) == (8, 4):
        table[("batch", 1)] = ("z", 2.0, 91e3)
        table[("batch", 2)] = ("z", 4.0, 91e3)
    return table


def reduce_kernel(pieces, halves, order, n_mats, *refs):
    mats, refs = refs[:n_mats], refs[n_mats:]
    vec, refs = refs[0], refs[1:]
    outs, refs = refs[:n_mats], refs[n_mats:]
    vec_out, refs = refs[0], refs[1:]
    spot = Spot()
    nb, nd = lax.axis_size("batch"), lax.axis_size("doc")
    batch, doc = mesh_keys(nb, nd)
    keys = batch + doc
    bufs = []
    for p in pieces:
        k = len(p.buffers())
        bufs.append(refs[:k])
        refs = refs[k:]
    vec_send, vec_recv = refs[:2]
    send, recv, twin_send, twin_recv, vs, vr = refs[2:]

    barrier = pltpu.get_barrier_semaphore()
    for key in keys:
        pl.semaphore_signal(barrier, inc=1, device_id=spot.peer(key), device_id_type=MESH)
    pl.semaphore_wait(barrier, len(keys))

    core = spot.mine(("doc", 0))
    twin = spot.peer(("doc", 0))
    flows = []
    base = 0
    twins = []
    for i, p in enumerate(pieces):
        flow = Flow(p, bufs[i], send, recv, base, spot)
        base += len(p.steps)
        flows.append(flow)
        half = halves[p.mat]
        copies = []
        for j in range(2 ** len(p.spread)):
            cols = pl.ds(pl.multiple_of((1 - core) * half + p.col + j * p.cols, 128), p.cols)
            dst = flow.grad.at[j] if p.spread else flow.grad
            lead = (slice(None),) * len(batch)
            copy = pltpu.make_async_remote_copy(
                src_ref=mats[p.mat].at[lead + (slice(None), cols)],
                dst_ref=dst,
                send_sem=twin_send.at[2 * i + j],
                recv_sem=twin_recv.at[2 * i + j],
                device_id=twin,
                device_id_type=MESH,
            )
            copy.start()
            copies.append(copy)
        twins.append(copies)

    vec_now = vec[...]
    vec_copies = []

    def vec_step(i):
        vec_send[i] = vec_now.astype(jnp.bfloat16)
        copy = pltpu.make_async_remote_copy(
            src_ref=vec_send.at[i],
            dst_ref=vec_recv.at[i],
            send_sem=vs.at[i],
            recv_sem=vr.at[i],
            device_id=spot.peer(keys[i]),
            device_id_type=MESH,
        )
        copy.start()
        vec_copies.append(copy)

    vec_step(0)
    for i, p in enumerate(pieces):
        half = halves[p.mat]
        for j, copy in enumerate(twins[i]):
            copy.wait()
            cols = pl.ds(pl.multiple_of(core * half + p.col + j * p.cols, 128), p.cols)
            for pick in itertools.product(range(2), repeat=len(batch)):
                at = ((j,) if p.spread else ()) + pick
                flows[i].grad[at] = flows[i].grad[at] + mats[p.mat][pick + (slice(None), cols)]
        flows[i].start(0)
        if i + 1 < len(keys):
            vec_copies[i].wait()
            vec_now = vec_now + vec_recv[i].astype(jnp.float32)
            vec_step(i + 1)
    for i in range(len(vec_copies), len(keys) + 1):
        vec_copies[i - 1].wait()
        vec_now = vec_now + vec_recv[i - 1].astype(jnp.float32)
        if i < len(keys):
            vec_step(i)
    vec_out[...] = vec_now

    for i, step in order:
        flows[i].finish(step)
        p = pieces[i]
        if step + 1 < len(p.steps):
            flows[i].start(step + 1)
        else:
            half = halves[p.mat]
            for side, buf in ((core, bufs[i][-2]), (1 - core, bufs[i][-1])):
                for j in range(2 ** len(p.spread)):
                    cols = pl.ds(pl.multiple_of(side * half + p.col + j * p.cols, 128), p.cols)
                    outs[p.mat][:, cols] = buf[j] if p.spread else buf[...]
    for flow in flows:
        flow.drain()


def reduce_params(mats, vectors, nb, nd):
    batch, doc = mesh_keys(nb, nd)
    shares = [(m.shape[0] // nb, m.shape[1]) for m in mats]
    halves = [c // 2 for _, c in shares]
    pieces = plan_pieces(nb, nd, [(r, c // 2) for r, c in shares])
    order = exchange_order(pieces, [3.0 * i for i in range(len(pieces))], link_table(nb, nd))
    keys = batch + doc
    scratch = []
    for p in pieces:
        scratch += [pltpu.VMEM(shape, jnp.bfloat16) for shape in p.buffers()]
    scratch += [pltpu.VMEM((len(keys),) + vectors.shape, jnp.bfloat16)] * 2
    steps = sum(len(p.steps) for p in pieces)
    dma = pltpu.SemaphoreType.DMA
    scratch += [dma((steps,)), dma((steps,)), dma((2 * len(pieces),)), dma((2 * len(pieces),))]
    scratch += [dma((len(keys),)), dma((len(keys),))]
    vm = pl.BlockSpec(memory_space=pltpu.VMEM)
    return pl.pallas_call(
        partial(reduce_kernel, pieces, halves, order, len(mats)),
        out_shape=[jax.ShapeDtypeStruct(s, jnp.bfloat16) for s in shares]
        + [jax.ShapeDtypeStruct(vectors.shape, jnp.float32)],
        in_specs=[vm] * (len(mats) + 1),
        out_specs=[vm] * (len(mats) + 1),
        scratch_shapes=scratch,
        compiler_params=pltpu.CompilerParams(
            collective_id=0, has_side_effects=True, vmem_limit_bytes=VMEM_BYTES
        ),
    )(*[m.reshape((2,) * len(batch) + (m.shape[0] // nb, m.shape[1])) for m in mats], vectors)


F32, BF16 = jnp.float32, jnp.bfloat16
NT = (((1,), (1,)), ((), ()))
TN = (((0,), (0,)), ((), ()))
EPS = 1e-06


def mm(a, b):
    return jnp.dot(a, b, preferred_element_type=F32)


def mm_nt(a, b):
    return lax.dot_general(a, b, NT, preferred_element_type=F32)


def mm_tn(a, b):
    return lax.dot_general(a, b, TN, preferred_element_type=F32)


def mm_exact(a, b, dims=(((1,), (0,)), ((), ()))):
    return lax.dot_general(a, b, dims, preferred_element_type=F32, precision=lax.Precision.HIGHEST)


def iota(shape, axis):
    return lax.broadcasted_iota(jnp.int32, shape, axis)


def normed(z):
    centred = z - jnp.mean(z, -1, keepdims=True)
    rstd = lax.rsqrt(jnp.mean(centred * centred, -1, keepdims=True) + EPS)
    return centred * rstd, rstd


def norm_back(grad, hat, rstd, gain):
    g = grad * gain
    inner = g - jnp.mean(g, -1, keepdims=True) - hat * jnp.mean(g * hat, -1, keepdims=True)
    return rstd * inner


def gelu(x):
    return 0.5 * x * (1.0 + lax.erf(x * math.sqrt(0.5)))


def gelu_slope(x):
    density = jnp.exp(-0.5 * x * x) * (1.0 / math.sqrt(2.0 * math.pi))
    return 0.5 * (1.0 + lax.erf(x * math.sqrt(0.5))) + x * density


def column_of(row_block):
    n, m = row_block.shape
    diag = iota((m, m), 0) == iota((m, m), 1)
    cols = [
        jnp.sum(jnp.where(diag, jnp.broadcast_to(row_block[i : i + 1, :], (m, m)), 0), 1, keepdims=True)
        for i in range(n)
    ]
    return jnp.concatenate(cols, 0)


class Net:
    def __init__(self, send, recv):
        self.send, self.recv, self.sends, self.recvs, self.open, self.due = send, recv, 0, 0, [], {}

    def branch(self):
        twin = Net(self.send, self.recv)
        twin.open = list(self.open)
        twin.due = {k: list(v) for k, v in self.due.items()}
        return twin

    def take(self):
        self.sends += 1
        self.recvs += 1
        return self.sends - 1, self.recvs - 1

    def copy(self, src, dst, peer, at):
        return pltpu.make_async_remote_copy(
            src_ref=src,
            dst_ref=dst,
            send_sem=self.send.at[at[0]],
            recv_sem=self.recv.at[at[1]],
            device_id=peer,
            device_id_type=MESH,
        )

    def put(self, src, dst, peer, at):
        self.copy(src, dst, peer, at).start()

    def group(self, due, copies, whole):
        at = self.take()
        for src, dst, peer in copies:
            self.put(src, dst, peer, at)
        all_of = self.copy(whole(len(copies)), whole(len(copies)), copies[0][2], at)
        self.expect(due, all_of.wait_recv)
        self.open.append(all_of.wait_send)

    def expect(self, due, wait):
        self.due.setdefault(due, []).append(wait)

    def collect(self, due):
        for wait in self.due.pop(due):
            wait()

    def drain(self):
        for wait in self.open:
            wait()
        self.open = []


class Trip:
    def __init__(self, tile, lead, halve, both, end):
        self.tile, self.lead, self.halve, self.both = tile, lead, halve, both
        self.steps = [("halve", k) for k in halve] + [("both", k) for k in both]
        self.sums = len(self.steps)
        ends = {"": [], "two": [("spread", ("doc", 1)), ("twin", ("doc", 0))], "three": [("three", None)]}
        self.steps += ends[end]
        self.end = end

    def buffers(self):
        shapes = [(2,) * len(self.lead) + self.tile]
        shapes += [(2,) * (len(self.lead) - i - 1) + self.tile for i in range(len(self.halve))]
        shapes += [self.tile] * len(self.both)
        return shapes + [((2, 2) if self.end else ()) + self.tile]

    def bytes(self, i):
        kind, key = self.steps[i]
        unit = 2 * math.prod(self.tile)
        if kind == "halve":
            return unit * 2 ** (len(self.lead) - i - 1)
        return unit * {"twin": 2, "three": 2}.get(kind, 1)


class TripRun:
    def __init__(self, trip, bufs, sems, net, spot):
        self.t, self.bufs, self.at_step, self.net, self.spot = trip, bufs, sems, net, spot
        self.live = {}

    @property
    def final(self):
        return self.bufs[-1]

    def at(self, fixed):
        return tuple(fixed.get(key, slice(None)) for key in self.t.lead)

    def place(self):
        return (self.spot.mine(("doc", 0)), self.spot.mine(("doc", 1))) if self.t.end else ()

    def start(self, step):
        kind, key = self.t.steps[step]
        if kind == "three":
            mine = self.final.at[self.place()]
            sem = self.at_step[step]
            for peer in self.spot.others():
                self.net.put(mine, mine, peer, sem)
            pair, one = self.final.at[0], self.final.at[0, 0]
            peer = self.spot.peer(("doc", 0))
            for view in (pair, one):
                copy = self.net.copy(view, view, peer, sem)
                self.net.expect(sem, copy.wait_recv)
                self.net.open.append(copy.wait_send)
            return
        if kind == "halve":
            src = self.bufs[0].at[self.at({**self.live, key: 1 - self.spot.mine(key)})]
            dst = self.bufs[1 + step]
        elif kind == "both":
            src, dst = self.bufs[0].at[self.at(self.live)], self.bufs[1 + step]
        elif kind == "spread":
            src = dst = self.final.at[self.place()]
        else:
            src = dst = self.final.at[self.spot.mine(key)]
        at = self.at_step[step]
        copy = self.net.copy(src, dst, self.spot.peer(key), at)
        copy.start()
        self.net.expect(at, copy.wait_recv)
        if kind == "both":
            self.net.expect(at, copy.wait_send)
        else:
            self.net.open.append(copy.wait_send)

    def finish(self, step):
        kind, key = self.t.steps[step]
        self.net.collect(self.at_step[step])
        if step < self.t.sums:
            if kind == "halve":
                self.live[key] = self.spot.mine(key)
            got = self.bufs[1 + step]
            free = [k for k in self.t.lead if k not in self.live]
            for pick in itertools.product(range(2), repeat=len(free)):
                at = self.at({**self.live, **dict(zip(free, pick))})
                total = self.bufs[0][at] + got[pick]
                if step + 1 == self.t.sums:
                    self.final[self.place()] = total
                else:
                    self.bufs[0][at] = total


ALONG_Z = 2


def layer_trips(share):
    y, z0, z1, x = ("batch", 0), ("batch", 1), ("batch", 2), ("doc", 1)
    block = [Trip((share, 384), [z1, y], [y, z1], [], "two") for _ in range(ALONG_Z)]
    block += [Trip((share, 384), [z1, z0], [z0, z1], [], "two") for _ in range(4 - ALONG_Z)]
    block += [Trip((share, 384), [z1, y], [y, z1], [], "two")]
    orders = [[y, z0, z1], [y, z0, z1], [y, z0, z1]]
    wide = [Trip((share, 128), [z1, z0, y], order, [], "two") for order in orders]
    small = Trip((16, 768), [], [], [y, z0, z1, x, ("doc", 0)], "")
    return block + wide + [small]


LINKS = {
    ("batch", 0): [("y", 2.0)],
    ("batch", 1): [("z", 2.0)],
    ("batch", 2): [("far", 4.0), ("z", 2.0)],
    ("doc", 1): [("x", 2.0)],
    ("doc", 0): [("twin", 0.2)],
    None: [("x", 2.0)],
}
IN_FLIGHT = 2
LINK_RATE = 91e3


def trip_program(trips, stages):
    def wire(i, step):
        uses = LINKS[trips[i].steps[step][1]]
        return [(link, trips[i].bytes(step) * copies / LINK_RATE) for link, copies in uses]

    def to_go(i, step):
        return sum(max(t for _, t in wire(i, n)) + 2.0 for n in range(step, len(trips[i].steps)))

    events = [(at, -1, n, 0) for n, (at, _) in enumerate(stages)]
    free, flying, waiting, program = {}, {}, {}, []
    while events:
        events.sort()
        now, kind, i, step = events.pop(0)
        if kind < 0:
            program.append(("make", i, 0))
            ready = [(n, 0) for n in stages[i][1]]
        else:
            program.append(("finish", i, step))
            flying[wire(i, step)[0][0]] -= 1
            ready = [(i, step + 1)] if step + 1 < len(trips[i].steps) else []
        for n, s in ready:
            waiting.setdefault(wire(n, s)[0][0], []).append((-to_go(n, s), n, s))
        for link, queue in waiting.items():
            while queue and flying.get(link, 0) < IN_FLIGHT:
                queue.sort()
                _, n, s = queue.pop(0)
                program.append(("start", n, s))
                flying[link] = flying.get(link, 0) + 1
                end = now
                for used, t in wire(n, s):
                    free[used] = max(now, free.get(used, 0.0)) + t
                    end = max(end, free[used])
                events.append((end + 1.8, 0, n, s))
    return program


def layer_kernel(trips, *refs):
    (
        hidden, segs, places, targets, query, doc_rows,
        bias_q, bias_v, bias_o, gain1, shift1, bias_up, bias_down, gain2, shift2,
        qkv_hbm, out_hbm, up_hbm, down_hbm, vocab_hbm,
        block_out, loss_out, grad_in, grad_query, mats_out, wide_out, vec_out,
        wqkv, wout, wup, wdown, wvoc,
        qb, kb, vb, mixed, first_norm, first_low, acc,
        x4, x4t, kvb, kv4, sp, sp_send, qm, qm_send,
        picks, tsend, trecv, target_rows, usend, urecv, ssend, srecv, logits,
        qexp, probs, probs_low,
        hints, hints_in, joint, joint_in,
        left0, left0_y, left1, left1_y, a1, a1_y, at, at_y, second_b, inner_b, rest_b, g1, g1_y, g2,
        vecs, up_bias_s,
        load_sem, send, recv, *trip_bufs,
    ) = refs
    bias_q, bias_v, bias_o, gain1, shift1, bias_up, bias_down, gain2, shift2 = (
        b[...].reshape(1, -1) for b in (bias_q, bias_v, bias_o, gain1, shift1, bias_up, bias_down, gain2, shift2)
    )
    left0, left1, a1, at, g1 = (left0, left0_y), (left1, left1_y), (a1, a1_y), (at, at_y), (g1, g1_y)
    spot = Spot()
    batch, doc = spot.at["batch"], spot.at["doc"]
    nb, nd = lax.axis_size("batch"), lax.axis_size("doc")
    core, x = spot.mine(("doc", 0)), spot.mine(("doc", 1))
    z0 = spot.mine(("batch", 1))
    rows, width = hidden.shape
    pairs, slots = places.shape
    n_pick = pairs * slots
    heads = width // HEAD_DIM
    share = width // nb
    net = Net(send, recv)

    loads = [
        pltpu.make_async_copy(qkv_hbm.at[:, pl.ds(width, 2 * width)], wqkv.at[:, pl.ds(width, 2 * width)], load_sem.at[0]),
        pltpu.make_async_copy(vocab_hbm, wvoc, load_sem.at[1]),
        pltpu.make_async_copy(qkv_hbm.at[:, pl.ds(0, width)], wqkv.at[:, pl.ds(0, width)], load_sem.at[2]),
        pltpu.make_async_copy(out_hbm, wout, load_sem.at[3]),
        pltpu.make_async_copy(up_hbm, wup, load_sem.at[4]),
        pltpu.make_async_copy(down_hbm, wdown, load_sem.at[5]),
    ]
    for load in loads:
        load.start()

    batch_peers = [(lax.rem(batch + j, nb), doc) for j in range(1, nb)]
    doc_peers = [(batch, lax.rem(doc + j, nd)) for j in range(1, nd)]

    def side_peer(dx, dz, to_core, key):
        tx = lax.rem(x + dx, 2)
        mine = spot.mine(key)
        tz = lax.rem(mine + dz, 2)
        return (batch + (tz - mine) * (1 << key[1]), 2 * tx + to_core), tx, tz

    routes = [("batch", 1), ("batch", 0)]
    twin = spot.peer(("doc", 0))
    slots_of = [4 * spot.mine(key) + doc for key in routes]

    def fan(due, part_of, dst, lanes, to_core, dzs, route):
        slot = slots_of[route]
        sem = net.take()
        land = dst.at[slot, :, pl.ds(0, lanes)]
        always = 0
        for dz in dzs:
            for dx in range(2):
                peer, tx, tz = side_peer(dx, dz, to_core, routes[route])
                copy = net.copy(part_of(tx, tz), land, peer, sem)
                if dx or dz:
                    copy.start()
                    always += 1
                else:
                    pl.when(core != to_core)(copy.start)
        own = 0 in dzs

        def sized(n):
            view = dst.at[pl.ds(0, n), :, pl.ds(0, lanes)]
            return net.copy(view, view, twin, sem)

        def sent():
            if own:
                pl.when(core != to_core)(sized(always + 1).wait_send)
                pl.when(core == to_core)(sized(always).wait_send)
            else:
                sized(always).wait_send()

        net.open.append(sent)
        net.expect(due, lambda: pl.when(core == to_core)(sized(4 * len(dzs) - own).wait_recv))

    far = [
        side_peer(dx, 1, lax.rem(core + dc, 2), key)[0] for key in routes for dx, dc in ((1, 0), (1, 1), (0, 1))
    ]
    everyone = batch_peers + doc_peers + far
    barrier = pltpu.get_barrier_semaphore()
    for peer in everyone:
        pl.semaphore_signal(barrier, inc=1, device_id=peer, device_id_type=MESH)
    pl.semaphore_wait(barrier, len(everyone))

    own_part = query.shape[1]
    spread_lanes = (iota((own_part, own_part * nd), 0) + own_part * doc == iota((own_part, own_part * nd), 1)).astype(F32)
    hints[0:pairs, :] = mm_exact(query[...], spread_lanes)
    hints[8 : 8 + pairs, :] = doc_rows[...]
    hints_in[doc, 0:pairs, :] = hints[0:pairs, :]
    hints_in[doc, 8 : 8 + pairs, :] = hints[8 : 8 + pairs, :]
    net.group("hint", [(hints, hints_in.at[doc], peer) for peer in doc_peers], lambda n: hints_in.at[pl.ds(0, n)])
    beside = spot.peer(("doc", 1))
    net.group("tokens", [(hidden, x4.at[doc], beside)], lambda n: x4.at[pl.ds(0, n)])
    net.group("all tokens", [(hidden, x4.at[doc], twin)], lambda n: x4.at[pl.ds(0, n)])
    x4[doc] = hidden[...]

    place_col = column_of(places[...])
    pick_bool = iota((n_pick, rows), 1) == place_col
    pick = pick_bool.astype(BF16)
    pick_f32 = pick_bool.astype(F32)
    tokens = hidden[...]
    loads[0].wait()
    kb[...] = mm(tokens, wqkv[:, width : 2 * width]).astype(BF16)
    vb[...] = (mm(tokens, wqkv[:, 2 * width :]) + bias_v).astype(BF16)
    tokens_p = mm(pick, tokens).astype(BF16)

    loads[1].wait()
    entries = wvoc.shape[0]
    target_col = jnp.concatenate([column_of(targets[j]) for j in range(nb)], 0) - batch * entries
    all_rows = nb * n_pick
    is_target = iota((all_rows, entries), 1) == target_col
    tsend[...] = mm(is_target.astype(BF16), wvoc[...]).astype(BF16).reshape(nb, nd, n_pick // nd, width)
    trecv[batch] = tsend[batch, doc]
    net.group("part", [(tsend.at[p[0], doc], trecv.at[batch], p) for p in batch_peers], lambda n: trecv.at[pl.ds(0, n)])

    loads[2].wait()
    query_p = (mm(tokens_p, wqkv[:, 0:width]) + bias_q).astype(BF16)

    tall = heads * n_pick
    own_head = iota((tall, width), 0) // n_pick == iota((tall, width), 1) // HEAD_DIM

    def expand(v):
        return jnp.where(own_head, jnp.concatenate([v] * heads, 0), jnp.zeros((), v.dtype))

    def fold(v):
        return jnp.sum(jnp.where(own_head, v, 0.0).reshape(heads, n_pick, width), 0)

    seg_row = segs[...]
    seg_pick = jnp.sum(jnp.where(pick_bool, jnp.broadcast_to(seg_row, (n_pick, rows)), 0), 1, keepdims=True)
    same_pick = seg_pick == seg_row
    scale = 1.0 / math.sqrt(HEAD_DIM)
    qexp[...] = expand(query_p)
    scores = mm_nt(qexp[...], kb[...]) * scale
    same_tall = jnp.concatenate([same_pick.astype(F32)] * heads, 0) > 0.5
    scores = jnp.where(same_tall, scores, -1e30)
    weights = jnp.exp(scores - jnp.max(scores, -1, keepdims=True))
    weights = weights / jnp.sum(weights, -1, keepdims=True)
    probs[...] = weights
    probs_low[...] = weights.astype(BF16)
    mixed_p = fold(mm(probs_low[...], vb[...])).astype(BF16)
    loads[3].wait()
    attended = mm(mixed_p, wout[...]) + bias_o
    hat1, rstd1 = normed(tokens_p.astype(F32) + attended)
    first_p = hat1 * gain1 + shift1
    first_low_p = first_p.astype(BF16)
    loads[4].wait()
    inner_p = mm(first_low_p, wup[...]) + bias_up
    active_p = gelu(inner_p).astype(BF16)
    loads[5].wait()
    second_p = mm(active_p, wdown[...]) + bias_down
    hat2, rstd2 = normed(first_p + second_p)
    picks[batch] = (hat2 * gain2 + shift2).astype(BF16)
    net.group("pick", [(picks.at[batch], picks.at[batch], p) for p in batch_peers], lambda n: picks.at[pl.ds(0, n)])

    ff = wup.shape[1]
    counts = [ALONG_Z, 4 - ALONG_Z]
    firsts = [0, ALONG_Z]
    quads = [(z1, other) for z1 in range(2) for other in range(2)]
    lanes0 = [4 * share * (counts[0] + 1), 4 * share * counts[1]]
    lanes1 = [8 * share, 4 * share]
    for route in range(2):
        wide_lanes = share * counts[route]
        for k in range(2):
            for n, (z1, other) in enumerate(quads):
                b = 4 * z1 + (2 * k + other if route == 0 else 2 * other + k)
                own = slice(b * share, (b + 1) * share)
                start = 4 * share * b + share * firsts[route]
                left0[route][k, :, n * wide_lanes : (n + 1) * wide_lanes] = active_p[:, start : start + wide_lanes]
                left1[route][k, :, n * share : (n + 1) * share] = first_low_p[:, own]
                if route == 0:
                    at0 = 4 * wide_lanes + n * share
                    left0[route][k, :, at0 : at0 + share] = mixed_p[:, own]
                    left1[route][k, :, (4 + n) * share : (5 + n) * share] = tokens_p[:, own]

    def keep_left(route, left, lanes):
        def keep():
            a1[route][slots_of[route], :, 0:lanes] = left[route][spot.mine(routes[route])]

        return keep

    for route in range(2):
        pl.when(core == 0)(keep_left(route, left0, lanes0[route]))
        pl.when(core == 1)(keep_left(route, left1, lanes1[route]))

    def send_left(dzs):
        for route in range(2):
            fan("left", lambda tx, tz: left0[route].at[tz], a1[route], lanes0[route], 0, dzs, route)
            fan("left", lambda tx, tz: left1[route].at[tz], a1[route], lanes1[route], 1, dzs, route)

    half_w, half_f = width // 2, ff // 2
    tall_half = tall // 2
    send_left([0])

    def half_heads(due, src, dst, to_core):
        sem = net.take()
        for dx in range(2):
            peer, tx, _ = side_peer(dx, 0, to_core, routes[0])
            copy = net.copy(src.at[tx], dst.at[doc], peer, sem)
            if dx:
                copy.start()
            else:
                pl.when(core != to_core)(copy.start)

        def keep():
            dst[doc] = src[x]

        def sized(n):
            view = dst.at[pl.ds(0, n)]
            return net.copy(view, view, twin, sem)

        def sent():
            pl.when(core != to_core)(sized(2).wait_send)
            pl.when(core == to_core)(sized(1).wait_send)

        pl.when(core == to_core)(keep)
        net.open.append(sent)
        net.expect(due, lambda: pl.when(core == to_core)(sized(3).wait_recv))

    def halves(dst, v):
        for s in range(2):
            dst[s] = v[:, s * half_w : (s + 1) * half_w]

    sp_send[1] = probs_low[...].reshape(2, tall_half, rows)
    half_heads("heads", sp_send.at[1], sp, 1)
    halves(qm_send.at[0], query_p)
    half_heads("heads", qm_send.at[0], qm, 0)

    seg_col = jnp.sum(
        jnp.where(iota((rows, rows), 0) == iota((rows, rows), 1), jnp.broadcast_to(seg_row, (rows, rows)), 0),
        1,
        keepdims=True,
    )
    qb[...] = (mm(tokens, wqkv[:, 0:width]) + bias_q).astype(BF16)

    def attend(i):
        lanes = pl.ds(pl.multiple_of(i * 128, 128), 128)
        q_s, k_s, v_s = qb[:, lanes], kb[:, lanes], vb[:, lanes]
        low = iota((rows, 128), 1) < HEAD_DIM
        same = seg_col == seg_row
        parts = []
        for side in (low, ~low):
            s = mm_nt(jnp.where(side, q_s, jnp.zeros((), BF16)), k_s) * scale
            s = jnp.where(same, s, -1e30)
            e = jnp.exp(s - jnp.max(s, -1, keepdims=True))
            p = (e / jnp.sum(e, -1, keepdims=True)).astype(BF16)
            parts.append(mm(p, v_s))
        mixed[:, lanes] = jnp.where(low, parts[0], parts[1]).astype(BF16)

    half_way = width // 256
    pl.loop(0, half_way)(attend)
    send_left([1])
    net.collect("tokens")
    net.group("all tokens", [(x4.at[beside[1]], x4.at[beside[1]], twin)], lambda n: x4.at[pl.ds(0, n)])
    net.collect("part")
    part = trecv[0].astype(F32)
    for j in range(1, nb):
        part += trecv[j].astype(F32)
    target_rows[doc] = part.astype(BF16)
    net.group("target", [(target_rows.at[doc], target_rows.at[doc], p) for p in doc_peers], lambda n: target_rows.at[pl.ds(0, n)])
    pl.loop(half_way, width // 128)(attend)

    net.collect("pick")
    logits[...] = mm_nt(picks[...].reshape(all_rows, width), wvoc[...])
    lg = logits[...]
    top = jnp.max(lg, 1, keepdims=True)
    chosen = jnp.sum(jnp.where(is_target, lg, 0.0), 1, keepdims=True)
    others = jnp.where(is_target, 0.0, jnp.exp(lg - top))
    total = jnp.sum(others, 1, keepdims=True)
    lane = iota((all_rows, 128), 1)
    stats = jnp.where(lane == 0, top, jnp.where(lane == 1, total, chosen)).T
    blank = jnp.zeros((8, 128 - n_pick), F32)
    for j in range(nb):
        ssend[j] = jnp.concatenate([stats[0:8, n_pick * j : n_pick * (j + 1)], blank], 1)
    srecv[batch] = ssend[batch]
    net.group("stats", [(ssend.at[p[0]], srecv.at[batch], p) for p in batch_peers], lambda n: srecv.at[pl.ds(0, n)])
    usend[...] = mm(others.astype(BF16), wvoc[...]).astype(BF16).reshape(nb, n_pick, width)
    urecv[batch] = usend[batch]
    net.group("back", [(usend.at[p[0]], urecv.at[batch], p) for p in batch_peers], lambda n: urecv.at[pl.ds(0, n)])

    tokens = hidden[...]
    hat, _ = normed(tokens.astype(F32) + mm(mixed[...], wout[...]) + bias_o)
    first_norm[...] = hat * gain1 + shift1
    first_low[...] = first_norm[...].astype(BF16)
    acc[...] = first_norm[...] + bias_down
    chunk = 512
    up_bias_s[...] = bias_up

    def feed(i):
        cols = pl.ds(pl.multiple_of(i * chunk, chunk), chunk)
        hid = mm(first_low[...], wup[:, cols]) + up_bias_s[:, cols]
        acc[...] += mm(gelu(hid).astype(BF16), wdown[cols, :])

    pl.loop(0, ff // chunk // 2)(feed)

    net.collect("stats")
    tops = [srecv[j][0:1, :] for j in range(nb)]
    peak = tops[0]
    for t in tops[1:]:
        peak = jnp.maximum(peak, t)
    factors = [jnp.exp(t - peak) for t in tops]
    rest = jnp.zeros_like(peak)
    chosen = jnp.zeros_like(peak)
    for j in range(nb):
        rest += factors[j] * srecv[j][1:2, :]
        chosen += srecv[j][2:3, :]
    whole = rest + jnp.exp(chosen - peak)
    logp = chosen - peak - jnp.log(whole)
    of_pair = iota((pairs, 128), 1) // slots == iota((pairs, 128), 0)
    reader = jnp.sum(jnp.where(of_pair, jnp.broadcast_to(logp, (pairs, 128)), 0.0), 1, keepdims=True) / slots
    joint[...] = jnp.zeros_like(joint)
    joint[0:pairs, :] = jnp.broadcast_to(reader, (pairs, 128))
    joint_in[doc] = joint[...]
    net.group("joint", [(joint, joint_in.at[doc], p) for p in doc_peers], lambda n: joint_in.at[pl.ds(0, n)])
    shares = jnp.concatenate([f / whole for f in factors] + [rest / whole] + [jnp.zeros_like(peak)] * (15 - nb), 0).T

    pl.loop(ff // chunk // 2, ff // chunk)(feed)
    hat, _ = normed(acc[...])
    block_out[...] = (hat * gain2 + shift2).astype(BF16)
    net.collect("all tokens")
    x4t[...] = x4[...].reshape(nd * rows, width).T

    net.collect("hint")
    full_query = hints_in[0, 0:pairs, :]
    for j in range(1, nd):
        full_query += hints_in[j, 0:pairs, :]
    docs = [hints_in[j, 8 : 8 + pairs, :] for j in range(nd)]
    score = [jnp.broadcast_to(jnp.sum(full_query * d, 1, keepdims=True), (pairs, 128)) for d in docs]
    net.collect("joint")
    both = [s + joint_in[j, 0:pairs, :] for j, s in enumerate(score)]

    def soft(vals):
        high = vals[0]
        for v in vals[1:]:
            high = jnp.maximum(high, v)
        es = [jnp.exp(v - high) for v in vals]
        tot = es[0]
        for e in es[1:]:
            tot = tot + e
        return [e / tot for e in es], high + jnp.log(tot)

    w_score, total_score = soft(score)
    w_joint, total_joint = soft(both)
    eye = iota((pairs, 128), 0) == iota((pairs, 128), 1)
    loss_out[...] = jnp.sum(jnp.where(eye, total_score - total_joint, 0.0), 0, keepdims=True)
    query_grad = (w_score[0] - w_joint[0]) * docs[0]
    for j in range(1, nd):
        query_grad += (w_score[j] - w_joint[j]) * docs[j]
    grad_query[...] = mm_exact(query_grad, spread_lanes, NT)
    mine = w_joint[0]
    for j in range(1, nd):
        mine = jnp.where(doc == j, w_joint[j], mine)
    row_weight = jnp.broadcast_to(mine.reshape(pairs, 1, 128), (pairs, slots, 128)).reshape(n_pick, 128)[:, 0:1]

    net.collect("left")

    def turn(route, lanes):
        def go():
            at[route][0:lanes, :] = a1[route][:, :, 0:lanes].reshape(8 * n_pick, lanes).T

        return go

    for route in range(2):
        pl.when(core == 0)(turn(route, lanes0[route]))
        pl.when(core == 1)(turn(route, lanes1[route]))

    net.collect("back")
    row_grad = jnp.zeros((n_pick, width), F32)
    for j in range(nb):
        row_grad += shares[0:n_pick, j : j + 1] * urecv[j].astype(F32)
    net.collect("target")
    at_target = target_rows[...].astype(F32).reshape(n_pick, width)
    row_grad -= shares[0:n_pick, nb : nb + 1] * at_target
    final_grad = row_grad * (row_weight / slots)

    def send_right(due, src, every, first, cols, dst, to_core, route):
        def part(tx):
            return pl.ds(pl.multiple_of(tx * every + first, 128), cols)

        fan(due, lambda tx, tz: src.at[:, part(tx)], dst, cols, to_core, [0, 1], route)

        def keep():
            dst[slots_of[route], :, 0:cols] = src[:, part(x)]

        pl.when(core == to_core)(keep)

    vecs[...] = jnp.zeros_like(vecs)
    sum_grad = norm_back(final_grad, hat2, rstd2, gain2)
    vecs[6:7, :] = jnp.sum(final_grad * hat2, 0, keepdims=True)
    vecs[7:8, :] = jnp.sum(final_grad, 0, keepdims=True)
    vecs[5:6, :] = jnp.sum(sum_grad, 0, keepdims=True)
    second_low = sum_grad.astype(BF16)
    second_b[...] = second_low
    for route in range(2):
        send_right(("g1", route), second_b, half_w, 0, half_w, g1[route], 0, route)
    inner_grad = mm_nt(second_low, wdown[...]) * gelu_slope(inner_p)
    inner_low = inner_grad.astype(BF16)
    inner_b[...] = inner_low
    for route in range(2):
        first, cols = firsts[route] * half_w, counts[route] * half_w
        send_right(("g1", route), inner_b, half_f, first, cols, g1[route], 1, route)
    up_bias_grad = jnp.sum(inner_grad, 0, keepdims=True)
    for i in range(ff // width):
        vecs[8 + i : 9 + i, :] = up_bias_grad[:, i * width : (i + 1) * width]
    first_grad = sum_grad + mm_nt(inner_low, wup[...])
    resid_grad = norm_back(first_grad, hat1, rstd1, gain1)
    resid_low = resid_grad.astype(BF16)
    rest_b[0] = resid_low
    send_right("g2", rest_b.at[0], half_w, 0, half_w, g2, 0, 0)
    vecs[3:4, :] = jnp.sum(first_grad * hat1, 0, keepdims=True)
    vecs[4:5, :] = jnp.sum(first_grad, 0, keepdims=True)
    vecs[2:3, :] = jnp.sum(resid_grad, 0, keepdims=True)
    mixed_grad_p = mm_nt(resid_low, wout[...]).astype(BF16)
    halves(qm_send.at[1], mixed_grad_p)
    half_heads("heads", qm_send.at[1], qm, 1)
    mixed_grad = expand(mixed_grad_p)
    prob_grad = mm_nt(mixed_grad, vb[...])
    p = probs[...]
    score_low = (p * (prob_grad - jnp.sum(prob_grad * p, -1, keepdims=True)) * scale).astype(BF16)
    sp_send[0] = score_low.reshape(2, tall_half, rows)
    half_heads("heads", sp_send.at[0], sp, 0)
    query_grad_p = fold(mm(score_low, kb[...]))
    rest_b[1] = query_grad_p.astype(BF16)
    send_right("g2", rest_b.at[1], half_w, 0, half_w, g2, 1, 0)
    vecs[0:1, :] = jnp.sum(query_grad_p, 0, keepdims=True)
    value_grad = mm_tn(probs_low[...], mixed_grad)
    kvb[1] = value_grad.astype(BF16)
    vecs[1:2, :] = jnp.sum(value_grad, 0, keepdims=True)

    sems = [[net.take() for _ in t.steps] for t in trips]
    groups, left_over = [], list(trip_bufs)
    for t in trips:
        k = len(t.buffers())
        groups.append(left_over[:k])
        left_over = left_over[k:]

    def tail(side, net):
        runs = [TripRun(t, groups[n], sems[n], net, spot) for n, t in enumerate(trips)]

        def make_wide():
            net.collect("heads")
            half_tall = iota((tall_half, half_w), 0) // n_pick == iota((tall_half, half_w), 1) // HEAD_DIM
            for d in range(nd):
                tiled = jnp.concatenate([qm[d]] * (heads // 2), 0)
                tiled = jnp.where(half_tall, tiled, jnp.zeros((), BF16))
                kv4[d] = mm_tn(sp[d], tiled).astype(BF16)
            right = kv4[...].reshape(nd * rows, half_w)
            for b in range(nb):
                out = mm(x4t[b * share : (b + 1) * share, :], right).astype(BF16)
                for n in range(3):
                    runs[5 + n].bufs[0][b // 4, b // 2 % 2, b % 2] = out[:, 128 * n : 128 * (n + 1)]

        def block(i, route, offsets, g, col):
            left = jnp.concatenate([at[route][pl.ds(pl.multiple_of(o, 32), share), :] for o in offsets], 0)
            right = g[:, :, pl.ds(col, half_w)].reshape(8 * n_pick, half_w)
            out = mm(left, right).astype(BF16)
            for n, (z1, other) in enumerate(quads):
                runs[i].bufs[0][z1, other] = out[n * share : (n + 1) * share]

        def make_blocks(route):
            net.collect(("g1", route))
            for i in range(counts[route]):
                offsets = [((1 - core) * (n * counts[route] + i) + core * n) * share for n in range(4)]
                block(firsts[route] + i, route, offsets, g1[route], pl.multiple_of(core * i * half_w, 128))

        def make_last():
            net.collect("g2")
            first_row = (1 - core) * 4 * share * counts[0] + core * 4 * share
            block(4, 0, [first_row + n * share for n in range(4)], g2, 0)

        def make_inward():
            kvb[0] = mm_tn(score_low, qexp[...]).astype(BF16)
            inward = mm_nt(kvb[0], wqkv[:, width : 2 * width]) + mm_nt(kvb[1], wqkv[:, 2 * width :])
            at_rows = resid_grad + mm_nt(rest_b[1], wqkv[:, 0:width])
            grad_in[...] = (inward + mm_exact(pick_f32, at_rows, TN)).astype(BF16)

        def make_sums():
            runs[8].bufs[0][...] = vecs[...].astype(BF16)

        along_y = list(range(ALONG_Z, 4))
        along_z = list(range(ALONG_Z))
        stages = (
            [
                (0.0, [8], make_sums),
                (0.6, along_y, lambda: make_blocks(1)),
                (1.2, along_z, lambda: make_blocks(0)),
                (1.8, [4], make_last),
                (5.0, [5, 6, 7], make_wide),
                (9.0, [], make_inward),
            ]
            if side == 0
            else [
                (0.0, [8], make_sums),
                (2.5, [5, 6, 7], make_wide),
                (5.0, along_y, lambda: make_blocks(1)),
                (5.6, along_z, lambda: make_blocks(0)),
                (6.2, [4], make_last),
                (10.0, [], make_inward),
            ]
        )
        last = []
        for what, i, step in trip_program(trips, [(t, made) for t, made, _ in stages]):
            if what == "make":
                stages[i][2]()
            elif what == "start":
                runs[i].start(step)
            elif trips[i].steps[step][1] == ("doc", 0):
                last.append((i, step))
            else:
                runs[i].finish(step)
        for i, step in last:
            runs[i].finish(step)
            if i < 5:
                mats_out[i] = runs[i].final[...]
            elif i < 8:
                wide_out[i - 5] = runs[i].final[...]
            else:
                vec_out[...] = runs[i].final[...]
        net.drain()

    for side in range(2):
        pl.when(core == side)(partial(tail, side, net.branch()))


def finish_kernel(block, grad, loss, gq, mats, wide, vec, *outs):
    (o_block, o_loss, o_grad, o_gq, o_qkv, o_qb, o_vb, o_out, o_ob, o_g1, o_s1, o_up, o_ub, o_down, o_db, o_g2, o_s2) = outs
    batch = lax.axis_index("batch")
    nb = lax.axis_size("batch")
    width = vec.shape[1]
    share, half = width // nb, width // 2
    o_block[...] = block[...]
    o_grad[...] = grad[...]
    o_loss[...] = loss[:, 0 : o_loss.shape[1]]
    o_gq[...] = gq[...]
    for s in range(2):
        cols = slice(s * half, (s + 1) * half)
        o_out[:, cols] = mats[4, 0, s].astype(F32)
        o_qkv[:, cols] = mats[4, 1, s].astype(F32)
        for i in range(4):
            o_down[i * share : (i + 1) * share, cols] = mats[i, 0, s].astype(F32)
            o_up[:, (4 * s + i) * half : (4 * s + i + 1) * half] = mats[i, 1, s].astype(F32)
        for c in range(2):
            for j in range(3):
                start = (1 + c) * width + s * half + 128 * j
                o_qkv[:, start : start + 128] = wide[j, c, s].astype(F32)
    v = vec[...].astype(F32)
    take = (iota((width, share), 0) == iota((width, share), 1) + batch * share).astype(F32)
    got = mm_exact(v, take)
    for i, o in enumerate((o_qb, o_vb, o_ob, o_g1, o_s1, o_db, o_g2, o_s2)):
        o[...] = got[i : i + 1, :]
    side = jnp.where(lax.rem(batch, 2) == 0, v[8:12, 0:half], v[8:12, half:])
    o_ub[...] = jnp.sum(jnp.where(iota((4, half), 0) == batch // 2, side, 0.0), 0)


def paired_local(*args):
    (
        hidden_in, segments, mask_pos, target_ids, query_emb, doc_emb,
        qkv_weight, query_bias, value_bias, out_weight, out_bias, gain_one, shift_one,
        up_weight, up_bias, down_weight, down_bias, gain_two, shift_two, vocab,
    ) = args
    rows, width = hidden_in.shape[2:]
    pairs, slots = mask_pos.shape[2:]
    n_pick = pairs * slots
    ff = up_weight.shape[1]
    entries = vocab.shape[0]
    nb, nd = lax.axis_size("batch"), lax.axis_size("doc")
    share = width // nb
    heads = width // HEAD_DIM
    trips = layer_trips(share)
    lanes_z, lanes_y = 4 * share * (ALONG_Z + 1), 4 * share * (4 - ALONG_Z)
    n_sems = sum(len(t.steps) for t in trips) + 28
    vm, hbm = pl.BlockSpec(memory_space=pltpu.VMEM), pl.BlockSpec(memory_space=pl.ANY)

    def v(shape, dtype=BF16):
        return pltpu.VMEM(shape, dtype)

    dma = pltpu.SemaphoreType.DMA
    scratch = [
        v(qkv_weight.shape), v(out_weight.shape), v(up_weight.shape), v(down_weight.shape), v(vocab.shape),
        v((rows, width)), v((rows, width)), v((rows, width)), v((rows, width)),
        v((rows, width), F32), v((rows, width)), v((rows, width), F32),
        v((nd, rows, width)), v((width, nd * rows)), v((2, rows, width)), v((nd, rows, width // 2)),
        v((nd, heads * n_pick // 2, rows)), v((2, 2, heads * n_pick // 2, rows)),
        v((nd, n_pick, width // 2)), v((2, 2, n_pick, width // 2)),
        v((nb, n_pick, width)), v((nb, nd, n_pick // nd, width)), v((nb, n_pick // nd, width)),
        v((nd, n_pick // nd, width)), v((nb, n_pick, width)),
        v((nb, n_pick, width)), v((nb, 8, 128), F32), v((nb, 8, 128), F32), v((nb * n_pick, entries), F32),
        v((heads * n_pick, width)), v((heads * n_pick, rows), F32), v((heads * n_pick, rows)),
        v((16, 128), F32), v((nd, 16, 128), F32), v((8, 128), F32), v((nd, 8, 128), F32),
        v((2, n_pick, lanes_z)), v((2, n_pick, lanes_y)), v((2, n_pick, width)), v((2, n_pick, width // 2)),
        v((8, n_pick, lanes_z)), v((8, n_pick, max(lanes_y, width // 2))), v((lanes_z, 8 * n_pick)),
        v((max(lanes_y, width // 2), 8 * n_pick)),
        v((n_pick, width)), v((n_pick, ff)), v((2, n_pick, width)),
        v((8, n_pick, ALONG_Z * width // 2)), v((8, n_pick, (4 - ALONG_Z) * width // 2)), v((8, n_pick, width // 2)),
        v((16, width), F32), v((1, ff), F32),
        dma((6,)), dma((n_sems,)), dma((n_sems,)),
    ]
    for t in trips:
        scratch += [v(shape) for shape in t.buffers()]
    sds = jax.ShapeDtypeStruct
    first = pl.pallas_call(
        partial(layer_kernel, trips),
        out_shape=[
            sds((rows, width), BF16),
            sds((1, 128), F32),
            sds((rows, width), BF16),
            sds((pairs, query_emb.shape[2]), F32),
            sds((5, 2, 2, share, 384), BF16),
            sds((3, 2, 2, share, 128), BF16),
            sds((16, width), BF16),
        ],
        in_specs=[vm] * 15 + [hbm] * 5,
        out_specs=[vm] * 7,
        scratch_shapes=scratch,
        compiler_params=pltpu.CompilerParams(
            collective_id=0, has_side_effects=True, vmem_limit_bytes=VMEM_BYTES
        ),
        name="layer",
    )
    biases = (query_bias, value_bias, out_bias, gain_one, shift_one, up_bias, down_bias, gain_two, shift_two)
    block, loss, grad, gq, mats, wide, vec = first(
        hidden_in.reshape(rows, width),
        segments.reshape(1, rows),
        mask_pos.reshape(pairs, slots),
        target_ids,
        query_emb.reshape(pairs, -1),
        doc_emb.reshape(pairs, -1),
        *biases,
        qkv_weight,
        out_weight,
        up_weight,
        down_weight,
        vocab,
    )
    small = sds((1, share), F32)
    outs = pl.pallas_call(
        finish_kernel,
        out_shape=[
            sds((rows, width), BF16), sds((1, pairs), F32), sds((rows, width), BF16), sds(gq.shape, F32),
            sds((share, 3 * width), F32), small, small, sds((share, width), F32), small, small, small,
            sds((share, ff), F32), sds((ff // nb,), F32), sds((ff // nb, width), F32), small, small, small,
        ],
        in_specs=[vm] * 7,
        out_specs=[vm] * 17,
        compiler_params=pltpu.CompilerParams(vmem_limit_bytes=VMEM_BYTES),
        name="finish",
    )(block, grad, loss, gq, mats, wide, vec)
    shapes = [hidden_in.shape, (1, pairs), hidden_in.shape, query_emb.shape]
    fixed = [o.reshape(s) for o, s in zip(outs[:4], shapes)]
    return tuple(fixed + [o.reshape(-1) if o.shape == (1, share) else o for o in outs[4:]])


def combined_all(x, axis, combine):
    everything = jax.tree.map(lambda part: lax.all_gather(part, axis), x)
    leading = jax.tree.map(lambda part: part[0], everything)

    def hop(k, so_far):
        return combine(so_far, jax.tree.map(lambda part: part[k], everything))

    return lax.fori_loop(1, lax.axis_size(axis), hop, leading)


def norm_rows(values, gain, shift):
    centre = jnp.mean(values, -1, keepdims=True)
    centred = values - centre
    spread = jnp.mean(centred * centred, -1, keepdims=True)
    return centred * lax.rsqrt(spread + 1e-06) * gain + shift


def lse_pair(earlier, later):
    maxima = jnp.maximum(earlier[0], later[0])
    totals = earlier[1] * jnp.exp(earlier[0] - maxima) + later[1] * jnp.exp(later[0] - maxima)
    return (maxima, totals)


def vocab_pair(earlier, later):
    return lse_pair(earlier[:2], later[:2]) + (earlier[2] + later[2],)


def place_rows(places, grads, seq_len):
    return jnp.zeros((seq_len, grads.shape[-1]), jnp.float32).at[places].add(grads)


def local(
    hidden_in,
    segments,
    mask_pos,
    target_ids,
    query_emb,
    doc_emb,
    qkv_weight,
    query_bias,
    value_bias,
    out_weight,
    out_bias,
    gain_one,
    shift_one,
    up_weight,
    up_bias,
    down_weight,
    down_bias,
    gain_two,
    shift_two,
    vocab,
):
    f32 = jnp.float32
    bf16 = jnp.bfloat16
    seq_count, _, seq_len, model_width = hidden_in.shape
    pair_count = mask_pos.shape[2]
    mask_count = mask_pos.shape[3]
    head_count = model_width // HEAD_DIM
    score_scale = 1.0 / math.sqrt(HEAD_DIM)
    split_shape = (seq_count, seq_len, head_count, HEAD_DIM)
    tokens = hidden_in.reshape(seq_count, seq_len, model_width)
    segs = segments.reshape(seq_count, seq_len)
    packed = jnp.einsum("nld,de->nle", tokens, qkv_weight, preferred_element_type=f32)
    queries = (packed[..., :model_width] + query_bias).astype(bf16).reshape(split_shape)
    key_rows = packed[..., model_width : 2 * model_width].astype(bf16).reshape(split_shape)
    value_rows = (packed[..., 2 * model_width :] + value_bias).astype(bf16).reshape(split_shape)
    same_seg = (segs[:, :, None] == segs[:, None, :])[:, None]
    raw_scores = jnp.einsum("nlhe,nmhe->nhlm", queries, key_rows, preferred_element_type=f32)

    def attend(scores_in):
        return jax.nn.softmax(jnp.where(same_seg, scores_in * score_scale, -1e30), axis=-1)

    probs, soft_back = jax.vjp(attend, raw_scores)
    probs_low = probs.astype(bf16)
    mixed_heads = jnp.einsum("nhlm,nmhe->nlhe", probs_low, value_rows, preferred_element_type=f32)
    mixed_low = mixed_heads.reshape(seq_count, seq_len, model_width).astype(bf16)
    attended = (
        jnp.einsum("nld,de->nle", mixed_low, out_weight, preferred_element_type=f32) + out_bias
    )
    first_norm, norm_back_one = jax.vjp(
        norm_rows, tokens.astype(f32) + attended, gain_one, shift_one
    )
    first_low = first_norm.astype(bf16)
    inner_act = (
        jnp.einsum("nld,df->nlf", first_low, up_weight, preferred_element_type=f32) + up_bias
    )
    active, gelu_back = jax.vjp(partial(jax.nn.gelu, approximate=False), inner_act)
    active_low = active.astype(bf16)
    second = (
        jnp.einsum("nlf,fd->nld", active_low, down_weight, preferred_element_type=f32) + down_bias
    )
    final_rows, norm_back_two = jax.vjp(norm_rows, first_norm + second, gain_two, shift_two)
    per_seq = pair_count * mask_count
    rows_dev = seq_count * per_seq
    flat_places = mask_pos.reshape(seq_count, per_seq)
    picked = jnp.take_along_axis(final_rows, flat_places[:, :, None], axis=1)
    picked_low = picked.reshape(rows_dev, model_width).astype(bf16)
    logits = lax.dot_general(
        lax.all_gather(picked_low, "batch", axis=0, tiled=True),
        vocab,
        (((1,), (1,)), ((), ())),
        preferred_element_type=f32,
    )
    shard_size = vocab.shape[0]
    vocab_ids = lax.axis_index("batch") * shard_size + lax.iota(jnp.int32, shard_size)
    is_target = target_ids.reshape(-1)[:, None] == vocab_ids[None, :]
    maxima = jnp.max(logits, 1)
    totals = jnp.sum(jnp.exp(logits - maxima[:, None]), 1)
    chosen = jnp.sum(jnp.where(is_target, logits, 0.0), 1)
    maxima, totals, chosen = combined_all((maxima, totals, chosen), "batch", vocab_pair)
    log_total = maxima + jnp.log(totals)
    first_own = lax.axis_index("batch") * rows_dev
    own_logp = lax.dynamic_slice_in_dim(chosen - log_total, first_own, rows_dev)
    reader = jnp.mean(own_logp.reshape(seq_count, pair_count, mask_count), -1)
    gathered_query = lax.all_gather(query_emb, "doc", axis=2, tiled=True)
    doc_rows = doc_emb.reshape(seq_count, pair_count, doc_emb.shape[-1])
    score = jnp.sum(gathered_query * doc_rows, -1)
    joint = score + reader
    unit_terms = jnp.ones_like(score)
    score_top, score_sum = combined_all((score, unit_terms), "doc", lse_pair)
    score_total = score_top + jnp.log(score_sum)
    shifted = joint - score_total
    joint_top, joint_sum = combined_all((shifted, unit_terms), "doc", lse_pair)
    joint_total = joint_top + jnp.log(joint_sum)
    loss = -joint_total
    weight_joint = jnp.exp(shifted - joint_total)
    weight_score = jnp.exp(score - score_total)
    score_grad = weight_score - weight_joint
    grad_query = lax.psum_scatter(
        score_grad[..., None] * doc_rows, "doc", scatter_dimension=2, tiled=True
    )
    row_scale = jnp.broadcast_to(
        (weight_joint / mask_count)[..., None], (seq_count, pair_count, mask_count)
    ).reshape(rows_dev)
    all_scale = lax.all_gather(row_scale, "batch", axis=0, tiled=True)
    vocab_probs = jnp.exp(logits - log_total[:, None])
    logit_grad = (all_scale[:, None] * (vocab_probs - is_target.astype(f32))).astype(bf16)
    picked_grad = lax.psum_scatter(
        jnp.dot(logit_grad, vocab, preferred_element_type=f32).astype(jnp.bfloat16),
        "batch",
        scatter_dimension=0,
        tiled=True,
    ).astype(jnp.float32)
    final_grad = jax.vmap(partial(place_rows, seq_len=seq_len))(
        flat_places, picked_grad.reshape(seq_count, per_seq, model_width)
    )
    sum_grad, grad_gain_two, grad_shift_two = norm_back_two(final_grad)
    grad_down_bias = jnp.sum(sum_grad, (0, 1))
    second_low = sum_grad.astype(bf16)
    grad_down_weight = jnp.einsum("nlf,nld->fd", active_low, second_low, preferred_element_type=f32)
    active_grad = jnp.einsum("nld,fd->nlf", second_low, down_weight, preferred_element_type=f32)
    (inner_grad,) = gelu_back(active_grad)
    grad_up_bias = jnp.sum(inner_grad, (0, 1))
    inner_low = inner_grad.astype(bf16)
    grad_up_weight = jnp.einsum("nld,nlf->df", first_low, inner_low, preferred_element_type=f32)
    first_grad = sum_grad + jnp.einsum(
        "nlf,df->nld", inner_low, up_weight, preferred_element_type=f32
    )
    resid_grad, grad_gain_one, grad_shift_one = norm_back_one(first_grad)
    grad_out_bias = jnp.sum(resid_grad, (0, 1))
    resid_low = resid_grad.astype(bf16)
    grad_out_weight = jnp.einsum("nld,nle->de", mixed_low, resid_low, preferred_element_type=f32)
    mixed_grad = (
        jnp.einsum("nle,de->nld", resid_low, out_weight, preferred_element_type=f32)
        .astype(bf16)
        .reshape(split_shape)
    )
    value_grad = jnp.einsum("nhlm,nlhe->nmhe", probs_low, mixed_grad, preferred_element_type=f32)
    prob_grad = jnp.einsum("nlhe,nmhe->nhlm", mixed_grad, value_rows, preferred_element_type=f32)
    (score_back,) = soft_back(prob_grad)
    score_low = score_back.astype(bf16)
    query_grad = jnp.einsum("nhlm,nmhe->nlhe", score_low, key_rows, preferred_element_type=f32)
    key_grad = jnp.einsum("nhlm,nlhe->nmhe", score_low, queries, preferred_element_type=f32)
    flat_shape = (seq_count, seq_len, model_width)
    query_grad = query_grad.reshape(flat_shape)
    key_grad = key_grad.reshape(flat_shape)
    value_grad = value_grad.reshape(flat_shape)
    grad_query_bias = jnp.sum(query_grad, (0, 1))
    grad_value_bias = jnp.sum(value_grad, (0, 1))
    packed_grad = jnp.concatenate([query_grad, key_grad, value_grad], -1).astype(bf16)
    grad_qkv_weight = jnp.einsum("nld,nle->de", tokens, packed_grad, preferred_element_type=f32)
    input_grad = resid_grad + jnp.einsum(
        "nle,de->nld", packed_grad, qkv_weight, preferred_element_type=f32
    )
    vectors = jnp.concatenate(
        [
            jnp.stack(
                [
                    grad_query_bias,
                    grad_value_bias,
                    grad_out_bias,
                    grad_gain_one,
                    grad_shift_one,
                    grad_down_bias,
                    grad_gain_two,
                    grad_shift_two,
                ]
            ),
            grad_up_bias.reshape(-1, model_width),
        ]
    )
    vectors = jnp.pad(vectors, ((0, -vectors.shape[0] % 16), (0, 0)))
    mats = (grad_down_weight, grad_up_weight, grad_out_weight, grad_qkv_weight)
    down_sum, up_sum, out_sum, qkv_sum, vector_sum = reduce_params(
        [m.astype(bf16) for m in mats], vectors, lax.axis_size("batch"), lax.axis_size("doc")
    )
    nb = lax.axis_size("batch")
    slot = lax.axis_index("batch")

    def share(v):
        return lax.dynamic_slice_in_dim(v, slot * (v.shape[0] // nb), v.shape[0] // nb)

    up_bias_sum = vector_sum[8 : 8 + grad_up_bias.shape[0] // model_width].reshape(-1)
    results = (
        qkv_sum.astype(f32),
        share(vector_sum[0]),
        share(vector_sum[1]),
        out_sum.astype(f32),
        share(vector_sum[2]),
        share(vector_sum[3]),
        share(vector_sum[4]),
        up_sum.astype(f32),
        share(up_bias_sum),
        down_sum.astype(f32),
        share(vector_sum[5]),
        share(vector_sum[6]),
        share(vector_sum[7]),
    )
    block_out = final_rows.astype(bf16).reshape(hidden_in.shape)
    grad_in = input_grad.astype(bf16).reshape(hidden_in.shape)
    return (
        block_out,
        loss,
        grad_in,
        grad_query,
        results[0],
        results[1],
        results[2],
        results[3],
        results[4],
        results[5],
        results[6],
        results[7],
        results[8],
        results[9],
        results[10],
        results[11],
        results[12],
    )


def solution(mesh):
    in_specs = (
        P("batch", "doc", None, None),
        P("batch", "doc", None),
        P("batch", "doc", None, None),
        P(),
        P("batch", None, "doc"),
        P("batch", "doc", None, None),
        P(),
        P(),
        P(),
        P(),
        P(),
        P(),
        P(),
        P(),
        P(),
        P(),
        P(),
        P(),
        P(),
        P("batch", None),
    )
    out_specs = (
        P("batch", "doc", None, None),
        P("batch", None),
        P("batch", "doc", None, None),
        P("batch", None, "doc"),
        P("batch", None),
        P("batch"),
        P("batch"),
        P("batch", None),
        P("batch"),
        P("batch"),
        P("batch"),
        P("batch", None),
        P("batch"),
        P("batch", None),
        P("batch"),
        P("batch"),
        P("batch"),
    )
    paired = dict(mesh.shape) == {"batch": 8, "doc": 4}
    return jax.shard_map(paired_local if paired else local, mesh=mesh, in_specs=in_specs, out_specs=out_specs, check_vma=False)
```

```python
from functools import partial
import itertools
import math

import jax
import jax.numpy as jnp
from jax import lax
from jax.experimental import pallas as pl
from jax.experimental.pallas import tpu as pltpu
from jax.sharding import PartitionSpec as P

HEAD_DIM = 64
MESH = pl.DeviceIdType.MESH
VMEM_BYTES = 64000000


class Spot:
    def __init__(self):
        self.at = {"batch": lax.axis_index("batch"), "doc": lax.axis_index("doc")}

    def mine(self, key):
        axis, k = key
        return lax.rem(self.at[axis] // (1 << k), 2)

    def others(self):
        nd = lax.axis_size("doc")
        return [(self.at["batch"], lax.rem(self.at["doc"] + j, nd)) for j in range(1, nd)]

    def peer(self, key):
        axis, k = key
        moved = dict(self.at)
        moved[axis] = self.at[axis] + (1 - 2 * self.mine(key)) * (1 << k)
        return (moved["batch"], moved["doc"])


def mesh_keys(nb, nd):
    batch = [("batch", k) for k in range(nb.bit_length() - 1)]
    doc = [("doc", k) for k in range(nd.bit_length() - 1)]
    return batch, doc


class Piece:
    def __init__(self, mat, col, rows, cols, lead, halve, both, spread):
        self.mat, self.col, self.rows, self.cols = mat, col, rows, cols
        self.lead, self.halve, self.both, self.spread = lead, halve, both, spread
        self.tile = (rows, cols)
        self.steps = (
            [("halve", key) for key in halve]
            + [("both", key) for key in both]
            + [("spread", key) for key in spread]
            + [("twin", ("doc", 0))]
        )
        self.width = cols * 2 ** len(spread)

    def buffers(self):
        two = [(2,) * (len(self.lead) - i - 1) + self.tile for i in range(len(self.halve))]
        two += [self.tile] * len(self.both)
        wide = (2,) * len(self.spread) + self.tile
        return [(2,) * len(self.lead) + self.tile] + two + [wide, wide]

    def bytes(self, i):
        kind, key = self.steps[i]
        unit = self.rows * self.cols * 2
        if kind == "halve":
            return unit * 2 ** (len(self.lead) - i - 1)
        return unit * (2 if kind == "twin" and self.spread else 1)


def plan_pieces(nb, nd, mats):
    batch, doc = mesh_keys(nb, nd)
    across = doc[1:]
    pieces = []
    for m, (rows, cols) in enumerate(mats):
        first = across[:1] if len(across) == 1 else []
        col = 0
        if first and cols % 256 == 0 and m == 0 or first and cols > 1024:
            wide = cols // 2 // 256 * 256 if m else 256
            chunk = 256 if wide % 512 else 512
            for _ in range(wide // chunk):
                pieces.append(
                    Piece(m, col, rows, chunk // 2, first + batch[::-1], first + batch, [], first)
                )
                col += chunk
        while col < cols:
            chunk = min(cols - col, 512)
            pieces.append(Piece(m, col, rows, chunk, batch[::-1], batch, across, []))
            col += chunk
    return pieces


def exchange_order(pieces, ready, topology):
    free = {}
    clock = [(ready[i], i, 0) for i in range(len(pieces))]
    done = []
    while clock:
        clock.sort()
        at, i, step = clock.pop(0)
        key = pieces[i].steps[step][1]
        link, weight, rate = topology[key]
        start = max(at, free.get(link, 0.0))
        end = start + pieces[i].bytes(step) * weight / rate
        free[link] = end
        done.append((end + 1.5, i, step))
        if step + 1 < len(pieces[i].steps):
            clock.append((end + 2.0, i, step + 1))
    return [(i, step) for _, i, step in sorted(done)]


class Flow:
    def __init__(self, piece, bufs, send, recv, base, spot):
        self.p, self.bufs, self.send, self.recv, self.base, self.spot = piece, bufs, send, recv, base, spot
        self.live = {}
        self.copies = []

    @property
    def grad(self):
        return self.bufs[0]

    def index(self, fixed):
        return tuple(fixed.get(key, slice(None)) for key in self.p.lead)

    def start(self, step):
        kind, key = self.p.steps[step]
        mine = self.spot.mine(key)
        n = len(self.p.halve) + len(self.p.both)
        if kind == "halve":
            src = self.bufs[0].at[self.index({**self.live, key: 1 - mine})]
            dst = self.bufs[1 + step]
        elif kind == "both":
            src = self.bufs[0].at[self.index(self.live)]
            dst = self.bufs[1 + step]
        elif kind == "spread":
            src = self.bufs[n + 1].at[mine]
            dst = self.bufs[n + 1].at[mine]
        else:
            src = self.bufs[n + 1]
            dst = self.bufs[n + 2]
        copy = pltpu.make_async_remote_copy(
            src_ref=src,
            dst_ref=dst,
            send_sem=self.send.at[self.base + step],
            recv_sem=self.recv.at[self.base + step],
            device_id=self.spot.peer(key),
            device_id_type=MESH,
        )
        copy.start()
        self.copies.append(copy)

    def finish(self, step):
        kind, key = self.p.steps[step]
        copy = self.copies[step]
        if kind == "both":
            copy.wait()
        else:
            copy.wait_recv()
        n = len(self.p.halve) + len(self.p.both)
        if kind in ("halve", "both"):
            if kind == "halve":
                self.live[key] = self.spot.mine(key)
            got = self.bufs[1 + step]
            free = [k for k in self.p.lead if k not in self.live]
            last = step + 1 == n
            for pick in itertools.product(range(2), repeat=len(free)):
                at = self.index({**self.live, **dict(zip(free, pick))})
                total = self.bufs[0][at] + got[pick]
                if last:
                    self.bufs[n + 1][tuple(self.spot.mine(k) for k in self.p.spread)] = total
                else:
                    self.bufs[0][at] = total

    def drain(self):
        for step, copy in enumerate(self.copies):
            if self.p.steps[step][0] != "both":
                copy.wait_send()


def link_table(nb, nd):
    batch, doc = mesh_keys(nb, nd)
    table = {key: (key, 2.0, 91e3) for key in batch + doc}
    table[("doc", 0)] = ("twin", 1.0, 450e3)
    if (nb, nd) == (8, 4):
        table[("batch", 1)] = ("z", 2.0, 91e3)
        table[("batch", 2)] = ("z", 4.0, 91e3)
    return table


def reduce_kernel(pieces, halves, order, n_mats, *refs):
    mats, refs = refs[:n_mats], refs[n_mats:]
    vec, refs = refs[0], refs[1:]
    outs, refs = refs[:n_mats], refs[n_mats:]
    vec_out, refs = refs[0], refs[1:]
    spot = Spot()
    nb, nd = lax.axis_size("batch"), lax.axis_size("doc")
    batch, doc = mesh_keys(nb, nd)
    keys = batch + doc
    bufs = []
    for p in pieces:
        k = len(p.buffers())
        bufs.append(refs[:k])
        refs = refs[k:]
    vec_send, vec_recv = refs[:2]
    send, recv, twin_send, twin_recv, vs, vr = refs[2:]

    barrier = pltpu.get_barrier_semaphore()
    for key in keys:
        pl.semaphore_signal(barrier, inc=1, device_id=spot.peer(key), device_id_type=MESH)
    pl.semaphore_wait(barrier, len(keys))

    core = spot.mine(("doc", 0))
    twin = spot.peer(("doc", 0))
    flows = []
    base = 0
    twins = []
    for i, p in enumerate(pieces):
        flow = Flow(p, bufs[i], send, recv, base, spot)
        base += len(p.steps)
        flows.append(flow)
        half = halves[p.mat]
        copies = []
        for j in range(2 ** len(p.spread)):
            cols = pl.ds(pl.multiple_of((1 - core) * half + p.col + j * p.cols, 128), p.cols)
            dst = flow.grad.at[j] if p.spread else flow.grad
            lead = (slice(None),) * len(batch)
            copy = pltpu.make_async_remote_copy(
                src_ref=mats[p.mat].at[lead + (slice(None), cols)],
                dst_ref=dst,
                send_sem=twin_send.at[2 * i + j],
                recv_sem=twin_recv.at[2 * i + j],
                device_id=twin,
                device_id_type=MESH,
            )
            copy.start()
            copies.append(copy)
        twins.append(copies)

    vec_now = vec[...]
    vec_copies = []

    def vec_step(i):
        vec_send[i] = vec_now.astype(jnp.bfloat16)
        copy = pltpu.make_async_remote_copy(
            src_ref=vec_send.at[i],
            dst_ref=vec_recv.at[i],
            send_sem=vs.at[i],
            recv_sem=vr.at[i],
            device_id=spot.peer(keys[i]),
            device_id_type=MESH,
        )
        copy.start()
        vec_copies.append(copy)

    vec_step(0)
    for i, p in enumerate(pieces):
        half = halves[p.mat]
        for j, copy in enumerate(twins[i]):
            copy.wait()
            cols = pl.ds(pl.multiple_of(core * half + p.col + j * p.cols, 128), p.cols)
            for pick in itertools.product(range(2), repeat=len(batch)):
                at = ((j,) if p.spread else ()) + pick
                flows[i].grad[at] = flows[i].grad[at] + mats[p.mat][pick + (slice(None), cols)]
        flows[i].start(0)
        if i + 1 < len(keys):
            vec_copies[i].wait()
            vec_now = vec_now + vec_recv[i].astype(jnp.float32)
            vec_step(i + 1)
    for i in range(len(vec_copies), len(keys) + 1):
        vec_copies[i - 1].wait()
        vec_now = vec_now + vec_recv[i - 1].astype(jnp.float32)
        if i < len(keys):
            vec_step(i)
    vec_out[...] = vec_now

    for i, step in order:
        flows[i].finish(step)
        p = pieces[i]
        if step + 1 < len(p.steps):
            flows[i].start(step + 1)
        else:
            half = halves[p.mat]
            for side, buf in ((core, bufs[i][-2]), (1 - core, bufs[i][-1])):
                for j in range(2 ** len(p.spread)):
                    cols = pl.ds(pl.multiple_of(side * half + p.col + j * p.cols, 128), p.cols)
                    outs[p.mat][:, cols] = buf[j] if p.spread else buf[...]
    for flow in flows:
        flow.drain()


def reduce_params(mats, vectors, nb, nd):
    batch, doc = mesh_keys(nb, nd)
    shares = [(m.shape[0] // nb, m.shape[1]) for m in mats]
    halves = [c // 2 for _, c in shares]
    pieces = plan_pieces(nb, nd, [(r, c // 2) for r, c in shares])
    order = exchange_order(pieces, [3.0 * i for i in range(len(pieces))], link_table(nb, nd))
    keys = batch + doc
    scratch = []
    for p in pieces:
        scratch += [pltpu.VMEM(shape, jnp.bfloat16) for shape in p.buffers()]
    scratch += [pltpu.VMEM((len(keys),) + vectors.shape, jnp.bfloat16)] * 2
    steps = sum(len(p.steps) for p in pieces)
    dma = pltpu.SemaphoreType.DMA
    scratch += [dma((steps,)), dma((steps,)), dma((2 * len(pieces),)), dma((2 * len(pieces),))]
    scratch += [dma((len(keys),)), dma((len(keys),))]
    vm = pl.BlockSpec(memory_space=pltpu.VMEM)
    return pl.pallas_call(
        partial(reduce_kernel, pieces, halves, order, len(mats)),
        out_shape=[jax.ShapeDtypeStruct(s, jnp.bfloat16) for s in shares]
        + [jax.ShapeDtypeStruct(vectors.shape, jnp.float32)],
        in_specs=[vm] * (len(mats) + 1),
        out_specs=[vm] * (len(mats) + 1),
        scratch_shapes=scratch,
        compiler_params=pltpu.CompilerParams(
            collective_id=0, has_side_effects=True, vmem_limit_bytes=VMEM_BYTES
        ),
    )(*[m.reshape((2,) * len(batch) + (m.shape[0] // nb, m.shape[1])) for m in mats], vectors)


F32, BF16 = jnp.float32, jnp.bfloat16
NT = (((1,), (1,)), ((), ()))
TN = (((0,), (0,)), ((), ()))
EPS = 1e-06


def mm(a, b):
    return jnp.dot(a, b, preferred_element_type=F32)


def mm_nt(a, b):
    return lax.dot_general(a, b, NT, preferred_element_type=F32)


def mm_tn(a, b):
    return lax.dot_general(a, b, TN, preferred_element_type=F32)


def mm_exact(a, b, dims=(((1,), (0,)), ((), ()))):
    return lax.dot_general(a, b, dims, preferred_element_type=F32, precision=lax.Precision.HIGHEST)


def iota(shape, axis):
    return lax.broadcasted_iota(jnp.int32, shape, axis)


def normed(z):
    centred = z - jnp.mean(z, -1, keepdims=True)
    rstd = lax.rsqrt(jnp.mean(centred * centred, -1, keepdims=True) + EPS)
    return centred * rstd, rstd


def norm_back(grad, hat, rstd, gain):
    g = grad * gain
    inner = g - jnp.mean(g, -1, keepdims=True) - hat * jnp.mean(g * hat, -1, keepdims=True)
    return rstd * inner


def gelu(x):
    return 0.5 * x * (1.0 + lax.erf(x * math.sqrt(0.5)))


def gelu_slope(x):
    density = jnp.exp(-0.5 * x * x) * (1.0 / math.sqrt(2.0 * math.pi))
    return 0.5 * (1.0 + lax.erf(x * math.sqrt(0.5))) + x * density


def column_of(row_block):
    n, m = row_block.shape
    diag = iota((m, m), 0) == iota((m, m), 1)
    cols = [
        jnp.sum(jnp.where(diag, jnp.broadcast_to(row_block[i : i + 1, :], (m, m)), 0), 1, keepdims=True)
        for i in range(n)
    ]
    return jnp.concatenate(cols, 0)


class Net:
    def __init__(self, send, recv):
        self.send, self.recv, self.sends, self.recvs, self.open, self.due = send, recv, 0, 0, [], {}

    def branch(self):
        twin = Net(self.send, self.recv)
        twin.open = list(self.open)
        twin.due = {k: list(v) for k, v in self.due.items()}
        return twin

    def take(self):
        self.sends += 1
        self.recvs += 1
        return self.sends - 1, self.recvs - 1

    def copy(self, src, dst, peer, at):
        return pltpu.make_async_remote_copy(
            src_ref=src,
            dst_ref=dst,
            send_sem=self.send.at[at[0]],
            recv_sem=self.recv.at[at[1]],
            device_id=peer,
            device_id_type=MESH,
        )

    def put(self, src, dst, peer, at):
        self.copy(src, dst, peer, at).start()

    def group(self, due, copies, whole):
        at = self.take()
        for src, dst, peer in copies:
            self.put(src, dst, peer, at)
        all_of = self.copy(whole(len(copies)), whole(len(copies)), copies[0][2], at)
        self.expect(due, all_of.wait_recv)
        self.open.append(all_of.wait_send)

    def expect(self, due, wait):
        self.due.setdefault(due, []).append(wait)

    def collect(self, due):
        for wait in self.due.pop(due):
            wait()

    def drain(self):
        for wait in self.open:
            wait()
        self.open = []


class Trip:
    def __init__(self, tile, lead, halve, both, end):
        self.tile, self.lead, self.halve, self.both = tile, lead, halve, both
        self.steps = [("halve", k) for k in halve] + [("both", k) for k in both]
        self.sums = len(self.steps)
        ends = {"": [], "two": [("spread", ("doc", 1)), ("twin", ("doc", 0))], "three": [("three", None)]}
        self.steps += ends[end]
        self.end = end

    def buffers(self):
        shapes = [(2,) * len(self.lead) + self.tile]
        shapes += [(2,) * (len(self.lead) - i - 1) + self.tile for i in range(len(self.halve))]
        shapes += [self.tile] * len(self.both)
        return shapes + [((4,) if self.end else ()) + self.tile]

    def bytes(self, i):
        kind, key = self.steps[i]
        unit = 2 * math.prod(self.tile)
        if kind == "halve":
            return unit * 2 ** (len(self.lead) - i - 1)
        return unit * {"twin": 2, "three": 2}.get(kind, 1)


class TripRun:
    def __init__(self, trip, bufs, sems, net, spot):
        self.t, self.bufs, self.at_step, self.net, self.spot = trip, bufs, sems, net, spot
        self.live = {}

    @property
    def final(self):
        return self.bufs[-1]

    def at(self, fixed):
        return tuple(fixed.get(key, slice(None)) for key in self.t.lead)

    def place(self):
        return (2 * self.spot.mine(("doc", 0)) + self.spot.mine(("doc", 1)),) if self.t.end else ()

    def start(self, step):
        kind, key = self.t.steps[step]
        if kind == "three":
            mine = self.final.at[self.place()]
            sem = self.at_step[step]
            for peer in self.spot.others():
                self.net.put(mine, mine, peer, sem)
            view = self.final.at[pl.ds(0, 3)]
            copy = self.net.copy(view, view, self.spot.peer(("doc", 0)), sem)
            self.net.expect(sem, copy.wait_recv)
            self.net.open.append(copy.wait_send)
            return
        if kind == "halve":
            src = self.bufs[0].at[self.at({**self.live, key: 1 - self.spot.mine(key)})]
            dst = self.bufs[1 + step]
        elif kind == "both":
            src, dst = self.bufs[0].at[self.at(self.live)], self.bufs[1 + step]
        elif kind == "spread":
            src = dst = self.final.at[self.place()]
        else:
            src = dst = self.final.at[pl.ds(2 * self.spot.mine(key), 2)]
        at = self.at_step[step]
        copy = self.net.copy(src, dst, self.spot.peer(key), at)
        copy.start()
        self.net.expect(at, copy.wait_recv)
        if kind == "both":
            self.net.expect(at, copy.wait_send)
        else:
            self.net.open.append(copy.wait_send)

    def finish(self, step):
        kind, key = self.t.steps[step]
        self.net.collect(self.at_step[step])
        if step < self.t.sums:
            if kind == "halve":
                self.live[key] = self.spot.mine(key)
            got = self.bufs[1 + step]
            free = [k for k in self.t.lead if k not in self.live]
            for pick in itertools.product(range(2), repeat=len(free)):
                at = self.at({**self.live, **dict(zip(free, pick))})
                total = self.bufs[0][at] + got[pick]
                if step + 1 == self.t.sums:
                    self.final[self.place()] = total
                else:
                    self.bufs[0][at] = total


ALONG_Z = 2


def layer_trips(share):
    y, z0, z1, x = ("batch", 0), ("batch", 1), ("batch", 2), ("doc", 1)
    block = [Trip((share, 384), [z1, y], [y, z1], [], "two") for _ in range(ALONG_Z)]
    block += [Trip((share, 384), [z1, z0], [z0, z1], [], "two") for _ in range(4 - ALONG_Z)]
    block += [Trip((share, 384), [z1, y], [y, z1], [], "two")]
    orders = [[y, z0, z1], [y, z0, z1], [y, z0, z1]]
    wide = [Trip((share, 128), [z1, z0, y], order, [], "three") for order in orders]
    small = Trip((16, 768), [], [], [y, z0, z1, x, ("doc", 0)], "")
    return block + wide + [small]


LINKS = {
    ("batch", 0): [("y", 2.0)],
    ("batch", 1): [("z", 2.0)],
    ("batch", 2): [("far", 4.0), ("z", 2.0)],
    ("doc", 1): [("x", 2.0)],
    ("doc", 0): [("twin", 0.2)],
    None: [("x", 2.0)],
}
IN_FLIGHT = 3
LINK_RATE = 91e3


def trip_program(trips, stages):
    def wire(i, step):
        uses = LINKS[trips[i].steps[step][1]]
        return [(link, trips[i].bytes(step) * copies / LINK_RATE) for link, copies in uses]

    def to_go(i, step):
        return sum(max(t for _, t in wire(i, n)) + 2.0 for n in range(step, len(trips[i].steps)))

    events = [(at, -1, n, 0) for n, (at, _) in enumerate(stages)]
    free, flying, waiting, program = {}, {}, {}, []
    while events:
        events.sort()
        now, kind, i, step = events.pop(0)
        if kind < 0:
            program.append(("make", i, 0))
            ready = [(n, 0) for n in stages[i][1]]
        else:
            program.append(("finish", i, step))
            flying[wire(i, step)[0][0]] -= 1
            ready = [(i, step + 1)] if step + 1 < len(trips[i].steps) else []
        for n, s in ready:
            waiting.setdefault(wire(n, s)[0][0], []).append((-to_go(n, s), n, s))
        for link, queue in waiting.items():
            while queue and flying.get(link, 0) < IN_FLIGHT:
                queue.sort()
                _, n, s = queue.pop(0)
                program.append(("start", n, s))
                flying[link] = flying.get(link, 0) + 1
                end = now
                for used, t in wire(n, s):
                    free[used] = max(now, free.get(used, 0.0)) + t
                    end = max(end, free[used])
                events.append((end + 1.8, 0, n, s))
    return program


def layer_kernel(trips, *refs):
    (
        hidden, segs, places, targets, query, doc_rows,
        bias_q, bias_v, bias_o, gain1, shift1, bias_up, bias_down, gain2, shift2,
        qkv_hbm, out_hbm, up_hbm, down_hbm, vocab_hbm,
        block_out, loss_out, grad_in, grad_query, mats_out, wide_out, vec_out,
        wqkv, wout, wup, wdown, wvoc,
        qb, kb, vb, mixed, first_norm, first_low, acc,
        x4, x4t, kvb, kv4, sp, sp_send, qm, qm_send,
        picks, tsend, trecv, target_rows, usend, urecv, ssend, srecv, logits,
        qexp, probs, probs_low,
        hints, hints_in, joint, joint_in,
        left0, left0_y, left1, left1_y, a1, a1_y, at, at_y, second_b, inner_b, rest_b, g1, g1_y, g2,
        vecs, up_bias_s,
        load_sem, send, recv, *trip_bufs,
    ) = refs
    bias_q, bias_v, bias_o, gain1, shift1, bias_up, bias_down, gain2, shift2 = (
        b[...].reshape(1, -1) for b in (bias_q, bias_v, bias_o, gain1, shift1, bias_up, bias_down, gain2, shift2)
    )
    left0, left1, a1, at, g1 = (left0, left0_y), (left1, left1_y), (a1, a1_y), (at, at_y), (g1, g1_y)
    spot = Spot()
    batch, doc = spot.at["batch"], spot.at["doc"]
    nb, nd = lax.axis_size("batch"), lax.axis_size("doc")
    core, x = spot.mine(("doc", 0)), spot.mine(("doc", 1))
    z0 = spot.mine(("batch", 1))
    rows, width = hidden.shape
    pairs, slots = places.shape
    n_pick = pairs * slots
    heads = width // HEAD_DIM
    share = width // nb
    net = Net(send, recv)

    loads = [
        pltpu.make_async_copy(qkv_hbm.at[:, pl.ds(width, 2 * width)], wqkv.at[:, pl.ds(width, 2 * width)], load_sem.at[0]),
        pltpu.make_async_copy(vocab_hbm, wvoc, load_sem.at[1]),
        pltpu.make_async_copy(qkv_hbm.at[:, pl.ds(0, width)], wqkv.at[:, pl.ds(0, width)], load_sem.at[2]),
        pltpu.make_async_copy(out_hbm, wout, load_sem.at[3]),
        pltpu.make_async_copy(up_hbm, wup, load_sem.at[4]),
        pltpu.make_async_copy(down_hbm, wdown, load_sem.at[5]),
    ]
    for load in loads:
        load.start()

    batch_peers = [(lax.rem(batch + j, nb), doc) for j in range(1, nb)]
    doc_peers = [(batch, lax.rem(doc + j, nd)) for j in range(1, nd)]

    def side_peer(dx, dz, to_core, key):
        tx = lax.rem(x + dx, 2)
        mine = spot.mine(key)
        tz = lax.rem(mine + dz, 2)
        return (batch + (tz - mine) * (1 << key[1]), 2 * tx + to_core), tx, tz

    routes = [("batch", 1), ("batch", 0)]
    twin = spot.peer(("doc", 0))
    slots_of = [4 * spot.mine(key) + doc for key in routes]

    def fan(due, part_of, dst, lanes, to_core, dzs, route):
        slot = slots_of[route]
        sem = net.take()
        land = dst.at[slot, :, pl.ds(0, lanes)]
        always = 0
        for dz in dzs:
            for dx in range(2):
                peer, tx, tz = side_peer(dx, dz, to_core, routes[route])
                copy = net.copy(part_of(tx, tz), land, peer, sem)
                if dx or dz:
                    copy.start()
                    always += 1
                else:
                    pl.when(core != to_core)(copy.start)
        own = 0 in dzs

        def sized(n):
            view = dst.at[pl.ds(0, n), :, pl.ds(0, lanes)]
            return net.copy(view, view, twin, sem)

        def sent():
            if own:
                pl.when(core != to_core)(sized(always + 1).wait_send)
                pl.when(core == to_core)(sized(always).wait_send)
            else:
                sized(always).wait_send()

        net.open.append(sent)
        net.expect(due, lambda: pl.when(core == to_core)(sized(4 * len(dzs) - own).wait_recv))

    far = [
        side_peer(dx, 1, lax.rem(core + dc, 2), key)[0] for key in routes for dx, dc in ((1, 0), (1, 1), (0, 1))
    ]
    everyone = batch_peers + doc_peers + far
    barrier = pltpu.get_barrier_semaphore()
    for peer in everyone:
        pl.semaphore_signal(barrier, inc=1, device_id=peer, device_id_type=MESH)

    place_col = column_of(places[...])
    pick_bool = iota((n_pick, rows), 1) == place_col
    pick = pick_bool.astype(BF16)
    pick_f32 = pick_bool.astype(F32)
    tokens = hidden[...]
    loads[0].wait()
    kb[...] = mm(tokens, wqkv[:, width : 2 * width]).astype(BF16)
    vb[...] = (mm(tokens, wqkv[:, 2 * width :]) + bias_v).astype(BF16)
    tokens_p = mm(pick, tokens).astype(BF16)

    pl.semaphore_wait(barrier, len(everyone))
    own_part = query.shape[1]
    spread_lanes = (iota((own_part, own_part * nd), 0) + own_part * doc == iota((own_part, own_part * nd), 1)).astype(F32)
    hints[0:pairs, :] = mm_exact(query[...], spread_lanes)
    hints[8 : 8 + pairs, :] = doc_rows[...]
    hints_in[doc, 0:pairs, :] = hints[0:pairs, :]
    hints_in[doc, 8 : 8 + pairs, :] = hints[8 : 8 + pairs, :]
    net.group("hint", [(hints, hints_in.at[doc], peer) for peer in doc_peers], lambda n: hints_in.at[pl.ds(0, n)])
    beside = spot.peer(("doc", 1))
    net.group("tokens", [(hidden, x4.at[doc], beside)], lambda n: x4.at[pl.ds(0, n)])
    net.group("all tokens", [(hidden, x4.at[doc], twin)], lambda n: x4.at[pl.ds(0, n)])
    x4[doc] = hidden[...]

    loads[1].wait()
    entries = wvoc.shape[0]
    target_col = jnp.concatenate([column_of(targets[j]) for j in range(nb)], 0) - batch * entries
    all_rows = nb * n_pick
    is_target = iota((all_rows, entries), 1) == target_col
    tsend[...] = mm(is_target.astype(BF16), wvoc[...]).astype(BF16).reshape(nb, nd, n_pick // nd, width)
    trecv[batch] = tsend[batch, doc]
    net.group("part", [(tsend.at[p[0], doc], trecv.at[batch], p) for p in batch_peers], lambda n: trecv.at[pl.ds(0, n)])

    loads[2].wait()
    query_p = (mm(tokens_p, wqkv[:, 0:width]) + bias_q).astype(BF16)

    tall = heads * n_pick
    own_head = iota((tall, width), 0) // n_pick == iota((tall, width), 1) // HEAD_DIM

    def expand(v):
        return jnp.where(own_head, jnp.concatenate([v] * heads, 0), jnp.zeros((), v.dtype))

    def fold(v):
        return jnp.sum(jnp.where(own_head, v, 0.0).reshape(heads, n_pick, width), 0)

    seg_row = segs[...]
    seg_pick = jnp.sum(jnp.where(pick_bool, jnp.broadcast_to(seg_row, (n_pick, rows)), 0), 1, keepdims=True)
    same_pick = seg_pick == seg_row
    scale = 1.0 / math.sqrt(HEAD_DIM)
    qexp[...] = expand(query_p)
    scores = mm_nt(qexp[...], kb[...]) * scale
    same_tall = jnp.concatenate([same_pick.astype(F32)] * heads, 0) > 0.5
    scores = jnp.where(same_tall, scores, -1e30)
    weights = jnp.exp(scores - jnp.max(scores, -1, keepdims=True))
    weights = weights / jnp.sum(weights, -1, keepdims=True)
    probs[...] = weights
    probs_low[...] = weights.astype(BF16)
    mixed_p = fold(mm(probs_low[...], vb[...])).astype(BF16)
    loads[3].wait()
    attended = mm(mixed_p, wout[...]) + bias_o
    hat1, rstd1 = normed(tokens_p.astype(F32) + attended)
    first_p = hat1 * gain1 + shift1
    first_low_p = first_p.astype(BF16)
    loads[4].wait()
    inner_p = mm(first_low_p, wup[...]) + bias_up
    active_p = gelu(inner_p).astype(BF16)
    loads[5].wait()
    second_p = mm(active_p, wdown[...]) + bias_down
    hat2, rstd2 = normed(first_p + second_p)
    picks[batch] = (hat2 * gain2 + shift2).astype(BF16)
    net.group("pick", [(picks.at[batch], picks.at[batch], p) for p in batch_peers], lambda n: picks.at[pl.ds(0, n)])

    ff = wup.shape[1]
    counts = [ALONG_Z, 4 - ALONG_Z]
    firsts = [0, ALONG_Z]
    quads = [(z1, other) for z1 in range(2) for other in range(2)]
    lanes0 = [4 * share * (counts[0] + 1), 4 * share * counts[1]]
    lanes1 = [8 * share, 4 * share]
    for route in range(2):
        wide_lanes = share * counts[route]
        for k in range(2):
            for n, (z1, other) in enumerate(quads):
                b = 4 * z1 + (2 * k + other if route == 0 else 2 * other + k)
                own = slice(b * share, (b + 1) * share)
                start = 4 * share * b + share * firsts[route]
                left0[route][k, :, n * wide_lanes : (n + 1) * wide_lanes] = active_p[:, start : start + wide_lanes]
                left1[route][k, :, n * share : (n + 1) * share] = first_low_p[:, own]
                if route == 0:
                    at0 = 4 * wide_lanes + n * share
                    left0[route][k, :, at0 : at0 + share] = mixed_p[:, own]
                    left1[route][k, :, (4 + n) * share : (5 + n) * share] = tokens_p[:, own]

    def keep_left(route, left, lanes):
        def keep():
            a1[route][slots_of[route], :, 0:lanes] = left[route][spot.mine(routes[route])]

        return keep

    for route in range(2):
        pl.when(core == 0)(keep_left(route, left0, lanes0[route]))
        pl.when(core == 1)(keep_left(route, left1, lanes1[route]))

    def send_left(dzs):
        for route in range(2):
            fan("left", lambda tx, tz: left0[route].at[tz], a1[route], lanes0[route], 0, dzs, route)
            fan("left", lambda tx, tz: left1[route].at[tz], a1[route], lanes1[route], 1, dzs, route)

    half_w, half_f = width // 2, ff // 2
    tall_half = tall // 2
    send_left([0])

    def half_heads(due, src, dst, to_core):
        sem = net.take()
        for dx in range(2):
            peer, tx, _ = side_peer(dx, 0, to_core, routes[0])
            copy = net.copy(src.at[tx], dst.at[doc], peer, sem)
            if dx:
                copy.start()
            else:
                pl.when(core != to_core)(copy.start)

        def keep():
            dst[doc] = src[x]

        def sized(n):
            view = dst.at[pl.ds(0, n)]
            return net.copy(view, view, twin, sem)

        def sent():
            pl.when(core != to_core)(sized(2).wait_send)
            pl.when(core == to_core)(sized(1).wait_send)

        pl.when(core == to_core)(keep)
        net.open.append(sent)
        net.expect(due, lambda: pl.when(core == to_core)(sized(3).wait_recv))

    def halves(dst, v):
        for s in range(2):
            dst[s] = v[:, s * half_w : (s + 1) * half_w]

    sp_send[1] = probs_low[...].reshape(2, tall_half, rows)
    half_heads("heads", sp_send.at[1], sp, 1)
    halves(qm_send.at[0], query_p)
    half_heads("heads", qm_send.at[0], qm, 0)

    seg_col = jnp.sum(
        jnp.where(iota((rows, rows), 0) == iota((rows, rows), 1), jnp.broadcast_to(seg_row, (rows, rows)), 0),
        1,
        keepdims=True,
    )
    qb[...] = (mm(tokens, wqkv[:, 0:width]) + bias_q).astype(BF16)

    def attend(i):
        lanes = pl.ds(pl.multiple_of(i * 128, 128), 128)
        q_s, k_s, v_s = qb[:, lanes], kb[:, lanes], vb[:, lanes]
        low = iota((rows, 128), 1) < HEAD_DIM
        same = seg_col == seg_row
        parts = []
        for side in (low, ~low):
            s = mm_nt(jnp.where(side, q_s, jnp.zeros((), BF16)), k_s) * scale
            s = jnp.where(same, s, -1e30)
            e = jnp.exp(s - jnp.max(s, -1, keepdims=True))
            p = (e / jnp.sum(e, -1, keepdims=True)).astype(BF16)
            parts.append(mm(p, v_s))
        mixed[:, lanes] = jnp.where(low, parts[0], parts[1]).astype(BF16)

    half_way = width // 256
    pl.loop(0, half_way)(attend)
    send_left([1])
    net.collect("tokens")
    net.group("all tokens", [(x4.at[beside[1]], x4.at[beside[1]], twin)], lambda n: x4.at[pl.ds(0, n)])
    net.collect("part")
    part = trecv[0].astype(F32)
    for j in range(1, nb):
        part += trecv[j].astype(F32)
    target_rows[doc] = part.astype(BF16)
    net.group("target", [(target_rows.at[doc], target_rows.at[doc], p) for p in doc_peers], lambda n: target_rows.at[pl.ds(0, n)])
    pl.loop(half_way, width // 128)(attend)

    net.collect("pick")
    logits[...] = mm_nt(picks[...].reshape(all_rows, width), wvoc[...])
    lg = logits[...]
    top = jnp.max(lg, 1, keepdims=True)
    chosen = jnp.sum(jnp.where(is_target, lg, 0.0), 1, keepdims=True)
    others = jnp.where(is_target, 0.0, jnp.exp(lg - top))
    total = jnp.sum(others, 1, keepdims=True)
    lane = iota((all_rows, 128), 1)
    stats = jnp.where(lane == 0, top, jnp.where(lane == 1, total, chosen)).T
    blank = jnp.zeros((8, 128 - n_pick), F32)
    for j in range(nb):
        ssend[j] = jnp.concatenate([stats[0:8, n_pick * j : n_pick * (j + 1)], blank], 1)
    srecv[batch] = ssend[batch]
    net.group("stats", [(ssend.at[p[0]], srecv.at[batch], p) for p in batch_peers], lambda n: srecv.at[pl.ds(0, n)])
    usend[...] = mm(others.astype(BF16), wvoc[...]).astype(BF16).reshape(nb, n_pick, width)
    urecv[batch] = usend[batch]
    net.group("back", [(usend.at[p[0]], urecv.at[batch], p) for p in batch_peers], lambda n: urecv.at[pl.ds(0, n)])

    tokens = hidden[...]
    hat, _ = normed(tokens.astype(F32) + mm(mixed[...], wout[...]) + bias_o)
    first_norm[...] = hat * gain1 + shift1
    first_low[...] = first_norm[...].astype(BF16)
    acc[...] = first_norm[...] + bias_down
    chunk = 512
    up_bias_s[...] = bias_up

    def feed(i):
        cols = pl.ds(pl.multiple_of(i * chunk, chunk), chunk)
        hid = mm(first_low[...], wup[:, cols]) + up_bias_s[:, cols]
        acc[...] += mm(gelu(hid).astype(BF16), wdown[cols, :])

    pl.loop(0, ff // chunk // 2)(feed)

    net.collect("stats")
    tops = [srecv[j][0:1, :] for j in range(nb)]
    peak = tops[0]
    for t in tops[1:]:
        peak = jnp.maximum(peak, t)
    factors = [jnp.exp(t - peak) for t in tops]
    rest = jnp.zeros_like(peak)
    chosen = jnp.zeros_like(peak)
    for j in range(nb):
        rest += factors[j] * srecv[j][1:2, :]
        chosen += srecv[j][2:3, :]
    whole = rest + jnp.exp(chosen - peak)
    logp = chosen - peak - jnp.log(whole)
    of_pair = iota((pairs, 128), 1) // slots == iota((pairs, 128), 0)
    reader = jnp.sum(jnp.where(of_pair, jnp.broadcast_to(logp, (pairs, 128)), 0.0), 1, keepdims=True) / slots
    joint[...] = jnp.zeros_like(joint)
    joint[0:pairs, :] = jnp.broadcast_to(reader, (pairs, 128))
    joint_in[doc] = joint[...]
    net.group("joint", [(joint, joint_in.at[doc], p) for p in doc_peers], lambda n: joint_in.at[pl.ds(0, n)])
    shares = jnp.concatenate([f / whole for f in factors] + [rest / whole] + [jnp.zeros_like(peak)] * (15 - nb), 0).T

    pl.loop(ff // chunk // 2, ff // chunk)(feed)
    hat, _ = normed(acc[...])
    block_out[...] = (hat * gain2 + shift2).astype(BF16)
    net.collect("all tokens")
    x4t[...] = x4[...].reshape(nd * rows, width).T

    net.collect("hint")
    full_query = hints_in[0, 0:pairs, :]
    for j in range(1, nd):
        full_query += hints_in[j, 0:pairs, :]
    docs = [hints_in[j, 8 : 8 + pairs, :] for j in range(nd)]
    score = [jnp.broadcast_to(jnp.sum(full_query * d, 1, keepdims=True), (pairs, 128)) for d in docs]
    net.collect("joint")
    both = [s + joint_in[j, 0:pairs, :] for j, s in enumerate(score)]

    def soft(vals):
        high = vals[0]
        for v in vals[1:]:
            high = jnp.maximum(high, v)
        es = [jnp.exp(v - high) for v in vals]
        tot = es[0]
        for e in es[1:]:
            tot = tot + e
        return [e / tot for e in es], high + jnp.log(tot)

    w_score, total_score = soft(score)
    w_joint, total_joint = soft(both)
    eye = iota((pairs, 128), 0) == iota((pairs, 128), 1)
    loss_out[...] = jnp.sum(jnp.where(eye, total_score - total_joint, 0.0), 0, keepdims=True)
    query_grad = (w_score[0] - w_joint[0]) * docs[0]
    for j in range(1, nd):
        query_grad += (w_score[j] - w_joint[j]) * docs[j]
    grad_query[...] = mm_exact(query_grad, spread_lanes, NT)
    mine = w_joint[0]
    for j in range(1, nd):
        mine = jnp.where(doc == j, w_joint[j], mine)
    row_weight = jnp.broadcast_to(mine.reshape(pairs, 1, 128), (pairs, slots, 128)).reshape(n_pick, 128)[:, 0:1]

    net.collect("left")

    def turn(route, lanes):
        def go():
            at[route][0:lanes, :] = a1[route][:, :, 0:lanes].reshape(8 * n_pick, lanes).T

        return go

    for route in range(2):
        pl.when(core == 0)(turn(route, lanes0[route]))
        pl.when(core == 1)(turn(route, lanes1[route]))

    net.collect("back")
    row_grad = jnp.zeros((n_pick, width), F32)
    for j in range(nb):
        row_grad += shares[0:n_pick, j : j + 1] * urecv[j].astype(F32)
    net.collect("target")
    at_target = target_rows[...].astype(F32).reshape(n_pick, width)
    row_grad -= shares[0:n_pick, nb : nb + 1] * at_target
    final_grad = row_grad * (row_weight / slots)

    def send_right(due, src, every, first, cols, dst, to_core, route):
        def part(tx):
            return pl.ds(pl.multiple_of(tx * every + first, 128), cols)

        fan(due, lambda tx, tz: src.at[:, part(tx)], dst, cols, to_core, [0, 1], route)

        def keep():
            dst[slots_of[route], :, 0:cols] = src[:, part(x)]

        pl.when(core == to_core)(keep)

    vecs[...] = jnp.zeros_like(vecs)
    sum_grad = norm_back(final_grad, hat2, rstd2, gain2)
    vecs[6:7, :] = jnp.sum(final_grad * hat2, 0, keepdims=True)
    vecs[7:8, :] = jnp.sum(final_grad, 0, keepdims=True)
    vecs[5:6, :] = jnp.sum(sum_grad, 0, keepdims=True)
    second_low = sum_grad.astype(BF16)
    second_b[...] = second_low
    for route in range(2):
        send_right(("g1", route), second_b, half_w, 0, half_w, g1[route], 0, route)
    inner_grad = mm_nt(second_low, wdown[...]) * gelu_slope(inner_p)
    inner_low = inner_grad.astype(BF16)
    inner_b[...] = inner_low
    for route in range(2):
        first, cols = firsts[route] * half_w, counts[route] * half_w
        send_right(("g1", route), inner_b, half_f, first, cols, g1[route], 1, route)
    up_bias_grad = jnp.sum(inner_grad, 0, keepdims=True)
    for i in range(ff // width):
        vecs[8 + i : 9 + i, :] = up_bias_grad[:, i * width : (i + 1) * width]
    first_grad = sum_grad + mm_nt(inner_low, wup[...])
    resid_grad = norm_back(first_grad, hat1, rstd1, gain1)
    resid_low = resid_grad.astype(BF16)
    rest_b[0] = resid_low
    send_right("g2", rest_b.at[0], half_w, 0, half_w, g2, 0, 0)
    vecs[3:4, :] = jnp.sum(first_grad * hat1, 0, keepdims=True)
    vecs[4:5, :] = jnp.sum(first_grad, 0, keepdims=True)
    vecs[2:3, :] = jnp.sum(resid_grad, 0, keepdims=True)
    mixed_grad_p = mm_nt(resid_low, wout[...]).astype(BF16)
    halves(qm_send.at[1], mixed_grad_p)
    half_heads("heads", qm_send.at[1], qm, 1)
    mixed_grad = expand(mixed_grad_p)
    prob_grad = mm_nt(mixed_grad, vb[...])
    p = probs[...]
    score_low = (p * (prob_grad - jnp.sum(prob_grad * p, -1, keepdims=True)) * scale).astype(BF16)
    sp_send[0] = score_low.reshape(2, tall_half, rows)
    half_heads("heads", sp_send.at[0], sp, 0)
    query_grad_p = fold(mm(score_low, kb[...]))
    rest_b[1] = query_grad_p.astype(BF16)
    send_right("g2", rest_b.at[1], half_w, 0, half_w, g2, 1, 0)
    vecs[0:1, :] = jnp.sum(query_grad_p, 0, keepdims=True)
    value_grad = mm_tn(probs_low[...], mixed_grad)
    kvb[1] = value_grad.astype(BF16)
    vecs[1:2, :] = jnp.sum(value_grad, 0, keepdims=True)

    sems = [[net.take() for _ in t.steps] for t in trips]
    groups, left_over = [], list(trip_bufs)
    for t in trips:
        k = len(t.buffers())
        groups.append(left_over[:k])
        left_over = left_over[k:]

    def tail(side, net):
        runs = [TripRun(t, groups[n], sems[n], net, spot) for n, t in enumerate(trips)]

        def make_wide():
            net.collect("heads")
            half_tall = iota((tall_half, half_w), 0) // n_pick == iota((tall_half, half_w), 1) // HEAD_DIM
            for d in range(nd):
                tiled = jnp.concatenate([qm[d]] * (heads // 2), 0)
                tiled = jnp.where(half_tall, tiled, jnp.zeros((), BF16))
                kv4[d] = mm_tn(sp[d], tiled).astype(BF16)
            right = kv4[...].reshape(nd * rows, half_w)
            for b in range(nb):
                out = mm(x4t[b * share : (b + 1) * share, :], right).astype(BF16)
                for n in range(3):
                    runs[5 + n].bufs[0][b // 4, b // 2 % 2, b % 2] = out[:, 128 * n : 128 * (n + 1)]

        def block(i, route, offsets, g, col):
            left = jnp.concatenate([at[route][pl.ds(pl.multiple_of(o, 32), share), :] for o in offsets], 0)
            right = g[:, :, pl.ds(col, half_w)].reshape(8 * n_pick, half_w)
            out = mm(left, right).astype(BF16)
            for n, (z1, other) in enumerate(quads):
                runs[i].bufs[0][z1, other] = out[n * share : (n + 1) * share]

        def make_blocks(route):
            net.collect(("g1", route))
            for i in range(counts[route]):
                offsets = [((1 - core) * (n * counts[route] + i) + core * n) * share for n in range(4)]
                block(firsts[route] + i, route, offsets, g1[route], pl.multiple_of(core * i * half_w, 128))

        def make_last():
            net.collect("g2")
            first_row = (1 - core) * 4 * share * counts[0] + core * 4 * share
            block(4, 0, [first_row + n * share for n in range(4)], g2, 0)

        def make_inward():
            kvb[0] = mm_tn(score_low, qexp[...]).astype(BF16)
            inward = mm_nt(kvb[0], wqkv[:, width : 2 * width]) + mm_nt(kvb[1], wqkv[:, 2 * width :])
            at_rows = resid_grad + mm_nt(rest_b[1], wqkv[:, 0:width])
            grad_in[...] = (inward + mm_exact(pick_f32, at_rows, TN)).astype(BF16)

        def make_sums():
            runs[8].bufs[0][...] = vecs[...].astype(BF16)

        along_y = list(range(ALONG_Z, 4))
        along_z = list(range(ALONG_Z))
        stages = (
            [
                (0.0, [8], make_sums),
                (0.6, along_y, lambda: make_blocks(1)),
                (1.2, along_z, lambda: make_blocks(0)),
                (1.8, [4], make_last),
                (8.0, [5, 6, 7], make_wide),
                (12.0, [], make_inward),
            ]
            if side == 0
            else [
                (0.0, [8], make_sums),
                (2.5, [5, 6, 7], make_wide),
                (5.0, along_y, lambda: make_blocks(1)),
                (5.6, along_z, lambda: make_blocks(0)),
                (6.2, [4], make_last),
                (10.0, [], make_inward),
            ]
        )
        last = []
        for what, i, step in trip_program(trips, [(t, made) for t, made, _ in stages]):
            if what == "make":
                stages[i][2]()
            elif what == "start":
                runs[i].start(step)
            elif trips[i].steps[step][1] in (("doc", 0), None):
                last.append((i, step))
            else:
                runs[i].finish(step)
        for i, step in last:
            runs[i].finish(step)
            if i < 5:
                mats_out[i] = runs[i].final[...].reshape(mats_out.shape[1:])
            elif i < 8:
                wide_out[i - 5] = runs[i].final[...].reshape(wide_out.shape[1:])
            else:
                vec_out[...] = runs[i].final[...]
        net.drain()

    for side in range(2):
        pl.when(core == side)(partial(tail, side, net.branch()))


def finish_kernel(block, grad, loss, gq, mats, wide, vec, *outs):
    (o_block, o_loss, o_grad, o_gq, o_qkv, o_qb, o_vb, o_out, o_ob, o_g1, o_s1, o_up, o_ub, o_down, o_db, o_g2, o_s2) = outs
    batch = lax.axis_index("batch")
    nb = lax.axis_size("batch")
    width = vec.shape[1]
    share, half = width // nb, width // 2
    o_block[...] = block[...]
    o_grad[...] = grad[...]
    o_loss[...] = loss[:, 0 : o_loss.shape[1]]
    o_gq[...] = gq[...]
    for s in range(2):
        cols = slice(s * half, (s + 1) * half)
        o_out[:, cols] = mats[4, 0, s].astype(F32)
        o_qkv[:, cols] = mats[4, 1, s].astype(F32)
        for i in range(4):
            o_down[i * share : (i + 1) * share, cols] = mats[i, 0, s].astype(F32)
            o_up[:, (4 * s + i) * half : (4 * s + i + 1) * half] = mats[i, 1, s].astype(F32)
        for c in range(2):
            for j in range(3):
                start = (1 + c) * width + s * half + 128 * j
                o_qkv[:, start : start + 128] = wide[j, c, s].astype(F32)
    v = vec[...].astype(F32)
    take = (iota((width, share), 0) == iota((width, share), 1) + batch * share).astype(F32)
    got = mm_exact(v, take)
    for i, o in enumerate((o_qb, o_vb, o_ob, o_g1, o_s1, o_db, o_g2, o_s2)):
        o[...] = got[i : i + 1, :]
    side = jnp.where(lax.rem(batch, 2) == 0, v[8:12, 0:half], v[8:12, half:])
    o_ub[...] = jnp.sum(jnp.where(iota((4, half), 0) == batch // 2, side, 0.0), 0)


def paired_local(*args):
    (
        hidden_in, segments, mask_pos, target_ids, query_emb, doc_emb,
        qkv_weight, query_bias, value_bias, out_weight, out_bias, gain_one, shift_one,
        up_weight, up_bias, down_weight, down_bias, gain_two, shift_two, vocab,
    ) = args
    rows, width = hidden_in.shape[2:]
    pairs, slots = mask_pos.shape[2:]
    n_pick = pairs * slots
    ff = up_weight.shape[1]
    entries = vocab.shape[0]
    nb, nd = lax.axis_size("batch"), lax.axis_size("doc")
    share = width // nb
    heads = width // HEAD_DIM
    trips = layer_trips(share)
    lanes_z, lanes_y = 4 * share * (ALONG_Z + 1), 4 * share * (4 - ALONG_Z)
    n_sems = sum(len(t.steps) for t in trips) + 28
    vm, hbm = pl.BlockSpec(memory_space=pltpu.VMEM), pl.BlockSpec(memory_space=pl.ANY)

    def v(shape, dtype=BF16):
        return pltpu.VMEM(shape, dtype)

    dma = pltpu.SemaphoreType.DMA
    scratch = [
        v(qkv_weight.shape), v(out_weight.shape), v(up_weight.shape), v(down_weight.shape), v(vocab.shape),
        v((rows, width)), v((rows, width)), v((rows, width)), v((rows, width)),
        v((rows, width), F32), v((rows, width)), v((rows, width), F32),
        v((nd, rows, width)), v((width, nd * rows)), v((2, rows, width)), v((nd, rows, width // 2)),
        v((nd, heads * n_pick // 2, rows)), v((2, 2, heads * n_pick // 2, rows)),
        v((nd, n_pick, width // 2)), v((2, 2, n_pick, width // 2)),
        v((nb, n_pick, width)), v((nb, nd, n_pick // nd, width)), v((nb, n_pick // nd, width)),
        v((nd, n_pick // nd, width)), v((nb, n_pick, width)),
        v((nb, n_pick, width)), v((nb, 8, 128), F32), v((nb, 8, 128), F32), v((nb * n_pick, entries), F32),
        v((heads * n_pick, width)), v((heads * n_pick, rows), F32), v((heads * n_pick, rows)),
        v((16, 128), F32), v((nd, 16, 128), F32), v((8, 128), F32), v((nd, 8, 128), F32),
        v((2, n_pick, lanes_z)), v((2, n_pick, lanes_y)), v((2, n_pick, width)), v((2, n_pick, width // 2)),
        v((8, n_pick, lanes_z)), v((8, n_pick, max(lanes_y, width // 2))), v((lanes_z, 8 * n_pick)),
        v((max(lanes_y, width // 2), 8 * n_pick)),
        v((n_pick, width)), v((n_pick, ff)), v((2, n_pick, width)),
        v((8, n_pick, ALONG_Z * width // 2)), v((8, n_pick, (4 - ALONG_Z) * width // 2)), v((8, n_pick, width // 2)),
        v((16, width), F32), v((1, ff), F32),
        dma((6,)), dma((n_sems,)), dma((n_sems,)),
    ]
    for t in trips:
        scratch += [v(shape) for shape in t.buffers()]
    sds = jax.ShapeDtypeStruct
    first = pl.pallas_call(
        partial(layer_kernel, trips),
        out_shape=[
            sds((rows, width), BF16),
            sds((1, 128), F32),
            sds((rows, width), BF16),
            sds((pairs, query_emb.shape[2]), F32),
            sds((5, 2, 2, share, 384), BF16),
            sds((3, 2, 2, share, 128), BF16),
            sds((16, width), BF16),
        ],
        in_specs=[vm] * 15 + [hbm] * 5,
        out_specs=[vm] * 7,
        scratch_shapes=scratch,
        compiler_params=pltpu.CompilerParams(
            collective_id=0, has_side_effects=True, vmem_limit_bytes=VMEM_BYTES
        ),
        name="layer",
    )
    biases = (query_bias, value_bias, out_bias, gain_one, shift_one, up_bias, down_bias, gain_two, shift_two)
    block, loss, grad, gq, mats, wide, vec = first(
        hidden_in.reshape(rows, width),
        segments.reshape(1, rows),
        mask_pos.reshape(pairs, slots),
        target_ids,
        query_emb.reshape(pairs, -1),
        doc_emb.reshape(pairs, -1),
        *biases,
        qkv_weight,
        out_weight,
        up_weight,
        down_weight,
        vocab,
    )
    small = sds((1, share), F32)
    outs = pl.pallas_call(
        finish_kernel,
        out_shape=[
            sds((rows, width), BF16), sds((1, pairs), F32), sds((rows, width), BF16), sds(gq.shape, F32),
            sds((share, 3 * width), F32), small, small, sds((share, width), F32), small, small, small,
            sds((share, ff), F32), sds((ff // nb,), F32), sds((ff // nb, width), F32), small, small, small,
        ],
        in_specs=[vm] * 7,
        out_specs=[vm] * 17,
        compiler_params=pltpu.CompilerParams(vmem_limit_bytes=VMEM_BYTES),
        name="finish",
    )(block, grad, loss, gq, mats, wide, vec)
    shapes = [hidden_in.shape, (1, pairs), hidden_in.shape, query_emb.shape]
    fixed = [o.reshape(s) for o, s in zip(outs[:4], shapes)]
    return tuple(fixed + [o.reshape(-1) if o.shape == (1, share) else o for o in outs[4:]])


def combined_all(x, axis, combine):
    everything = jax.tree.map(lambda part: lax.all_gather(part, axis), x)
    leading = jax.tree.map(lambda part: part[0], everything)

    def hop(k, so_far):
        return combine(so_far, jax.tree.map(lambda part: part[k], everything))

    return lax.fori_loop(1, lax.axis_size(axis), hop, leading)


def norm_rows(values, gain, shift):
    centre = jnp.mean(values, -1, keepdims=True)
    centred = values - centre
    spread = jnp.mean(centred * centred, -1, keepdims=True)
    return centred * lax.rsqrt(spread + 1e-06) * gain + shift


def lse_pair(earlier, later):
    maxima = jnp.maximum(earlier[0], later[0])
    totals = earlier[1] * jnp.exp(earlier[0] - maxima) + later[1] * jnp.exp(later[0] - maxima)
    return (maxima, totals)


def vocab_pair(earlier, later):
    return lse_pair(earlier[:2], later[:2]) + (earlier[2] + later[2],)


def place_rows(places, grads, seq_len):
    return jnp.zeros((seq_len, grads.shape[-1]), jnp.float32).at[places].add(grads)


def local(
    hidden_in,
    segments,
    mask_pos,
    target_ids,
    query_emb,
    doc_emb,
    qkv_weight,
    query_bias,
    value_bias,
    out_weight,
    out_bias,
    gain_one,
    shift_one,
    up_weight,
    up_bias,
    down_weight,
    down_bias,
    gain_two,
    shift_two,
    vocab,
):
    f32 = jnp.float32
    bf16 = jnp.bfloat16
    seq_count, _, seq_len, model_width = hidden_in.shape
    pair_count = mask_pos.shape[2]
    mask_count = mask_pos.shape[3]
    head_count = model_width // HEAD_DIM
    score_scale = 1.0 / math.sqrt(HEAD_DIM)
    split_shape = (seq_count, seq_len, head_count, HEAD_DIM)
    tokens = hidden_in.reshape(seq_count, seq_len, model_width)
    segs = segments.reshape(seq_count, seq_len)
    packed = jnp.einsum("nld,de->nle", tokens, qkv_weight, preferred_element_type=f32)
    queries = (packed[..., :model_width] + query_bias).astype(bf16).reshape(split_shape)
    key_rows = packed[..., model_width : 2 * model_width].astype(bf16).reshape(split_shape)
    value_rows = (packed[..., 2 * model_width :] + value_bias).astype(bf16).reshape(split_shape)
    same_seg = (segs[:, :, None] == segs[:, None, :])[:, None]
    raw_scores = jnp.einsum("nlhe,nmhe->nhlm", queries, key_rows, preferred_element_type=f32)

    def attend(scores_in):
        return jax.nn.softmax(jnp.where(same_seg, scores_in * score_scale, -1e30), axis=-1)

    probs, soft_back = jax.vjp(attend, raw_scores)
    probs_low = probs.astype(bf16)
    mixed_heads = jnp.einsum("nhlm,nmhe->nlhe", probs_low, value_rows, preferred_element_type=f32)
    mixed_low = mixed_heads.reshape(seq_count, seq_len, model_width).astype(bf16)
    attended = (
        jnp.einsum("nld,de->nle", mixed_low, out_weight, preferred_element_type=f32) + out_bias
    )
    first_norm, norm_back_one = jax.vjp(
        norm_rows, tokens.astype(f32) + attended, gain_one, shift_one
    )
    first_low = first_norm.astype(bf16)
    inner_act = (
        jnp.einsum("nld,df->nlf", first_low, up_weight, preferred_element_type=f32) + up_bias
    )
    active, gelu_back = jax.vjp(partial(jax.nn.gelu, approximate=False), inner_act)
    active_low = active.astype(bf16)
    second = (
        jnp.einsum("nlf,fd->nld", active_low, down_weight, preferred_element_type=f32) + down_bias
    )
    final_rows, norm_back_two = jax.vjp(norm_rows, first_norm + second, gain_two, shift_two)
    per_seq = pair_count * mask_count
    rows_dev = seq_count * per_seq
    flat_places = mask_pos.reshape(seq_count, per_seq)
    picked = jnp.take_along_axis(final_rows, flat_places[:, :, None], axis=1)
    picked_low = picked.reshape(rows_dev, model_width).astype(bf16)
    logits = lax.dot_general(
        lax.all_gather(picked_low, "batch", axis=0, tiled=True),
        vocab,
        (((1,), (1,)), ((), ())),
        preferred_element_type=f32,
    )
    shard_size = vocab.shape[0]
    vocab_ids = lax.axis_index("batch") * shard_size + lax.iota(jnp.int32, shard_size)
    is_target = target_ids.reshape(-1)[:, None] == vocab_ids[None, :]
    maxima = jnp.max(logits, 1)
    totals = jnp.sum(jnp.exp(logits - maxima[:, None]), 1)
    chosen = jnp.sum(jnp.where(is_target, logits, 0.0), 1)
    maxima, totals, chosen = combined_all((maxima, totals, chosen), "batch", vocab_pair)
    log_total = maxima + jnp.log(totals)
    first_own = lax.axis_index("batch") * rows_dev
    own_logp = lax.dynamic_slice_in_dim(chosen - log_total, first_own, rows_dev)
    reader = jnp.mean(own_logp.reshape(seq_count, pair_count, mask_count), -1)
    gathered_query = lax.all_gather(query_emb, "doc", axis=2, tiled=True)
    doc_rows = doc_emb.reshape(seq_count, pair_count, doc_emb.shape[-1])
    score = jnp.sum(gathered_query * doc_rows, -1)
    joint = score + reader
    unit_terms = jnp.ones_like(score)
    score_top, score_sum = combined_all((score, unit_terms), "doc", lse_pair)
    score_total = score_top + jnp.log(score_sum)
    shifted = joint - score_total
    joint_top, joint_sum = combined_all((shifted, unit_terms), "doc", lse_pair)
    joint_total = joint_top + jnp.log(joint_sum)
    loss = -joint_total
    weight_joint = jnp.exp(shifted - joint_total)
    weight_score = jnp.exp(score - score_total)
    score_grad = weight_score - weight_joint
    grad_query = lax.psum_scatter(
        score_grad[..., None] * doc_rows, "doc", scatter_dimension=2, tiled=True
    )
    row_scale = jnp.broadcast_to(
        (weight_joint / mask_count)[..., None], (seq_count, pair_count, mask_count)
    ).reshape(rows_dev)
    all_scale = lax.all_gather(row_scale, "batch", axis=0, tiled=True)
    vocab_probs = jnp.exp(logits - log_total[:, None])
    logit_grad = (all_scale[:, None] * (vocab_probs - is_target.astype(f32))).astype(bf16)
    picked_grad = lax.psum_scatter(
        jnp.dot(logit_grad, vocab, preferred_element_type=f32).astype(jnp.bfloat16),
        "batch",
        scatter_dimension=0,
        tiled=True,
    ).astype(jnp.float32)
    final_grad = jax.vmap(partial(place_rows, seq_len=seq_len))(
        flat_places, picked_grad.reshape(seq_count, per_seq, model_width)
    )
    sum_grad, grad_gain_two, grad_shift_two = norm_back_two(final_grad)
    grad_down_bias = jnp.sum(sum_grad, (0, 1))
    second_low = sum_grad.astype(bf16)
    grad_down_weight = jnp.einsum("nlf,nld->fd", active_low, second_low, preferred_element_type=f32)
    active_grad = jnp.einsum("nld,fd->nlf", second_low, down_weight, preferred_element_type=f32)
    (inner_grad,) = gelu_back(active_grad)
    grad_up_bias = jnp.sum(inner_grad, (0, 1))
    inner_low = inner_grad.astype(bf16)
    grad_up_weight = jnp.einsum("nld,nlf->df", first_low, inner_low, preferred_element_type=f32)
    first_grad = sum_grad + jnp.einsum(
        "nlf,df->nld", inner_low, up_weight, preferred_element_type=f32
    )
    resid_grad, grad_gain_one, grad_shift_one = norm_back_one(first_grad)
    grad_out_bias = jnp.sum(resid_grad, (0, 1))
    resid_low = resid_grad.astype(bf16)
    grad_out_weight = jnp.einsum("nld,nle->de", mixed_low, resid_low, preferred_element_type=f32)
    mixed_grad = (
        jnp.einsum("nle,de->nld", resid_low, out_weight, preferred_element_type=f32)
        .astype(bf16)
        .reshape(split_shape)
    )
    value_grad = jnp.einsum("nhlm,nlhe->nmhe", probs_low, mixed_grad, preferred_element_type=f32)
    prob_grad = jnp.einsum("nlhe,nmhe->nhlm", mixed_grad, value_rows, preferred_element_type=f32)
    (score_back,) = soft_back(prob_grad)
    score_low = score_back.astype(bf16)
    query_grad = jnp.einsum("nhlm,nmhe->nlhe", score_low, key_rows, preferred_element_type=f32)
    key_grad = jnp.einsum("nhlm,nlhe->nmhe", score_low, queries, preferred_element_type=f32)
    flat_shape = (seq_count, seq_len, model_width)
    query_grad = query_grad.reshape(flat_shape)
    key_grad = key_grad.reshape(flat_shape)
    value_grad = value_grad.reshape(flat_shape)
    grad_query_bias = jnp.sum(query_grad, (0, 1))
    grad_value_bias = jnp.sum(value_grad, (0, 1))
    packed_grad = jnp.concatenate([query_grad, key_grad, value_grad], -1).astype(bf16)
    grad_qkv_weight = jnp.einsum("nld,nle->de", tokens, packed_grad, preferred_element_type=f32)
    input_grad = resid_grad + jnp.einsum(
        "nle,de->nld", packed_grad, qkv_weight, preferred_element_type=f32
    )
    vectors = jnp.concatenate(
        [
            jnp.stack(
                [
                    grad_query_bias,
                    grad_value_bias,
                    grad_out_bias,
                    grad_gain_one,
                    grad_shift_one,
                    grad_down_bias,
                    grad_gain_two,
                    grad_shift_two,
                ]
            ),
            grad_up_bias.reshape(-1, model_width),
        ]
    )
    vectors = jnp.pad(vectors, ((0, -vectors.shape[0] % 16), (0, 0)))
    mats = (grad_down_weight, grad_up_weight, grad_out_weight, grad_qkv_weight)
    down_sum, up_sum, out_sum, qkv_sum, vector_sum = reduce_params(
        [m.astype(bf16) for m in mats], vectors, lax.axis_size("batch"), lax.axis_size("doc")
    )
    nb = lax.axis_size("batch")
    slot = lax.axis_index("batch")

    def share(v):
        return lax.dynamic_slice_in_dim(v, slot * (v.shape[0] // nb), v.shape[0] // nb)

    up_bias_sum = vector_sum[8 : 8 + grad_up_bias.shape[0] // model_width].reshape(-1)
    results = (
        qkv_sum.astype(f32),
        share(vector_sum[0]),
        share(vector_sum[1]),
        out_sum.astype(f32),
        share(vector_sum[2]),
        share(vector_sum[3]),
        share(vector_sum[4]),
        up_sum.astype(f32),
        share(up_bias_sum),
        down_sum.astype(f32),
        share(vector_sum[5]),
        share(vector_sum[6]),
        share(vector_sum[7]),
    )
    block_out = final_rows.astype(bf16).reshape(hidden_in.shape)
    grad_in = input_grad.astype(bf16).reshape(hidden_in.shape)
    return (
        block_out,
        loss,
        grad_in,
        grad_query,
        results[0],
        results[1],
        results[2],
        results[3],
        results[4],
        results[5],
        results[6],
        results[7],
        results[8],
        results[9],
        results[10],
        results[11],
        results[12],
    )


def solution(mesh):
    in_specs = (
        P("batch", "doc", None, None),
        P("batch", "doc", None),
        P("batch", "doc", None, None),
        P(),
        P("batch", None, "doc"),
        P("batch", "doc", None, None),
        P(),
        P(),
        P(),
        P(),
        P(),
        P(),
        P(),
        P(),
        P(),
        P(),
        P(),
        P(),
        P(),
        P("batch", None),
    )
    out_specs = (
        P("batch", "doc", None, None),
        P("batch", None),
        P("batch", "doc", None, None),
        P("batch", None, "doc"),
        P("batch", None),
        P("batch"),
        P("batch"),
        P("batch", None),
        P("batch"),
        P("batch"),
        P("batch"),
        P("batch", None),
        P("batch"),
        P("batch", None),
        P("batch"),
        P("batch"),
        P("batch"),
    )
    paired = dict(mesh.shape) == {"batch": 8, "doc": 4}
    return jax.shard_map(paired_local if paired else local, mesh=mesh, in_specs=in_specs, out_specs=out_specs, check_vma=False)
```

```python
from functools import partial
import itertools
import math

import jax
import jax.numpy as jnp
from jax import lax
from jax.experimental import pallas as pl
from jax.experimental.pallas import tpu as pltpu
from jax.sharding import PartitionSpec as P

HEAD_DIM = 64
MESH = pl.DeviceIdType.MESH
VMEM_BYTES = 64000000


class Spot:
    def __init__(self):
        self.at = {"batch": lax.axis_index("batch"), "doc": lax.axis_index("doc")}

    def mine(self, key):
        axis, k = key
        return lax.rem(self.at[axis] // (1 << k), 2)

    def others(self):
        nd = lax.axis_size("doc")
        return [(self.at["batch"], lax.rem(self.at["doc"] + j, nd)) for j in range(1, nd)]

    def peer(self, key):
        axis, k = key
        moved = dict(self.at)
        moved[axis] = self.at[axis] + (1 - 2 * self.mine(key)) * (1 << k)
        return (moved["batch"], moved["doc"])


def mesh_keys(nb, nd):
    batch = [("batch", k) for k in range(nb.bit_length() - 1)]
    doc = [("doc", k) for k in range(nd.bit_length() - 1)]
    return batch, doc


class Piece:
    def __init__(self, mat, col, rows, cols, lead, halve, both, spread):
        self.mat, self.col, self.rows, self.cols = mat, col, rows, cols
        self.lead, self.halve, self.both, self.spread = lead, halve, both, spread
        self.tile = (rows, cols)
        self.steps = (
            [("halve", key) for key in halve]
            + [("both", key) for key in both]
            + [("spread", key) for key in spread]
            + [("twin", ("doc", 0))]
        )
        self.width = cols * 2 ** len(spread)

    def buffers(self):
        two = [(2,) * (len(self.lead) - i - 1) + self.tile for i in range(len(self.halve))]
        two += [self.tile] * len(self.both)
        wide = (2,) * len(self.spread) + self.tile
        return [(2,) * len(self.lead) + self.tile] + two + [wide, wide]

    def bytes(self, i):
        kind, key = self.steps[i]
        unit = self.rows * self.cols * 2
        if kind == "halve":
            return unit * 2 ** (len(self.lead) - i - 1)
        return unit * (2 if kind == "twin" and self.spread else 1)


def plan_pieces(nb, nd, mats):
    batch, doc = mesh_keys(nb, nd)
    across = doc[1:]
    pieces = []
    for m, (rows, cols) in enumerate(mats):
        first = across[:1] if len(across) == 1 else []
        col = 0
        if first and cols % 256 == 0 and m == 0 or first and cols > 1024:
            wide = cols // 2 // 256 * 256 if m else 256
            chunk = 256 if wide % 512 else 512
            for _ in range(wide // chunk):
                pieces.append(
                    Piece(m, col, rows, chunk // 2, first + batch[::-1], first + batch, [], first)
                )
                col += chunk
        while col < cols:
            chunk = min(cols - col, 512)
            pieces.append(Piece(m, col, rows, chunk, batch[::-1], batch, across, []))
            col += chunk
    return pieces


def exchange_order(pieces, ready, topology):
    free = {}
    clock = [(ready[i], i, 0) for i in range(len(pieces))]
    done = []
    while clock:
        clock.sort()
        at, i, step = clock.pop(0)
        key = pieces[i].steps[step][1]
        link, weight, rate = topology[key]
        start = max(at, free.get(link, 0.0))
        end = start + pieces[i].bytes(step) * weight / rate
        free[link] = end
        done.append((end + 1.5, i, step))
        if step + 1 < len(pieces[i].steps):
            clock.append((end + 2.0, i, step + 1))
    return [(i, step) for _, i, step in sorted(done)]


class Flow:
    def __init__(self, piece, bufs, send, recv, base, spot):
        self.p, self.bufs, self.send, self.recv, self.base, self.spot = piece, bufs, send, recv, base, spot
        self.live = {}
        self.copies = []

    @property
    def grad(self):
        return self.bufs[0]

    def index(self, fixed):
        return tuple(fixed.get(key, slice(None)) for key in self.p.lead)

    def start(self, step):
        kind, key = self.p.steps[step]
        mine = self.spot.mine(key)
        n = len(self.p.halve) + len(self.p.both)
        if kind == "halve":
            src = self.bufs[0].at[self.index({**self.live, key: 1 - mine})]
            dst = self.bufs[1 + step]
        elif kind == "both":
            src = self.bufs[0].at[self.index(self.live)]
            dst = self.bufs[1 + step]
        elif kind == "spread":
            src = self.bufs[n + 1].at[mine]
            dst = self.bufs[n + 1].at[mine]
        else:
            src = self.bufs[n + 1]
            dst = self.bufs[n + 2]
        copy = pltpu.make_async_remote_copy(
            src_ref=src,
            dst_ref=dst,
            send_sem=self.send.at[self.base + step],
            recv_sem=self.recv.at[self.base + step],
            device_id=self.spot.peer(key),
            device_id_type=MESH,
        )
        copy.start()
        self.copies.append(copy)

    def finish(self, step):
        kind, key = self.p.steps[step]
        copy = self.copies[step]
        if kind == "both":
            copy.wait()
        else:
            copy.wait_recv()
        n = len(self.p.halve) + len(self.p.both)
        if kind in ("halve", "both"):
            if kind == "halve":
                self.live[key] = self.spot.mine(key)
            got = self.bufs[1 + step]
            free = [k for k in self.p.lead if k not in self.live]
            last = step + 1 == n
            for pick in itertools.product(range(2), repeat=len(free)):
                at = self.index({**self.live, **dict(zip(free, pick))})
                total = self.bufs[0][at] + got[pick]
                if last:
                    self.bufs[n + 1][tuple(self.spot.mine(k) for k in self.p.spread)] = total
                else:
                    self.bufs[0][at] = total

    def drain(self):
        for step, copy in enumerate(self.copies):
            if self.p.steps[step][0] != "both":
                copy.wait_send()


def link_table(nb, nd):
    batch, doc = mesh_keys(nb, nd)
    table = {key: (key, 2.0, 91e3) for key in batch + doc}
    table[("doc", 0)] = ("twin", 1.0, 450e3)
    if (nb, nd) == (8, 4):
        table[("batch", 1)] = ("z", 2.0, 91e3)
        table[("batch", 2)] = ("z", 4.0, 91e3)
    return table


def reduce_kernel(pieces, halves, order, n_mats, *refs):
    mats, refs = refs[:n_mats], refs[n_mats:]
    vec, refs = refs[0], refs[1:]
    outs, refs = refs[:n_mats], refs[n_mats:]
    vec_out, refs = refs[0], refs[1:]
    spot = Spot()
    nb, nd = lax.axis_size("batch"), lax.axis_size("doc")
    batch, doc = mesh_keys(nb, nd)
    keys = batch + doc
    bufs = []
    for p in pieces:
        k = len(p.buffers())
        bufs.append(refs[:k])
        refs = refs[k:]
    vec_send, vec_recv = refs[:2]
    send, recv, twin_send, twin_recv, vs, vr = refs[2:]

    barrier = pltpu.get_barrier_semaphore()
    for key in keys:
        pl.semaphore_signal(barrier, inc=1, device_id=spot.peer(key), device_id_type=MESH)
    pl.semaphore_wait(barrier, len(keys))

    core = spot.mine(("doc", 0))
    twin = spot.peer(("doc", 0))
    flows = []
    base = 0
    twins = []
    for i, p in enumerate(pieces):
        flow = Flow(p, bufs[i], send, recv, base, spot)
        base += len(p.steps)
        flows.append(flow)
        half = halves[p.mat]
        copies = []
        for j in range(2 ** len(p.spread)):
            cols = pl.ds(pl.multiple_of((1 - core) * half + p.col + j * p.cols, 128), p.cols)
            dst = flow.grad.at[j] if p.spread else flow.grad
            lead = (slice(None),) * len(batch)
            copy = pltpu.make_async_remote_copy(
                src_ref=mats[p.mat].at[lead + (slice(None), cols)],
                dst_ref=dst,
                send_sem=twin_send.at[2 * i + j],
                recv_sem=twin_recv.at[2 * i + j],
                device_id=twin,
                device_id_type=MESH,
            )
            copy.start()
            copies.append(copy)
        twins.append(copies)

    vec_now = vec[...]
    vec_copies = []

    def vec_step(i):
        vec_send[i] = vec_now.astype(jnp.bfloat16)
        copy = pltpu.make_async_remote_copy(
            src_ref=vec_send.at[i],
            dst_ref=vec_recv.at[i],
            send_sem=vs.at[i],
            recv_sem=vr.at[i],
            device_id=spot.peer(keys[i]),
            device_id_type=MESH,
        )
        copy.start()
        vec_copies.append(copy)

    vec_step(0)
    for i, p in enumerate(pieces):
        half = halves[p.mat]
        for j, copy in enumerate(twins[i]):
            copy.wait()
            cols = pl.ds(pl.multiple_of(core * half + p.col + j * p.cols, 128), p.cols)
            for pick in itertools.product(range(2), repeat=len(batch)):
                at = ((j,) if p.spread else ()) + pick
                flows[i].grad[at] = flows[i].grad[at] + mats[p.mat][pick + (slice(None), cols)]
        flows[i].start(0)
        if i + 1 < len(keys):
            vec_copies[i].wait()
            vec_now = vec_now + vec_recv[i].astype(jnp.float32)
            vec_step(i + 1)
    for i in range(len(vec_copies), len(keys) + 1):
        vec_copies[i - 1].wait()
        vec_now = vec_now + vec_recv[i - 1].astype(jnp.float32)
        if i < len(keys):
            vec_step(i)
    vec_out[...] = vec_now

    for i, step in order:
        flows[i].finish(step)
        p = pieces[i]
        if step + 1 < len(p.steps):
            flows[i].start(step + 1)
        else:
            half = halves[p.mat]
            for side, buf in ((core, bufs[i][-2]), (1 - core, bufs[i][-1])):
                for j in range(2 ** len(p.spread)):
                    cols = pl.ds(pl.multiple_of(side * half + p.col + j * p.cols, 128), p.cols)
                    outs[p.mat][:, cols] = buf[j] if p.spread else buf[...]
    for flow in flows:
        flow.drain()


def reduce_params(mats, vectors, nb, nd):
    batch, doc = mesh_keys(nb, nd)
    shares = [(m.shape[0] // nb, m.shape[1]) for m in mats]
    halves = [c // 2 for _, c in shares]
    pieces = plan_pieces(nb, nd, [(r, c // 2) for r, c in shares])
    order = exchange_order(pieces, [3.0 * i for i in range(len(pieces))], link_table(nb, nd))
    keys = batch + doc
    scratch = []
    for p in pieces:
        scratch += [pltpu.VMEM(shape, jnp.bfloat16) for shape in p.buffers()]
    scratch += [pltpu.VMEM((len(keys),) + vectors.shape, jnp.bfloat16)] * 2
    steps = sum(len(p.steps) for p in pieces)
    dma = pltpu.SemaphoreType.DMA
    scratch += [dma((steps,)), dma((steps,)), dma((2 * len(pieces),)), dma((2 * len(pieces),))]
    scratch += [dma((len(keys),)), dma((len(keys),))]
    vm = pl.BlockSpec(memory_space=pltpu.VMEM)
    return pl.pallas_call(
        partial(reduce_kernel, pieces, halves, order, len(mats)),
        out_shape=[jax.ShapeDtypeStruct(s, jnp.bfloat16) for s in shares]
        + [jax.ShapeDtypeStruct(vectors.shape, jnp.float32)],
        in_specs=[vm] * (len(mats) + 1),
        out_specs=[vm] * (len(mats) + 1),
        scratch_shapes=scratch,
        compiler_params=pltpu.CompilerParams(
            collective_id=0, has_side_effects=True, vmem_limit_bytes=VMEM_BYTES
        ),
    )(*[m.reshape((2,) * len(batch) + (m.shape[0] // nb, m.shape[1])) for m in mats], vectors)


F32, BF16 = jnp.float32, jnp.bfloat16
NT = (((1,), (1,)), ((), ()))
TN = (((0,), (0,)), ((), ()))
EPS = 1e-06


def mm(a, b):
    return jnp.dot(a, b, preferred_element_type=F32)


def mm_nt(a, b):
    return lax.dot_general(a, b, NT, preferred_element_type=F32)


def mm_tn(a, b):
    return lax.dot_general(a, b, TN, preferred_element_type=F32)


def mm_exact(a, b, dims=(((1,), (0,)), ((), ()))):
    return lax.dot_general(a, b, dims, preferred_element_type=F32, precision=lax.Precision.HIGHEST)


def iota(shape, axis):
    return lax.broadcasted_iota(jnp.int32, shape, axis)


def normed(z):
    centred = z - jnp.mean(z, -1, keepdims=True)
    rstd = lax.rsqrt(jnp.mean(centred * centred, -1, keepdims=True) + EPS)
    return centred * rstd, rstd


def norm_back(grad, hat, rstd, gain):
    g = grad * gain
    inner = g - jnp.mean(g, -1, keepdims=True) - hat * jnp.mean(g * hat, -1, keepdims=True)
    return rstd * inner


def gelu(x):
    return 0.5 * x * (1.0 + lax.erf(x * math.sqrt(0.5)))


def gelu_slope(x):
    density = jnp.exp(-0.5 * x * x) * (1.0 / math.sqrt(2.0 * math.pi))
    return 0.5 * (1.0 + lax.erf(x * math.sqrt(0.5))) + x * density


def column_of(row_block):
    n, m = row_block.shape
    diag = iota((m, m), 0) == iota((m, m), 1)
    cols = [
        jnp.sum(jnp.where(diag, jnp.broadcast_to(row_block[i : i + 1, :], (m, m)), 0), 1, keepdims=True)
        for i in range(n)
    ]
    return jnp.concatenate(cols, 0)


class Net:
    def __init__(self, send, recv):
        self.send, self.recv, self.sends, self.recvs, self.open, self.due = send, recv, 0, 0, [], {}

    def branch(self):
        twin = Net(self.send, self.recv)
        twin.open = list(self.open)
        twin.due = {k: list(v) for k, v in self.due.items()}
        return twin

    def take(self):
        self.sends += 1
        self.recvs += 1
        return self.sends - 1, self.recvs - 1

    def copy(self, src, dst, peer, at):
        return pltpu.make_async_remote_copy(
            src_ref=src,
            dst_ref=dst,
            send_sem=self.send.at[at[0]],
            recv_sem=self.recv.at[at[1]],
            device_id=peer,
            device_id_type=MESH,
        )

    def put(self, src, dst, peer, at):
        self.copy(src, dst, peer, at).start()

    def group(self, due, copies, whole):
        at = self.take()
        for src, dst, peer in copies:
            self.put(src, dst, peer, at)
        all_of = self.copy(whole(len(copies)), whole(len(copies)), copies[0][2], at)
        self.expect(due, all_of.wait_recv)
        self.open.append(all_of.wait_send)

    def expect(self, due, wait):
        self.due.setdefault(due, []).append(wait)

    def collect(self, due):
        for wait in self.due.pop(due):
            wait()

    def drain(self):
        for wait in self.open:
            wait()
        self.open = []


class Trip:
    def __init__(self, tile, lead, halve, both, end):
        self.tile, self.lead, self.halve, self.both = tile, lead, halve, both
        self.steps = [("halve", k) for k in halve] + [("both", k) for k in both]
        self.sums = len(self.steps)
        ends = {"": [], "two": [("spread", ("doc", 1)), ("twin", ("doc", 0))], "three": [("three", None)]}
        self.steps += ends[end]
        self.end = end

    def buffers(self):
        shapes = [(2,) * len(self.lead) + self.tile]
        shapes += [(2,) * (len(self.lead) - i - 1) + self.tile for i in range(len(self.halve))]
        shapes += [self.tile] * len(self.both)
        return shapes + [((4,) if self.end else ()) + self.tile]

    def bytes(self, i):
        kind, key = self.steps[i]
        unit = 2 * math.prod(self.tile)
        if kind == "halve":
            return unit * 2 ** (len(self.lead) - i - 1)
        return unit * {"twin": 2, "three": 2}.get(kind, 1)


class TripRun:
    def __init__(self, trip, bufs, sems, net, spot):
        self.t, self.bufs, self.at_step, self.net, self.spot = trip, bufs, sems, net, spot
        self.live = {}

    @property
    def final(self):
        return self.bufs[-1]

    def at(self, fixed):
        return tuple(fixed.get(key, slice(None)) for key in self.t.lead)

    def place(self):
        return (2 * self.spot.mine(("doc", 0)) + self.spot.mine(("doc", 1)),) if self.t.end else ()

    def start(self, step):
        kind, key = self.t.steps[step]
        if kind == "three":
            mine = self.final.at[self.place()]
            sem = self.at_step[step]
            for peer in self.spot.others():
                self.net.put(mine, mine, peer, sem)
            view = self.final.at[pl.ds(0, 3)]
            copy = self.net.copy(view, view, self.spot.peer(("doc", 0)), sem)
            self.net.expect(sem, copy.wait_recv)
            self.net.open.append(copy.wait_send)
            return
        if kind == "halve":
            src = self.bufs[0].at[self.at({**self.live, key: 1 - self.spot.mine(key)})]
            dst = self.bufs[1 + step]
        elif kind == "both":
            src, dst = self.bufs[0].at[self.at(self.live)], self.bufs[1 + step]
        elif kind == "spread":
            src = dst = self.final.at[self.place()]
        else:
            src = dst = self.final.at[pl.ds(2 * self.spot.mine(key), 2)]
        at = self.at_step[step]
        copy = self.net.copy(src, dst, self.spot.peer(key), at)
        copy.start()
        self.net.expect(at, copy.wait_recv)
        if kind == "both":
            self.net.expect(at, copy.wait_send)
        else:
            self.net.open.append(copy.wait_send)

    def finish(self, step):
        kind, key = self.t.steps[step]
        self.net.collect(self.at_step[step])
        if step < self.t.sums:
            if kind == "halve":
                self.live[key] = self.spot.mine(key)
            got = self.bufs[1 + step]
            free = [k for k in self.t.lead if k not in self.live]
            for pick in itertools.product(range(2), repeat=len(free)):
                at = self.at({**self.live, **dict(zip(free, pick))})
                total = self.bufs[0][at] + got[pick]
                if step + 1 == self.t.sums:
                    self.final[self.place()] = total
                else:
                    self.bufs[0][at] = total


ALONG_Z = 2


def layer_trips(share):
    y, z0, z1, x = ("batch", 0), ("batch", 1), ("batch", 2), ("doc", 1)
    block = [Trip((share, 384), [z1, y], [y, z1], [], "two") for _ in range(ALONG_Z)]
    block += [Trip((share, 384), [z1, z0], [z0, z1], [], "two") for _ in range(4 - ALONG_Z)]
    block += [Trip((share, 384), [z1, y], [y, z1], [], "two")]
    orders = [[y, z0, z1], [y, z0, z1], [y, z0, z1]]
    wide = [Trip((share, 128), [z1, z0, y], order, [], "three") for order in orders]
    small = Trip((16, 768), [], [], [y, z0, z1, x, ("doc", 0)], "")
    return block + wide + [small]


LINKS = {
    ("batch", 0): [("y", 2.0)],
    ("batch", 1): [("z", 2.0)],
    ("batch", 2): [("far", 4.0), ("z", 2.0)],
    ("doc", 1): [("x", 2.0)],
    ("doc", 0): [("twin", 0.2)],
    None: [("x", 2.0)],
}
IN_FLIGHT = 3
LINK_RATE = 100e3


def trip_program(trips, stages):
    def wire(i, step):
        uses = LINKS[trips[i].steps[step][1]]
        return [(link, trips[i].bytes(step) * copies / LINK_RATE) for link, copies in uses]

    def to_go(i, step):
        return sum(max(t for _, t in wire(i, n)) + 2.0 for n in range(step, len(trips[i].steps)))

    events = [(at, -1, n, 0) for n, (at, _) in enumerate(stages)]
    free, flying, waiting, program = {}, {}, {}, []
    while events:
        events.sort()
        now, kind, i, step = events.pop(0)
        if kind < 0:
            program.append(("make", i, 0))
            ready = [(n, 0) for n in stages[i][1]]
        else:
            program.append(("finish", i, step))
            flying[wire(i, step)[0][0]] -= 1
            ready = [(i, step + 1)] if step + 1 < len(trips[i].steps) else []
        for n, s in ready:
            waiting.setdefault(wire(n, s)[0][0], []).append((-to_go(n, s), n, s))
        for link, queue in waiting.items():
            while queue and flying.get(link, 0) < IN_FLIGHT:
                queue.sort()
                _, n, s = queue.pop(0)
                program.append(("start", n, s))
                flying[link] = flying.get(link, 0) + 1
                end = now
                for used, t in wire(n, s):
                    free[used] = max(now, free.get(used, 0.0)) + t
                    end = max(end, free[used])
                events.append((end + 1.8, 0, n, s))
    return program


def layer_kernel(trips, *refs):
    (
        hidden, segs, places, targets, query, doc_rows,
        bias_q, bias_v, bias_o, gain1, shift1, bias_up, bias_down, gain2, shift2,
        qkv_hbm, out_hbm, up_hbm, down_hbm, vocab_hbm,
        block_out, loss_out, grad_in, grad_query, mats_out, wide_out, vec_out,
        wqkv, wout, wup, wdown, wvoc,
        qb, kb, vb, mixed, first_norm, first_low, acc,
        x4, x4t, kvb, kv4, sp, sp_send, qm, qm_send,
        picks, tsend, trecv, target_rows, usend, urecv, ssend, srecv, logits,
        qexp, probs, probs_low,
        hints, hints_in, joint, joint_in,
        left0, left0_y, left1, left1_y, a1, a1_y, at, at_y, second_b, inner_b, rest_b, g1, g1_y, g2,
        vecs, up_bias_s,
        block_v, grad_v, load_sem, store_sem, send, recv, *trip_bufs,
    ) = refs
    bias_q, bias_v, bias_o, gain1, shift1, bias_up, bias_down, gain2, shift2 = (
        b[...].reshape(1, -1) for b in (bias_q, bias_v, bias_o, gain1, shift1, bias_up, bias_down, gain2, shift2)
    )
    left0, left1, a1, at, g1 = (left0, left0_y), (left1, left1_y), (a1, a1_y), (at, at_y), (g1, g1_y)
    spot = Spot()
    batch, doc = spot.at["batch"], spot.at["doc"]
    nb, nd = lax.axis_size("batch"), lax.axis_size("doc")
    core, x = spot.mine(("doc", 0)), spot.mine(("doc", 1))
    z0 = spot.mine(("batch", 1))
    rows, width = hidden.shape
    pairs, slots = places.shape
    n_pick = pairs * slots
    heads = width // HEAD_DIM
    share = width // nb
    net = Net(send, recv)

    loads = [
        pltpu.make_async_copy(qkv_hbm.at[:, pl.ds(width, 2 * width)], wqkv.at[:, pl.ds(width, 2 * width)], load_sem.at[0]),
        pltpu.make_async_copy(vocab_hbm, wvoc, load_sem.at[1]),
        pltpu.make_async_copy(qkv_hbm.at[:, pl.ds(0, width)], wqkv.at[:, pl.ds(0, width)], load_sem.at[2]),
        pltpu.make_async_copy(out_hbm, wout, load_sem.at[3]),
        pltpu.make_async_copy(up_hbm, wup, load_sem.at[4]),
        pltpu.make_async_copy(down_hbm, wdown, load_sem.at[5]),
    ]
    for load in loads:
        load.start()

    batch_peers = [(lax.rem(batch + j, nb), doc) for j in range(1, nb)]
    doc_peers = [(batch, lax.rem(doc + j, nd)) for j in range(1, nd)]

    def side_peer(dx, dz, to_core, key):
        tx = lax.rem(x + dx, 2)
        mine = spot.mine(key)
        tz = lax.rem(mine + dz, 2)
        return (batch + (tz - mine) * (1 << key[1]), 2 * tx + to_core), tx, tz

    routes = [("batch", 1), ("batch", 0)]
    twin = spot.peer(("doc", 0))
    slots_of = [4 * spot.mine(key) + doc for key in routes]

    def fan(due, part_of, dst, lanes, to_core, dzs, route):
        slot = slots_of[route]
        sem = net.take()
        land = dst.at[slot, :, pl.ds(0, lanes)]
        always = 0
        for dz in dzs:
            for dx in range(2):
                peer, tx, tz = side_peer(dx, dz, to_core, routes[route])
                copy = net.copy(part_of(tx, tz), land, peer, sem)
                if dx or dz:
                    copy.start()
                    always += 1
                else:
                    pl.when(core != to_core)(copy.start)
        own = 0 in dzs

        def sized(n):
            view = dst.at[pl.ds(0, n), :, pl.ds(0, lanes)]
            return net.copy(view, view, twin, sem)

        def sent():
            if own:
                pl.when(core != to_core)(sized(always + 1).wait_send)
                pl.when(core == to_core)(sized(always).wait_send)
            else:
                sized(always).wait_send()

        net.open.append(sent)
        net.expect(due, lambda: pl.when(core == to_core)(sized(4 * len(dzs) - own).wait_recv))

    far = [
        side_peer(dx, 1, lax.rem(core + dc, 2), key)[0] for key in routes for dx, dc in ((1, 0), (1, 1), (0, 1))
    ]
    everyone = batch_peers + doc_peers + far
    barrier = pltpu.get_barrier_semaphore()
    for peer in everyone:
        pl.semaphore_signal(barrier, inc=1, device_id=peer, device_id_type=MESH)

    place_col = column_of(places[...])
    pick_bool = iota((n_pick, rows), 1) == place_col
    pick = pick_bool.astype(BF16)
    pick_f32 = pick_bool.astype(F32)
    tokens = hidden[...]
    loads[0].wait()
    kb[...] = mm(tokens, wqkv[:, width : 2 * width]).astype(BF16)
    vb[...] = (mm(tokens, wqkv[:, 2 * width :]) + bias_v).astype(BF16)
    tokens_p = mm(pick, tokens).astype(BF16)

    pl.semaphore_wait(barrier, len(everyone))
    own_part = query.shape[1]
    spread_lanes = (iota((own_part, own_part * nd), 0) + own_part * doc == iota((own_part, own_part * nd), 1)).astype(F32)
    hints[0:pairs, :] = mm_exact(query[...], spread_lanes)
    hints[8 : 8 + pairs, :] = doc_rows[...]
    hints_in[doc, 0:pairs, :] = hints[0:pairs, :]
    hints_in[doc, 8 : 8 + pairs, :] = hints[8 : 8 + pairs, :]
    net.group("hint", [(hints, hints_in.at[doc], peer) for peer in doc_peers], lambda n: hints_in.at[pl.ds(0, n)])
    beside = spot.peer(("doc", 1))
    net.group("tokens", [(hidden, x4.at[doc], beside)], lambda n: x4.at[pl.ds(0, n)])
    net.group("all tokens", [(hidden, x4.at[doc], twin)], lambda n: x4.at[pl.ds(0, n)])
    x4[doc] = hidden[...]

    loads[1].wait()
    entries = wvoc.shape[0]
    target_col = jnp.concatenate([column_of(targets[j]) for j in range(nb)], 0) - batch * entries
    all_rows = nb * n_pick
    is_target = iota((all_rows, entries), 1) == target_col
    tsend[...] = mm(is_target.astype(BF16), wvoc[...]).astype(BF16).reshape(nb, nd, n_pick // nd, width)
    trecv[batch] = tsend[batch, doc]
    net.group("part", [(tsend.at[p[0], doc], trecv.at[batch], p) for p in batch_peers], lambda n: trecv.at[pl.ds(0, n)])

    loads[2].wait()
    query_p = (mm(tokens_p, wqkv[:, 0:width]) + bias_q).astype(BF16)

    tall = heads * n_pick
    own_head = iota((tall, width), 0) // n_pick == iota((tall, width), 1) // HEAD_DIM

    def expand(v):
        return jnp.where(own_head, jnp.concatenate([v] * heads, 0), jnp.zeros((), v.dtype))

    def fold(v):
        return jnp.sum(jnp.where(own_head, v, 0.0).reshape(heads, n_pick, width), 0)

    seg_row = segs[...]
    seg_pick = jnp.sum(jnp.where(pick_bool, jnp.broadcast_to(seg_row, (n_pick, rows)), 0), 1, keepdims=True)
    same_pick = seg_pick == seg_row
    scale = 1.0 / math.sqrt(HEAD_DIM)
    qexp[...] = expand(query_p)
    scores = mm_nt(qexp[...], kb[...]) * scale
    same_tall = jnp.concatenate([same_pick.astype(F32)] * heads, 0) > 0.5
    scores = jnp.where(same_tall, scores, -1e30)
    weights = jnp.exp(scores - jnp.max(scores, -1, keepdims=True))
    weights = weights / jnp.sum(weights, -1, keepdims=True)
    probs[...] = weights
    probs_low[...] = weights.astype(BF16)
    mixed_p = fold(mm(probs_low[...], vb[...])).astype(BF16)
    loads[3].wait()
    attended = mm(mixed_p, wout[...]) + bias_o
    hat1, rstd1 = normed(tokens_p.astype(F32) + attended)
    first_p = hat1 * gain1 + shift1
    first_low_p = first_p.astype(BF16)
    loads[4].wait()
    inner_p = mm(first_low_p, wup[...]) + bias_up
    active_p = gelu(inner_p).astype(BF16)
    loads[5].wait()
    second_p = mm(active_p, wdown[...]) + bias_down
    hat2, rstd2 = normed(first_p + second_p)
    picks[batch] = (hat2 * gain2 + shift2).astype(BF16)
    net.group("pick", [(picks.at[batch], picks.at[batch], p) for p in batch_peers], lambda n: picks.at[pl.ds(0, n)])

    ff = wup.shape[1]
    counts = [ALONG_Z, 4 - ALONG_Z]
    firsts = [0, ALONG_Z]
    quads = [(z1, other) for z1 in range(2) for other in range(2)]
    lanes0 = [4 * share * (counts[0] + 1), 4 * share * counts[1]]
    lanes1 = [8 * share, 4 * share]
    for route in range(2):
        wide_lanes = share * counts[route]
        for k in range(2):
            for n, (z1, other) in enumerate(quads):
                b = 4 * z1 + (2 * k + other if route == 0 else 2 * other + k)
                own = slice(b * share, (b + 1) * share)
                start = 4 * share * b + share * firsts[route]
                left0[route][k, :, n * wide_lanes : (n + 1) * wide_lanes] = active_p[:, start : start + wide_lanes]
                left1[route][k, :, n * share : (n + 1) * share] = first_low_p[:, own]
                if route == 0:
                    at0 = 4 * wide_lanes + n * share
                    left0[route][k, :, at0 : at0 + share] = mixed_p[:, own]
                    left1[route][k, :, (4 + n) * share : (5 + n) * share] = tokens_p[:, own]

    def keep_left(route, left, lanes):
        def keep():
            a1[route][slots_of[route], :, 0:lanes] = left[route][spot.mine(routes[route])]

        return keep

    for route in range(2):
        pl.when(core == 0)(keep_left(route, left0, lanes0[route]))
        pl.when(core == 1)(keep_left(route, left1, lanes1[route]))

    def send_left(dzs):
        for route in range(2):
            fan("left", lambda tx, tz: left0[route].at[tz], a1[route], lanes0[route], 0, dzs, route)
            fan("left", lambda tx, tz: left1[route].at[tz], a1[route], lanes1[route], 1, dzs, route)

    half_w, half_f = width // 2, ff // 2
    tall_half = tall // 2
    send_left([0])

    def half_heads(due, src, dst, to_core):
        sem = net.take()
        for dx in range(2):
            peer, tx, _ = side_peer(dx, 0, to_core, routes[0])
            copy = net.copy(src.at[tx], dst.at[doc], peer, sem)
            if dx:
                copy.start()
            else:
                pl.when(core != to_core)(copy.start)

        def keep():
            dst[doc] = src[x]

        def sized(n):
            view = dst.at[pl.ds(0, n)]
            return net.copy(view, view, twin, sem)

        def sent():
            pl.when(core != to_core)(sized(2).wait_send)
            pl.when(core == to_core)(sized(1).wait_send)

        pl.when(core == to_core)(keep)
        net.open.append(sent)
        net.expect(due, lambda: pl.when(core == to_core)(sized(3).wait_recv))

    def halves(dst, v):
        for s in range(2):
            dst[s] = v[:, s * half_w : (s + 1) * half_w]

    sp_send[1] = probs_low[...].reshape(2, tall_half, rows)
    half_heads("heads", sp_send.at[1], sp, 1)
    halves(qm_send.at[0], query_p)
    half_heads("heads", qm_send.at[0], qm, 0)

    seg_col = jnp.sum(
        jnp.where(iota((rows, rows), 0) == iota((rows, rows), 1), jnp.broadcast_to(seg_row, (rows, rows)), 0),
        1,
        keepdims=True,
    )
    qb[...] = (mm(tokens, wqkv[:, 0:width]) + bias_q).astype(BF16)

    def attend(i):
        lanes = pl.ds(pl.multiple_of(i * 128, 128), 128)
        q_s, k_s, v_s = qb[:, lanes], kb[:, lanes], vb[:, lanes]
        low = iota((rows, 128), 1) < HEAD_DIM
        same = seg_col == seg_row
        parts = []
        for side in (low, ~low):
            s = mm_nt(jnp.where(side, q_s, jnp.zeros((), BF16)), k_s) * scale
            s = jnp.where(same, s, -1e30)
            e = jnp.exp(s - jnp.max(s, -1, keepdims=True))
            p = (e / jnp.sum(e, -1, keepdims=True)).astype(BF16)
            parts.append(mm(p, v_s))
        mixed[:, lanes] = jnp.where(low, parts[0], parts[1]).astype(BF16)

    half_way = width // 256
    pl.loop(0, half_way)(attend)
    send_left([1])
    net.collect("tokens")
    net.group("all tokens", [(x4.at[beside[1]], x4.at[beside[1]], twin)], lambda n: x4.at[pl.ds(0, n)])
    net.collect("part")
    part = trecv[0].astype(F32)
    for j in range(1, nb):
        part += trecv[j].astype(F32)
    target_rows[doc] = part.astype(BF16)
    net.group("target", [(target_rows.at[doc], target_rows.at[doc], p) for p in doc_peers], lambda n: target_rows.at[pl.ds(0, n)])
    pl.loop(half_way, width // 128)(attend)

    net.collect("pick")
    logits[...] = mm_nt(picks[...].reshape(all_rows, width), wvoc[...])
    lg = logits[...]
    top = jnp.max(lg, 1, keepdims=True)
    chosen = jnp.sum(jnp.where(is_target, lg, 0.0), 1, keepdims=True)
    others = jnp.where(is_target, 0.0, jnp.exp(lg - top))
    total = jnp.sum(others, 1, keepdims=True)
    lane = iota((all_rows, 128), 1)
    stats = jnp.where(lane == 0, top, jnp.where(lane == 1, total, chosen)).T
    blank = jnp.zeros((8, 128 - n_pick), F32)
    for j in range(nb):
        ssend[j] = jnp.concatenate([stats[0:8, n_pick * j : n_pick * (j + 1)], blank], 1)
    srecv[batch] = ssend[batch]
    net.group("stats", [(ssend.at[p[0]], srecv.at[batch], p) for p in batch_peers], lambda n: srecv.at[pl.ds(0, n)])
    usend[...] = mm(others.astype(BF16), wvoc[...]).astype(BF16).reshape(nb, n_pick, width)
    urecv[batch] = usend[batch]
    net.group("back", [(usend.at[p[0]], urecv.at[batch], p) for p in batch_peers], lambda n: urecv.at[pl.ds(0, n)])

    tokens = hidden[...]
    hat, _ = normed(tokens.astype(F32) + mm(mixed[...], wout[...]) + bias_o)
    first_norm[...] = hat * gain1 + shift1
    first_low[...] = first_norm[...].astype(BF16)
    acc[...] = first_norm[...] + bias_down
    chunk = 512
    up_bias_s[...] = bias_up

    def feed(i):
        cols = pl.ds(pl.multiple_of(i * chunk, chunk), chunk)
        hid = mm(first_low[...], wup[:, cols]) + up_bias_s[:, cols]
        acc[...] += mm(gelu(hid).astype(BF16), wdown[cols, :])

    pl.loop(0, ff // chunk // 2)(feed)

    net.collect("stats")
    tops = [srecv[j][0:1, :] for j in range(nb)]
    peak = tops[0]
    for t in tops[1:]:
        peak = jnp.maximum(peak, t)
    factors = [jnp.exp(t - peak) for t in tops]
    rest = jnp.zeros_like(peak)
    chosen = jnp.zeros_like(peak)
    for j in range(nb):
        rest += factors[j] * srecv[j][1:2, :]
        chosen += srecv[j][2:3, :]
    whole = rest + jnp.exp(chosen - peak)
    logp = chosen - peak - jnp.log(whole)
    of_pair = iota((pairs, 128), 1) // slots == iota((pairs, 128), 0)
    reader = jnp.sum(jnp.where(of_pair, jnp.broadcast_to(logp, (pairs, 128)), 0.0), 1, keepdims=True) / slots
    joint[...] = jnp.zeros_like(joint)
    joint[0:pairs, :] = jnp.broadcast_to(reader, (pairs, 128))
    joint_in[doc] = joint[...]
    net.group("joint", [(joint, joint_in.at[doc], p) for p in doc_peers], lambda n: joint_in.at[pl.ds(0, n)])
    shares = jnp.concatenate([f / whole for f in factors] + [rest / whole] + [jnp.zeros_like(peak)] * (15 - nb), 0).T

    pl.loop(ff // chunk // 2, ff // chunk)(feed)
    hat, _ = normed(acc[...])
    block_v[...] = (hat * gain2 + shift2).astype(BF16)
    block_store = pltpu.make_async_copy(block_v, block_out, store_sem.at[8])
    block_store.start()
    net.collect("all tokens")
    x4t[...] = x4[...].reshape(nd * rows, width).T

    net.collect("hint")
    full_query = hints_in[0, 0:pairs, :]
    for j in range(1, nd):
        full_query += hints_in[j, 0:pairs, :]
    docs = [hints_in[j, 8 : 8 + pairs, :] for j in range(nd)]
    score = [jnp.broadcast_to(jnp.sum(full_query * d, 1, keepdims=True), (pairs, 128)) for d in docs]
    net.collect("joint")
    both = [s + joint_in[j, 0:pairs, :] for j, s in enumerate(score)]

    def soft(vals):
        high = vals[0]
        for v in vals[1:]:
            high = jnp.maximum(high, v)
        es = [jnp.exp(v - high) for v in vals]
        tot = es[0]
        for e in es[1:]:
            tot = tot + e
        return [e / tot for e in es], high + jnp.log(tot)

    w_score, total_score = soft(score)
    w_joint, total_joint = soft(both)
    eye = iota((pairs, 128), 0) == iota((pairs, 128), 1)
    loss_out[...] = jnp.sum(jnp.where(eye, total_score - total_joint, 0.0), 0, keepdims=True)
    query_grad = (w_score[0] - w_joint[0]) * docs[0]
    for j in range(1, nd):
        query_grad += (w_score[j] - w_joint[j]) * docs[j]
    grad_query[...] = mm_exact(query_grad, spread_lanes, NT)
    mine = w_joint[0]
    for j in range(1, nd):
        mine = jnp.where(doc == j, w_joint[j], mine)
    row_weight = jnp.broadcast_to(mine.reshape(pairs, 1, 128), (pairs, slots, 128)).reshape(n_pick, 128)[:, 0:1]

    net.collect("left")

    def turn(route, lanes):
        def go():
            at[route][0:lanes, :] = a1[route][:, :, 0:lanes].reshape(8 * n_pick, lanes).T

        return go

    for route in range(2):
        pl.when(core == 0)(turn(route, lanes0[route]))
        pl.when(core == 1)(turn(route, lanes1[route]))

    net.collect("back")
    row_grad = jnp.zeros((n_pick, width), F32)
    for j in range(nb):
        row_grad += shares[0:n_pick, j : j + 1] * urecv[j].astype(F32)
    net.collect("target")
    at_target = target_rows[...].astype(F32).reshape(n_pick, width)
    row_grad -= shares[0:n_pick, nb : nb + 1] * at_target
    final_grad = row_grad * (row_weight / slots)

    def send_right(due, src, every, first, cols, dst, to_core, route):
        def part(tx):
            return pl.ds(pl.multiple_of(tx * every + first, 128), cols)

        fan(due, lambda tx, tz: src.at[:, part(tx)], dst, cols, to_core, [0, 1], route)

        def keep():
            dst[slots_of[route], :, 0:cols] = src[:, part(x)]

        pl.when(core == to_core)(keep)

    vecs[...] = jnp.zeros_like(vecs)
    sum_grad = norm_back(final_grad, hat2, rstd2, gain2)
    vecs[6:7, :] = jnp.sum(final_grad * hat2, 0, keepdims=True)
    vecs[7:8, :] = jnp.sum(final_grad, 0, keepdims=True)
    vecs[5:6, :] = jnp.sum(sum_grad, 0, keepdims=True)
    second_low = sum_grad.astype(BF16)
    second_b[...] = second_low
    for route in range(2):
        send_right(("g1", route), second_b, half_w, 0, half_w, g1[route], 0, route)
    inner_grad = mm_nt(second_low, wdown[...]) * gelu_slope(inner_p)
    inner_low = inner_grad.astype(BF16)
    inner_b[...] = inner_low
    for route in range(2):
        first, cols = firsts[route] * half_w, counts[route] * half_w
        send_right(("g1", route), inner_b, half_f, first, cols, g1[route], 1, route)
    up_bias_grad = jnp.sum(inner_grad, 0, keepdims=True)
    for i in range(ff // width):
        vecs[8 + i : 9 + i, :] = up_bias_grad[:, i * width : (i + 1) * width]
    first_grad = sum_grad + mm_nt(inner_low, wup[...])
    resid_grad = norm_back(first_grad, hat1, rstd1, gain1)
    resid_low = resid_grad.astype(BF16)
    rest_b[0] = resid_low
    send_right("g2", rest_b.at[0], half_w, 0, half_w, g2, 0, 0)
    vecs[3:4, :] = jnp.sum(first_grad * hat1, 0, keepdims=True)
    vecs[4:5, :] = jnp.sum(first_grad, 0, keepdims=True)
    vecs[2:3, :] = jnp.sum(resid_grad, 0, keepdims=True)
    mixed_grad_p = mm_nt(resid_low, wout[...]).astype(BF16)
    halves(qm_send.at[1], mixed_grad_p)
    half_heads("heads", qm_send.at[1], qm, 1)
    mixed_grad = expand(mixed_grad_p)
    prob_grad = mm_nt(mixed_grad, vb[...])
    p = probs[...]
    score_low = (p * (prob_grad - jnp.sum(prob_grad * p, -1, keepdims=True)) * scale).astype(BF16)
    sp_send[0] = score_low.reshape(2, tall_half, rows)
    half_heads("heads", sp_send.at[0], sp, 0)
    query_grad_p = fold(mm(score_low, kb[...]))
    rest_b[1] = query_grad_p.astype(BF16)
    send_right("g2", rest_b.at[1], half_w, 0, half_w, g2, 1, 0)
    vecs[0:1, :] = jnp.sum(query_grad_p, 0, keepdims=True)
    value_grad = mm_tn(probs_low[...], mixed_grad)
    kvb[1] = value_grad.astype(BF16)
    vecs[1:2, :] = jnp.sum(value_grad, 0, keepdims=True)

    sems = [[net.take() for _ in t.steps] for t in trips]
    groups, left_over = [], list(trip_bufs)
    for t in trips:
        k = len(t.buffers())
        groups.append(left_over[:k])
        left_over = left_over[k:]

    def tail(side, net):
        runs = [TripRun(t, groups[n], sems[n], net, spot) for n, t in enumerate(trips)]
        stores = []

        def store(src, dst, n):
            copy = pltpu.make_async_copy(src, dst, store_sem.at[n])
            copy.start()
            stores.append(copy)

        def make_wide():
            net.collect("heads")
            half_tall = iota((tall_half, half_w), 0) // n_pick == iota((tall_half, half_w), 1) // HEAD_DIM
            for d in range(nd):
                tiled = jnp.concatenate([qm[d]] * (heads // 2), 0)
                tiled = jnp.where(half_tall, tiled, jnp.zeros((), BF16))
                kv4[d] = mm_tn(sp[d], tiled).astype(BF16)
            right = kv4[...].reshape(nd * rows, half_w)
            for b in range(nb):
                out = mm(x4t[b * share : (b + 1) * share, :], right).astype(BF16)
                for n in range(3):
                    runs[5 + n].bufs[0][b // 4, b // 2 % 2, b % 2] = out[:, 128 * n : 128 * (n + 1)]

        def block(i, route, offsets, g, col):
            left = jnp.concatenate([at[route][pl.ds(pl.multiple_of(o, 32), share), :] for o in offsets], 0)
            right = g[:, :, pl.ds(col, half_w)].reshape(8 * n_pick, half_w)
            out = mm(left, right).astype(BF16)
            for n, (z1, other) in enumerate(quads):
                runs[i].bufs[0][z1, other] = out[n * share : (n + 1) * share]

        def make_blocks(route):
            net.collect(("g1", route))
            for i in range(counts[route]):
                offsets = [((1 - core) * (n * counts[route] + i) + core * n) * share for n in range(4)]
                block(firsts[route] + i, route, offsets, g1[route], pl.multiple_of(core * i * half_w, 128))

        def make_last():
            net.collect("g2")
            first_row = (1 - core) * 4 * share * counts[0] + core * 4 * share
            block(4, 0, [first_row + n * share for n in range(4)], g2, 0)

        def make_inward():
            kvb[0] = mm_tn(score_low, qexp[...]).astype(BF16)
            inward = mm_nt(kvb[0], wqkv[:, width : 2 * width]) + mm_nt(kvb[1], wqkv[:, 2 * width :])
            at_rows = resid_grad + mm_nt(rest_b[1], wqkv[:, 0:width])
            grad_v[...] = (inward + mm_exact(pick_f32, at_rows, TN)).astype(BF16)
            store(grad_v, grad_in, 9)

        def make_sums():
            runs[8].bufs[0][...] = vecs[...].astype(BF16)

        along_y = list(range(ALONG_Z, 4))
        along_z = list(range(ALONG_Z))
        stages = (
            [
                (0.0, [8], make_sums),
                (0.6, along_y, lambda: make_blocks(1)),
                (1.2, along_z, lambda: make_blocks(0)),
                (1.8, [4], make_last),
                (8.0, [5, 6, 7], make_wide),
                (12.0, [], make_inward),
            ]
            if side == 0
            else [
                (0.0, [8], make_sums),
                (2.5, [5, 6, 7], make_wide),
                (5.0, along_y, lambda: make_blocks(1)),
                (5.6, along_z, lambda: make_blocks(0)),
                (6.2, [4], make_last),
                (10.0, [], make_inward),
            ]
        )
        last = []
        for what, i, step in trip_program(trips, [(t, made) for t, made, _ in stages]):
            if what == "make":
                stages[i][2]()
            elif what == "start":
                runs[i].start(step)
            elif trips[i].steps[step][1] in (("doc", 0), None):
                last.append((i, step))
            else:
                runs[i].finish(step)
        for i, step in last:
            runs[i].finish(step)
            if i < 5:
                store(runs[i].final, mats_out.at[i], i)
            elif i < 8:
                store(runs[i].final, wide_out.at[i - 5], i)
            else:
                vec_out[...] = runs[i].final[...]
        for copy in stores:
            copy.wait()
        net.drain()

    for side in range(2):
        pl.when(core == side)(partial(tail, side, net.branch()))
    block_store.wait()


def finish_kernel(block, grad, loss, gq, mats, wide, vec, *outs):
    (o_block, o_loss, o_grad, o_gq, o_qkv, o_qb, o_vb, o_out, o_ob, o_g1, o_s1, o_up, o_ub, o_down, o_db, o_g2, o_s2) = outs
    batch = lax.axis_index("batch")
    nb = lax.axis_size("batch")
    width = vec.shape[1]
    share, half = width // nb, width // 2
    o_block[...] = block[...]
    o_grad[...] = grad[...]
    o_loss[...] = loss[:, 0 : o_loss.shape[1]]
    o_gq[...] = gq[...]
    for s in range(2):
        cols = slice(s * half, (s + 1) * half)
        o_out[:, cols] = mats[4, s].astype(F32)
        o_qkv[:, cols] = mats[4, 2 + s].astype(F32)
        for i in range(4):
            o_down[i * share : (i + 1) * share, cols] = mats[i, s].astype(F32)
            o_up[:, (4 * s + i) * half : (4 * s + i + 1) * half] = mats[i, 2 + s].astype(F32)
        for c in range(2):
            for j in range(3):
                start = (1 + c) * width + s * half + 128 * j
                o_qkv[:, start : start + 128] = wide[j, 2 * c + s].astype(F32)
    v = vec[...].astype(F32)
    take = (iota((width, share), 0) == iota((width, share), 1) + batch * share).astype(F32)
    got = mm_exact(v, take)
    for i, o in enumerate((o_qb, o_vb, o_ob, o_g1, o_s1, o_db, o_g2, o_s2)):
        o[...] = got[i : i + 1, :]
    side = jnp.where(lax.rem(batch, 2) == 0, v[8:12, 0:half], v[8:12, half:])
    o_ub[...] = jnp.sum(jnp.where(iota((4, half), 0) == batch // 2, side, 0.0), 0)


def paired_local(*args):
    (
        hidden_in, segments, mask_pos, target_ids, query_emb, doc_emb,
        qkv_weight, query_bias, value_bias, out_weight, out_bias, gain_one, shift_one,
        up_weight, up_bias, down_weight, down_bias, gain_two, shift_two, vocab,
    ) = args
    rows, width = hidden_in.shape[2:]
    pairs, slots = mask_pos.shape[2:]
    n_pick = pairs * slots
    ff = up_weight.shape[1]
    entries = vocab.shape[0]
    nb, nd = lax.axis_size("batch"), lax.axis_size("doc")
    share = width // nb
    heads = width // HEAD_DIM
    trips = layer_trips(share)
    lanes_z, lanes_y = 4 * share * (ALONG_Z + 1), 4 * share * (4 - ALONG_Z)
    n_sems = sum(len(t.steps) for t in trips) + 28
    vm, hbm = pl.BlockSpec(memory_space=pltpu.VMEM), pl.BlockSpec(memory_space=pl.ANY)

    def v(shape, dtype=BF16):
        return pltpu.VMEM(shape, dtype)

    dma = pltpu.SemaphoreType.DMA
    scratch = [
        v(qkv_weight.shape), v(out_weight.shape), v(up_weight.shape), v(down_weight.shape), v(vocab.shape),
        v((rows, width)), v((rows, width)), v((rows, width)), v((rows, width)),
        v((rows, width), F32), v((rows, width)), v((rows, width), F32),
        v((nd, rows, width)), v((width, nd * rows)), v((2, rows, width)), v((nd, rows, width // 2)),
        v((nd, heads * n_pick // 2, rows)), v((2, 2, heads * n_pick // 2, rows)),
        v((nd, n_pick, width // 2)), v((2, 2, n_pick, width // 2)),
        v((nb, n_pick, width)), v((nb, nd, n_pick // nd, width)), v((nb, n_pick // nd, width)),
        v((nd, n_pick // nd, width)), v((nb, n_pick, width)),
        v((nb, n_pick, width)), v((nb, 8, 128), F32), v((nb, 8, 128), F32), v((nb * n_pick, entries), F32),
        v((heads * n_pick, width)), v((heads * n_pick, rows), F32), v((heads * n_pick, rows)),
        v((16, 128), F32), v((nd, 16, 128), F32), v((8, 128), F32), v((nd, 8, 128), F32),
        v((2, n_pick, lanes_z)), v((2, n_pick, lanes_y)), v((2, n_pick, width)), v((2, n_pick, width // 2)),
        v((8, n_pick, lanes_z)), v((8, n_pick, max(lanes_y, width // 2))), v((lanes_z, 8 * n_pick)),
        v((max(lanes_y, width // 2), 8 * n_pick)),
        v((n_pick, width)), v((n_pick, ff)), v((2, n_pick, width)),
        v((8, n_pick, ALONG_Z * width // 2)), v((8, n_pick, (4 - ALONG_Z) * width // 2)), v((8, n_pick, width // 2)),
        v((16, width), F32), v((1, ff), F32),
        v((rows, width)), v((rows, width)), dma((6,)), dma((10,)), dma((n_sems,)), dma((n_sems,)),
    ]
    for t in trips:
        scratch += [v(shape) for shape in t.buffers()]
    sds = jax.ShapeDtypeStruct
    first = pl.pallas_call(
        partial(layer_kernel, trips),
        out_shape=[
            sds((rows, width), BF16),
            sds((1, 128), F32),
            sds((rows, width), BF16),
            sds((pairs, query_emb.shape[2]), F32),
            sds((5, 4, share, 384), BF16),
            sds((3, 4, share, 128), BF16),
            sds((16, width), BF16),
        ],
        in_specs=[vm] * 15 + [hbm] * 5,
        out_specs=[hbm, vm, hbm, vm, hbm, hbm, vm],
        scratch_shapes=scratch,
        compiler_params=pltpu.CompilerParams(
            collective_id=0, has_side_effects=True, vmem_limit_bytes=VMEM_BYTES
        ),
        name="layer",
    )
    biases = (query_bias, value_bias, out_bias, gain_one, shift_one, up_bias, down_bias, gain_two, shift_two)
    block, loss, grad, gq, mats, wide, vec = first(
        hidden_in.reshape(rows, width),
        segments.reshape(1, rows),
        mask_pos.reshape(pairs, slots),
        target_ids,
        query_emb.reshape(pairs, -1),
        doc_emb.reshape(pairs, -1),
        *biases,
        qkv_weight,
        out_weight,
        up_weight,
        down_weight,
        vocab,
    )
    small = sds((1, share), F32)
    outs = pl.pallas_call(
        finish_kernel,
        out_shape=[
            sds((rows, width), BF16), sds((1, pairs), F32), sds((rows, width), BF16), sds(gq.shape, F32),
            sds((share, 3 * width), F32), small, small, sds((share, width), F32), small, small, small,
            sds((share, ff), F32), sds((ff // nb,), F32), sds((ff // nb, width), F32), small, small, small,
        ],
        in_specs=[vm] * 7,
        out_specs=[vm] * 17,
        compiler_params=pltpu.CompilerParams(vmem_limit_bytes=VMEM_BYTES),
        name="finish",
    )(block, grad, loss, gq, mats, wide, vec)
    shapes = [hidden_in.shape, (1, pairs), hidden_in.shape, query_emb.shape]
    fixed = [o.reshape(s) for o, s in zip(outs[:4], shapes)]
    return tuple(fixed + [o.reshape(-1) if o.shape == (1, share) else o for o in outs[4:]])


def combined_all(x, axis, combine):
    everything = jax.tree.map(lambda part: lax.all_gather(part, axis), x)
    leading = jax.tree.map(lambda part: part[0], everything)

    def hop(k, so_far):
        return combine(so_far, jax.tree.map(lambda part: part[k], everything))

    return lax.fori_loop(1, lax.axis_size(axis), hop, leading)


def norm_rows(values, gain, shift):
    centre = jnp.mean(values, -1, keepdims=True)
    centred = values - centre
    spread = jnp.mean(centred * centred, -1, keepdims=True)
    return centred * lax.rsqrt(spread + 1e-06) * gain + shift


def lse_pair(earlier, later):
    maxima = jnp.maximum(earlier[0], later[0])
    totals = earlier[1] * jnp.exp(earlier[0] - maxima) + later[1] * jnp.exp(later[0] - maxima)
    return (maxima, totals)


def vocab_pair(earlier, later):
    return lse_pair(earlier[:2], later[:2]) + (earlier[2] + later[2],)


def place_rows(places, grads, seq_len):
    return jnp.zeros((seq_len, grads.shape[-1]), jnp.float32).at[places].add(grads)


def local(
    hidden_in,
    segments,
    mask_pos,
    target_ids,
    query_emb,
    doc_emb,
    qkv_weight,
    query_bias,
    value_bias,
    out_weight,
    out_bias,
    gain_one,
    shift_one,
    up_weight,
    up_bias,
    down_weight,
    down_bias,
    gain_two,
    shift_two,
    vocab,
):
    f32 = jnp.float32
    bf16 = jnp.bfloat16
    seq_count, _, seq_len, model_width = hidden_in.shape
    pair_count = mask_pos.shape[2]
    mask_count = mask_pos.shape[3]
    head_count = model_width // HEAD_DIM
    score_scale = 1.0 / math.sqrt(HEAD_DIM)
    split_shape = (seq_count, seq_len, head_count, HEAD_DIM)
    tokens = hidden_in.reshape(seq_count, seq_len, model_width)
    segs = segments.reshape(seq_count, seq_len)
    packed = jnp.einsum("nld,de->nle", tokens, qkv_weight, preferred_element_type=f32)
    queries = (packed[..., :model_width] + query_bias).astype(bf16).reshape(split_shape)
    key_rows = packed[..., model_width : 2 * model_width].astype(bf16).reshape(split_shape)
    value_rows = (packed[..., 2 * model_width :] + value_bias).astype(bf16).reshape(split_shape)
    same_seg = (segs[:, :, None] == segs[:, None, :])[:, None]
    raw_scores = jnp.einsum("nlhe,nmhe->nhlm", queries, key_rows, preferred_element_type=f32)

    def attend(scores_in):
        return jax.nn.softmax(jnp.where(same_seg, scores_in * score_scale, -1e30), axis=-1)

    probs, soft_back = jax.vjp(attend, raw_scores)
    probs_low = probs.astype(bf16)
    mixed_heads = jnp.einsum("nhlm,nmhe->nlhe", probs_low, value_rows, preferred_element_type=f32)
    mixed_low = mixed_heads.reshape(seq_count, seq_len, model_width).astype(bf16)
    attended = (
        jnp.einsum("nld,de->nle", mixed_low, out_weight, preferred_element_type=f32) + out_bias
    )
    first_norm, norm_back_one = jax.vjp(
        norm_rows, tokens.astype(f32) + attended, gain_one, shift_one
    )
    first_low = first_norm.astype(bf16)
    inner_act = (
        jnp.einsum("nld,df->nlf", first_low, up_weight, preferred_element_type=f32) + up_bias
    )
    active, gelu_back = jax.vjp(partial(jax.nn.gelu, approximate=False), inner_act)
    active_low = active.astype(bf16)
    second = (
        jnp.einsum("nlf,fd->nld", active_low, down_weight, preferred_element_type=f32) + down_bias
    )
    final_rows, norm_back_two = jax.vjp(norm_rows, first_norm + second, gain_two, shift_two)
    per_seq = pair_count * mask_count
    rows_dev = seq_count * per_seq
    flat_places = mask_pos.reshape(seq_count, per_seq)
    picked = jnp.take_along_axis(final_rows, flat_places[:, :, None], axis=1)
    picked_low = picked.reshape(rows_dev, model_width).astype(bf16)
    logits = lax.dot_general(
        lax.all_gather(picked_low, "batch", axis=0, tiled=True),
        vocab,
        (((1,), (1,)), ((), ())),
        preferred_element_type=f32,
    )
    shard_size = vocab.shape[0]
    vocab_ids = lax.axis_index("batch") * shard_size + lax.iota(jnp.int32, shard_size)
    is_target = target_ids.reshape(-1)[:, None] == vocab_ids[None, :]
    maxima = jnp.max(logits, 1)
    totals = jnp.sum(jnp.exp(logits - maxima[:, None]), 1)
    chosen = jnp.sum(jnp.where(is_target, logits, 0.0), 1)
    maxima, totals, chosen = combined_all((maxima, totals, chosen), "batch", vocab_pair)
    log_total = maxima + jnp.log(totals)
    first_own = lax.axis_index("batch") * rows_dev
    own_logp = lax.dynamic_slice_in_dim(chosen - log_total, first_own, rows_dev)
    reader = jnp.mean(own_logp.reshape(seq_count, pair_count, mask_count), -1)
    gathered_query = lax.all_gather(query_emb, "doc", axis=2, tiled=True)
    doc_rows = doc_emb.reshape(seq_count, pair_count, doc_emb.shape[-1])
    score = jnp.sum(gathered_query * doc_rows, -1)
    joint = score + reader
    unit_terms = jnp.ones_like(score)
    score_top, score_sum = combined_all((score, unit_terms), "doc", lse_pair)
    score_total = score_top + jnp.log(score_sum)
    shifted = joint - score_total
    joint_top, joint_sum = combined_all((shifted, unit_terms), "doc", lse_pair)
    joint_total = joint_top + jnp.log(joint_sum)
    loss = -joint_total
    weight_joint = jnp.exp(shifted - joint_total)
    weight_score = jnp.exp(score - score_total)
    score_grad = weight_score - weight_joint
    grad_query = lax.psum_scatter(
        score_grad[..., None] * doc_rows, "doc", scatter_dimension=2, tiled=True
    )
    row_scale = jnp.broadcast_to(
        (weight_joint / mask_count)[..., None], (seq_count, pair_count, mask_count)
    ).reshape(rows_dev)
    all_scale = lax.all_gather(row_scale, "batch", axis=0, tiled=True)
    vocab_probs = jnp.exp(logits - log_total[:, None])
    logit_grad = (all_scale[:, None] * (vocab_probs - is_target.astype(f32))).astype(bf16)
    picked_grad = lax.psum_scatter(
        jnp.dot(logit_grad, vocab, preferred_element_type=f32).astype(jnp.bfloat16),
        "batch",
        scatter_dimension=0,
        tiled=True,
    ).astype(jnp.float32)
    final_grad = jax.vmap(partial(place_rows, seq_len=seq_len))(
        flat_places, picked_grad.reshape(seq_count, per_seq, model_width)
    )
    sum_grad, grad_gain_two, grad_shift_two = norm_back_two(final_grad)
    grad_down_bias = jnp.sum(sum_grad, (0, 1))
    second_low = sum_grad.astype(bf16)
    grad_down_weight = jnp.einsum("nlf,nld->fd", active_low, second_low, preferred_element_type=f32)
    active_grad = jnp.einsum("nld,fd->nlf", second_low, down_weight, preferred_element_type=f32)
    (inner_grad,) = gelu_back(active_grad)
    grad_up_bias = jnp.sum(inner_grad, (0, 1))
    inner_low = inner_grad.astype(bf16)
    grad_up_weight = jnp.einsum("nld,nlf->df", first_low, inner_low, preferred_element_type=f32)
    first_grad = sum_grad + jnp.einsum(
        "nlf,df->nld", inner_low, up_weight, preferred_element_type=f32
    )
    resid_grad, grad_gain_one, grad_shift_one = norm_back_one(first_grad)
    grad_out_bias = jnp.sum(resid_grad, (0, 1))
    resid_low = resid_grad.astype(bf16)
    grad_out_weight = jnp.einsum("nld,nle->de", mixed_low, resid_low, preferred_element_type=f32)
    mixed_grad = (
        jnp.einsum("nle,de->nld", resid_low, out_weight, preferred_element_type=f32)
        .astype(bf16)
        .reshape(split_shape)
    )
    value_grad = jnp.einsum("nhlm,nlhe->nmhe", probs_low, mixed_grad, preferred_element_type=f32)
    prob_grad = jnp.einsum("nlhe,nmhe->nhlm", mixed_grad, value_rows, preferred_element_type=f32)
    (score_back,) = soft_back(prob_grad)
    score_low = score_back.astype(bf16)
    query_grad = jnp.einsum("nhlm,nmhe->nlhe", score_low, key_rows, preferred_element_type=f32)
    key_grad = jnp.einsum("nhlm,nlhe->nmhe", score_low, queries, preferred_element_type=f32)
    flat_shape = (seq_count, seq_len, model_width)
    query_grad = query_grad.reshape(flat_shape)
    key_grad = key_grad.reshape(flat_shape)
    value_grad = value_grad.reshape(flat_shape)
    grad_query_bias = jnp.sum(query_grad, (0, 1))
    grad_value_bias = jnp.sum(value_grad, (0, 1))
    packed_grad = jnp.concatenate([query_grad, key_grad, value_grad], -1).astype(bf16)
    grad_qkv_weight = jnp.einsum("nld,nle->de", tokens, packed_grad, preferred_element_type=f32)
    input_grad = resid_grad + jnp.einsum(
        "nle,de->nld", packed_grad, qkv_weight, preferred_element_type=f32
    )
    vectors = jnp.concatenate(
        [
            jnp.stack(
                [
                    grad_query_bias,
                    grad_value_bias,
                    grad_out_bias,
                    grad_gain_one,
                    grad_shift_one,
                    grad_down_bias,
                    grad_gain_two,
                    grad_shift_two,
                ]
            ),
            grad_up_bias.reshape(-1, model_width),
        ]
    )
    vectors = jnp.pad(vectors, ((0, -vectors.shape[0] % 16), (0, 0)))
    mats = (grad_down_weight, grad_up_weight, grad_out_weight, grad_qkv_weight)
    down_sum, up_sum, out_sum, qkv_sum, vector_sum = reduce_params(
        [m.astype(bf16) for m in mats], vectors, lax.axis_size("batch"), lax.axis_size("doc")
    )
    nb = lax.axis_size("batch")
    slot = lax.axis_index("batch")

    def share(v):
        return lax.dynamic_slice_in_dim(v, slot * (v.shape[0] // nb), v.shape[0] // nb)

    up_bias_sum = vector_sum[8 : 8 + grad_up_bias.shape[0] // model_width].reshape(-1)
    results = (
        qkv_sum.astype(f32),
        share(vector_sum[0]),
        share(vector_sum[1]),
        out_sum.astype(f32),
        share(vector_sum[2]),
        share(vector_sum[3]),
        share(vector_sum[4]),
        up_sum.astype(f32),
        share(up_bias_sum),
        down_sum.astype(f32),
        share(vector_sum[5]),
        share(vector_sum[6]),
        share(vector_sum[7]),
    )
    block_out = final_rows.astype(bf16).reshape(hidden_in.shape)
    grad_in = input_grad.astype(bf16).reshape(hidden_in.shape)
    return (
        block_out,
        loss,
        grad_in,
        grad_query,
        results[0],
        results[1],
        results[2],
        results[3],
        results[4],
        results[5],
        results[6],
        results[7],
        results[8],
        results[9],
        results[10],
        results[11],
        results[12],
    )


def solution(mesh):
    in_specs = (
        P("batch", "doc", None, None),
        P("batch", "doc", None),
        P("batch", "doc", None, None),
        P(),
        P("batch", None, "doc"),
        P("batch", "doc", None, None),
        P(),
        P(),
        P(),
        P(),
        P(),
        P(),
        P(),
        P(),
        P(),
        P(),
        P(),
        P(),
        P(),
        P("batch", None),
    )
    out_specs = (
        P("batch", "doc", None, None),
        P("batch", None),
        P("batch", "doc", None, None),
        P("batch", None, "doc"),
        P("batch", None),
        P("batch"),
        P("batch"),
        P("batch", None),
        P("batch"),
        P("batch"),
        P("batch"),
        P("batch", None),
        P("batch"),
        P("batch", None),
        P("batch"),
        P("batch"),
        P("batch"),
    )
    paired = dict(mesh.shape) == {"batch": 8, "doc": 4}
    return jax.shard_map(paired_local if paired else local, mesh=mesh, in_specs=in_specs, out_specs=out_specs, check_vma=False)
```

```python
from functools import partial
import itertools
import math

import jax
import jax.numpy as jnp
from jax import lax
from jax.experimental import pallas as pl
from jax.experimental.pallas import tpu as pltpu
from jax.sharding import PartitionSpec as P

HEAD_DIM = 64
MESH = pl.DeviceIdType.MESH
VMEM_BYTES = 64000000


class Spot:
    def __init__(self):
        self.at = {"batch": lax.axis_index("batch"), "doc": lax.axis_index("doc")}

    def mine(self, key):
        axis, k = key
        return lax.rem(self.at[axis] // (1 << k), 2)

    def others(self):
        nd = lax.axis_size("doc")
        return [(self.at["batch"], lax.rem(self.at["doc"] + j, nd)) for j in range(1, nd)]

    def peer(self, key):
        axis, k = key
        moved = dict(self.at)
        moved[axis] = self.at[axis] + (1 - 2 * self.mine(key)) * (1 << k)
        return (moved["batch"], moved["doc"])


def mesh_keys(nb, nd):
    batch = [("batch", k) for k in range(nb.bit_length() - 1)]
    doc = [("doc", k) for k in range(nd.bit_length() - 1)]
    return batch, doc


class Piece:
    def __init__(self, mat, col, rows, cols, lead, halve, both, spread):
        self.mat, self.col, self.rows, self.cols = mat, col, rows, cols
        self.lead, self.halve, self.both, self.spread = lead, halve, both, spread
        self.tile = (rows, cols)
        self.steps = (
            [("halve", key) for key in halve]
            + [("both", key) for key in both]
            + [("spread", key) for key in spread]
            + [("twin", ("doc", 0))]
        )
        self.width = cols * 2 ** len(spread)

    def buffers(self):
        two = [(2,) * (len(self.lead) - i - 1) + self.tile for i in range(len(self.halve))]
        two += [self.tile] * len(self.both)
        wide = (2,) * len(self.spread) + self.tile
        return [(2,) * len(self.lead) + self.tile] + two + [wide, wide]

    def bytes(self, i):
        kind, key = self.steps[i]
        unit = self.rows * self.cols * 2
        if kind == "halve":
            return unit * 2 ** (len(self.lead) - i - 1)
        return unit * (2 if kind == "twin" and self.spread else 1)


def plan_pieces(nb, nd, mats):
    batch, doc = mesh_keys(nb, nd)
    across = doc[1:]
    pieces = []
    for m, (rows, cols) in enumerate(mats):
        first = across[:1] if len(across) == 1 else []
        col = 0
        if first and cols % 256 == 0 and m == 0 or first and cols > 1024:
            wide = cols // 2 // 256 * 256 if m else 256
            chunk = 256 if wide % 512 else 512
            for _ in range(wide // chunk):
                pieces.append(
                    Piece(m, col, rows, chunk // 2, first + batch[::-1], first + batch, [], first)
                )
                col += chunk
        while col < cols:
            chunk = min(cols - col, 512)
            pieces.append(Piece(m, col, rows, chunk, batch[::-1], batch, across, []))
            col += chunk
    return pieces


def exchange_order(pieces, ready, topology):
    free = {}
    clock = [(ready[i], i, 0) for i in range(len(pieces))]
    done = []
    while clock:
        clock.sort()
        at, i, step = clock.pop(0)
        key = pieces[i].steps[step][1]
        link, weight, rate = topology[key]
        start = max(at, free.get(link, 0.0))
        end = start + pieces[i].bytes(step) * weight / rate
        free[link] = end
        done.append((end + 1.5, i, step))
        if step + 1 < len(pieces[i].steps):
            clock.append((end + 2.0, i, step + 1))
    return [(i, step) for _, i, step in sorted(done)]


class Flow:
    def __init__(self, piece, bufs, send, recv, base, spot):
        self.p, self.bufs, self.send, self.recv, self.base, self.spot = piece, bufs, send, recv, base, spot
        self.live = {}
        self.copies = []

    @property
    def grad(self):
        return self.bufs[0]

    def index(self, fixed):
        return tuple(fixed.get(key, slice(None)) for key in self.p.lead)

    def start(self, step):
        kind, key = self.p.steps[step]
        mine = self.spot.mine(key)
        n = len(self.p.halve) + len(self.p.both)
        if kind == "halve":
            src = self.bufs[0].at[self.index({**self.live, key: 1 - mine})]
            dst = self.bufs[1 + step]
        elif kind == "both":
            src = self.bufs[0].at[self.index(self.live)]
            dst = self.bufs[1 + step]
        elif kind == "spread":
            src = self.bufs[n + 1].at[mine]
            dst = self.bufs[n + 1].at[mine]
        else:
            src = self.bufs[n + 1]
            dst = self.bufs[n + 2]
        copy = pltpu.make_async_remote_copy(
            src_ref=src,
            dst_ref=dst,
            send_sem=self.send.at[self.base + step],
            recv_sem=self.recv.at[self.base + step],
            device_id=self.spot.peer(key),
            device_id_type=MESH,
        )
        copy.start()
        self.copies.append(copy)

    def finish(self, step):
        kind, key = self.p.steps[step]
        copy = self.copies[step]
        if kind == "both":
            copy.wait()
        else:
            copy.wait_recv()
        n = len(self.p.halve) + len(self.p.both)
        if kind in ("halve", "both"):
            if kind == "halve":
                self.live[key] = self.spot.mine(key)
            got = self.bufs[1 + step]
            free = [k for k in self.p.lead if k not in self.live]
            last = step + 1 == n
            for pick in itertools.product(range(2), repeat=len(free)):
                at = self.index({**self.live, **dict(zip(free, pick))})
                total = self.bufs[0][at] + got[pick]
                if last:
                    self.bufs[n + 1][tuple(self.spot.mine(k) for k in self.p.spread)] = total
                else:
                    self.bufs[0][at] = total

    def drain(self):
        for step, copy in enumerate(self.copies):
            if self.p.steps[step][0] != "both":
                copy.wait_send()


def link_table(nb, nd):
    batch, doc = mesh_keys(nb, nd)
    table = {key: (key, 2.0, 91e3) for key in batch + doc}
    table[("doc", 0)] = ("twin", 1.0, 450e3)
    if (nb, nd) == (8, 4):
        table[("batch", 1)] = ("z", 2.0, 91e3)
        table[("batch", 2)] = ("z", 4.0, 91e3)
    return table


def reduce_kernel(pieces, halves, order, n_mats, *refs):
    mats, refs = refs[:n_mats], refs[n_mats:]
    vec, refs = refs[0], refs[1:]
    outs, refs = refs[:n_mats], refs[n_mats:]
    vec_out, refs = refs[0], refs[1:]
    spot = Spot()
    nb, nd = lax.axis_size("batch"), lax.axis_size("doc")
    batch, doc = mesh_keys(nb, nd)
    keys = batch + doc
    bufs = []
    for p in pieces:
        k = len(p.buffers())
        bufs.append(refs[:k])
        refs = refs[k:]
    vec_send, vec_recv = refs[:2]
    send, recv, twin_send, twin_recv, vs, vr = refs[2:]

    barrier = pltpu.get_barrier_semaphore()
    for key in keys:
        pl.semaphore_signal(barrier, inc=1, device_id=spot.peer(key), device_id_type=MESH)
    pl.semaphore_wait(barrier, len(keys))

    core = spot.mine(("doc", 0))
    twin = spot.peer(("doc", 0))
    flows = []
    base = 0
    twins = []
    for i, p in enumerate(pieces):
        flow = Flow(p, bufs[i], send, recv, base, spot)
        base += len(p.steps)
        flows.append(flow)
        half = halves[p.mat]
        copies = []
        for j in range(2 ** len(p.spread)):
            cols = pl.ds(pl.multiple_of((1 - core) * half + p.col + j * p.cols, 128), p.cols)
            dst = flow.grad.at[j] if p.spread else flow.grad
            lead = (slice(None),) * len(batch)
            copy = pltpu.make_async_remote_copy(
                src_ref=mats[p.mat].at[lead + (slice(None), cols)],
                dst_ref=dst,
                send_sem=twin_send.at[2 * i + j],
                recv_sem=twin_recv.at[2 * i + j],
                device_id=twin,
                device_id_type=MESH,
            )
            copy.start()
            copies.append(copy)
        twins.append(copies)

    vec_now = vec[...]
    vec_copies = []

    def vec_step(i):
        vec_send[i] = vec_now.astype(jnp.bfloat16)
        copy = pltpu.make_async_remote_copy(
            src_ref=vec_send.at[i],
            dst_ref=vec_recv.at[i],
            send_sem=vs.at[i],
            recv_sem=vr.at[i],
            device_id=spot.peer(keys[i]),
            device_id_type=MESH,
        )
        copy.start()
        vec_copies.append(copy)

    vec_step(0)
    for i, p in enumerate(pieces):
        half = halves[p.mat]
        for j, copy in enumerate(twins[i]):
            copy.wait()
            cols = pl.ds(pl.multiple_of(core * half + p.col + j * p.cols, 128), p.cols)
            for pick in itertools.product(range(2), repeat=len(batch)):
                at = ((j,) if p.spread else ()) + pick
                flows[i].grad[at] = flows[i].grad[at] + mats[p.mat][pick + (slice(None), cols)]
        flows[i].start(0)
        if i + 1 < len(keys):
            vec_copies[i].wait()
            vec_now = vec_now + vec_recv[i].astype(jnp.float32)
            vec_step(i + 1)
    for i in range(len(vec_copies), len(keys) + 1):
        vec_copies[i - 1].wait()
        vec_now = vec_now + vec_recv[i - 1].astype(jnp.float32)
        if i < len(keys):
            vec_step(i)
    vec_out[...] = vec_now

    for i, step in order:
        flows[i].finish(step)
        p = pieces[i]
        if step + 1 < len(p.steps):
            flows[i].start(step + 1)
        else:
            half = halves[p.mat]
            for side, buf in ((core, bufs[i][-2]), (1 - core, bufs[i][-1])):
                for j in range(2 ** len(p.spread)):
                    cols = pl.ds(pl.multiple_of(side * half + p.col + j * p.cols, 128), p.cols)
                    outs[p.mat][:, cols] = buf[j] if p.spread else buf[...]
    for flow in flows:
        flow.drain()


def reduce_params(mats, vectors, nb, nd):
    batch, doc = mesh_keys(nb, nd)
    shares = [(m.shape[0] // nb, m.shape[1]) for m in mats]
    halves = [c // 2 for _, c in shares]
    pieces = plan_pieces(nb, nd, [(r, c // 2) for r, c in shares])
    order = exchange_order(pieces, [3.0 * i for i in range(len(pieces))], link_table(nb, nd))
    keys = batch + doc
    scratch = []
    for p in pieces:
        scratch += [pltpu.VMEM(shape, jnp.bfloat16) for shape in p.buffers()]
    scratch += [pltpu.VMEM((len(keys),) + vectors.shape, jnp.bfloat16)] * 2
    steps = sum(len(p.steps) for p in pieces)
    dma = pltpu.SemaphoreType.DMA
    scratch += [dma((steps,)), dma((steps,)), dma((2 * len(pieces),)), dma((2 * len(pieces),))]
    scratch += [dma((len(keys),)), dma((len(keys),))]
    vm = pl.BlockSpec(memory_space=pltpu.VMEM)
    return pl.pallas_call(
        partial(reduce_kernel, pieces, halves, order, len(mats)),
        out_shape=[jax.ShapeDtypeStruct(s, jnp.bfloat16) for s in shares]
        + [jax.ShapeDtypeStruct(vectors.shape, jnp.float32)],
        in_specs=[vm] * (len(mats) + 1),
        out_specs=[vm] * (len(mats) + 1),
        scratch_shapes=scratch,
        compiler_params=pltpu.CompilerParams(
            collective_id=0, has_side_effects=True, vmem_limit_bytes=VMEM_BYTES
        ),
    )(*[m.reshape((2,) * len(batch) + (m.shape[0] // nb, m.shape[1])) for m in mats], vectors)


F32, BF16 = jnp.float32, jnp.bfloat16
NT = (((1,), (1,)), ((), ()))
TN = (((0,), (0,)), ((), ()))
EPS = 1e-06


def mm(a, b):
    return jnp.dot(a, b, preferred_element_type=F32)


def mm_nt(a, b):
    return lax.dot_general(a, b, NT, preferred_element_type=F32)


def mm_tn(a, b):
    return lax.dot_general(a, b, TN, preferred_element_type=F32)


def mm_exact(a, b, dims=(((1,), (0,)), ((), ()))):
    return lax.dot_general(a, b, dims, preferred_element_type=F32, precision=lax.Precision.HIGHEST)


def iota(shape, axis):
    return lax.broadcasted_iota(jnp.int32, shape, axis)


def normed(z):
    centred = z - jnp.mean(z, -1, keepdims=True)
    rstd = lax.rsqrt(jnp.mean(centred * centred, -1, keepdims=True) + EPS)
    return centred * rstd, rstd


def norm_back(grad, hat, rstd, gain):
    g = grad * gain
    inner = g - jnp.mean(g, -1, keepdims=True) - hat * jnp.mean(g * hat, -1, keepdims=True)
    return rstd * inner


def gelu(x):
    return 0.5 * x * (1.0 + lax.erf(x * math.sqrt(0.5)))


def gelu_slope(x):
    density = jnp.exp(-0.5 * x * x) * (1.0 / math.sqrt(2.0 * math.pi))
    return 0.5 * (1.0 + lax.erf(x * math.sqrt(0.5))) + x * density


def column_of(row_block):
    n, m = row_block.shape
    diag = iota((m, m), 0) == iota((m, m), 1)
    cols = [
        jnp.sum(jnp.where(diag, jnp.broadcast_to(row_block[i : i + 1, :], (m, m)), 0), 1, keepdims=True)
        for i in range(n)
    ]
    return jnp.concatenate(cols, 0)


class Net:
    def __init__(self, send, recv):
        self.send, self.recv, self.sends, self.recvs, self.open, self.due = send, recv, 0, 0, [], {}

    def branch(self):
        twin = Net(self.send, self.recv)
        twin.open = list(self.open)
        twin.due = {k: list(v) for k, v in self.due.items()}
        return twin

    def take(self):
        self.sends += 1
        self.recvs += 1
        return self.sends - 1, self.recvs - 1

    def take_chain(self, n):
        self.sends += 1
        self.recvs += n
        return [(self.sends - 1, self.recvs - n + i) for i in range(n)]

    def copy(self, src, dst, peer, at):
        return pltpu.make_async_remote_copy(
            src_ref=src,
            dst_ref=dst,
            send_sem=self.send.at[at[0]],
            recv_sem=self.recv.at[at[1]],
            device_id=peer,
            device_id_type=MESH,
        )

    def put(self, src, dst, peer, at):
        self.copy(src, dst, peer, at).start()

    def group(self, due, copies, whole):
        at = self.take()
        for src, dst, peer in copies:
            self.put(src, dst, peer, at)
        all_of = self.copy(whole(len(copies)), whole(len(copies)), copies[0][2], at)
        self.expect(due, all_of.wait_recv)
        self.open.append(all_of.wait_send)

    def expect(self, due, wait):
        self.due.setdefault(due, []).append(wait)

    def collect(self, due):
        for wait in self.due.pop(due):
            wait()

    def drain(self):
        for wait in self.open:
            wait()
        self.open = []


class Trip:
    def __init__(self, tile, lead, halve, both, end):
        self.tile, self.lead, self.halve, self.both = tile, lead, halve, both
        self.steps = [("halve", k) for k in halve] + [("both", k) for k in both]
        self.sums = len(self.steps)
        ends = {"": [], "two": [("spread", ("doc", 1)), ("twin", ("doc", 0))], "three": [("three", None)]}
        self.steps += ends[end]
        self.end = end

    def buffers(self):
        shapes = [(2,) * len(self.lead) + self.tile]
        shapes += [(2,) * (len(self.lead) - i - 1) + self.tile for i in range(len(self.halve))]
        shapes += [self.tile] * len(self.both)
        return shapes + [((4,) if self.end else ()) + self.tile]

    def bytes(self, i):
        kind, key = self.steps[i]
        unit = 2 * math.prod(self.tile)
        if kind == "halve":
            return unit * 2 ** (len(self.lead) - i - 1)
        return unit * {"twin": 2, "three": 2}.get(kind, 1)


class TripRun:
    def __init__(self, trip, bufs, sems, net, spot):
        self.t, self.bufs, self.at_step, self.net, self.spot = trip, bufs, sems, net, spot
        self.live = {}

    @property
    def final(self):
        return self.bufs[-1]

    def at(self, fixed):
        return tuple(fixed.get(key, slice(None)) for key in self.t.lead)

    def place(self):
        return (2 * self.spot.mine(("doc", 0)) + self.spot.mine(("doc", 1)),) if self.t.end else ()

    def start(self, step):
        kind, key = self.t.steps[step]
        if kind == "three":
            mine = self.final.at[self.place()]
            sem = self.at_step[step]
            for peer in self.spot.others():
                self.net.put(mine, mine, peer, sem)
            view = self.final.at[pl.ds(0, 3)]
            copy = self.net.copy(view, view, self.spot.peer(("doc", 0)), sem)
            self.net.expect(sem, copy.wait_recv)
            self.net.expect(sem, copy.wait_send)
            return
        if kind == "halve":
            src = self.bufs[0].at[self.at({**self.live, key: 1 - self.spot.mine(key)})]
            dst = self.bufs[1 + step]
        elif kind == "both":
            src, dst = self.bufs[0].at[self.at(self.live)], self.bufs[1 + step]
        elif kind == "spread":
            src = dst = self.final.at[self.place()]
        else:
            src = dst = self.final.at[pl.ds(2 * self.spot.mine(key), 2)]
        at = self.at_step[step]
        copy = self.net.copy(src, dst, self.spot.peer(key), at)
        copy.start()
        self.net.expect(at, copy.wait_recv)
        self.net.expect(at, copy.wait_send)

    def finish(self, step):
        kind, key = self.t.steps[step]
        self.net.collect(self.at_step[step])
        if step < self.t.sums:
            if kind == "halve":
                self.live[key] = self.spot.mine(key)
            got = self.bufs[1 + step]
            free = [k for k in self.t.lead if k not in self.live]
            for pick in itertools.product(range(2), repeat=len(free)):
                at = self.at({**self.live, **dict(zip(free, pick))})
                total = self.bufs[0][at] + got[pick]
                if step + 1 == self.t.sums:
                    self.final[self.place()] = total
                else:
                    self.bufs[0][at] = total


ALONG_Z = 2


def layer_trips(share):
    y, z0, z1, x = ("batch", 0), ("batch", 1), ("batch", 2), ("doc", 1)
    block = [Trip((share, 384), [z1, y], [y, z1], [], "two") for _ in range(ALONG_Z)]
    block += [Trip((share, 384), [z1, z0], [z0, z1], [], "two") for _ in range(4 - ALONG_Z)]
    block += [Trip((share, 384), [z1, y], [y, z1], [], "two")]
    orders = [[y, z0, z1], [y, z0, z1], [y, z0, z1]]
    wide = [Trip((share, 128), [z1, z0, y], order, [], "three") for order in orders]
    small = Trip((16, 768), [], [], [y, z0, z1, x, ("doc", 0)], "")
    return block + wide + [small]


LINKS = {
    ("batch", 0): [("y", 2.0)],
    ("batch", 1): [("z", 2.0)],
    ("batch", 2): [("far", 4.0), ("z", 2.0)],
    ("doc", 1): [("x", 2.0)],
    ("doc", 0): [("twin", 0.2)],
    None: [("x", 2.0)],
}
IN_FLIGHT = 3
LINK_RATE = 115e3


def trip_program(trips, stages):
    def wire(i, step):
        uses = LINKS[trips[i].steps[step][1]]
        return [(link, trips[i].bytes(step) * copies / LINK_RATE) for link, copies in uses]

    def to_go(i, step):
        return sum(max(t for _, t in wire(i, n)) + 2.0 for n in range(step, len(trips[i].steps)))

    events = [(at, -1, n, 0) for n, (at, _) in enumerate(stages)]
    free, flying, waiting, program = {}, {}, {}, []
    while events:
        events.sort()
        now, kind, i, step = events.pop(0)
        if kind < 0:
            program.append(("make", i, 0))
            ready = [(n, 0) for n in stages[i][1]]
        else:
            program.append(("finish", i, step))
            flying[wire(i, step)[0][0]] -= 1
            ready = [(i, step + 1)] if step + 1 < len(trips[i].steps) else []
        for n, s in ready:
            waiting.setdefault(wire(n, s)[0][0], []).append((-to_go(n, s), n, s))
        for link, queue in waiting.items():
            while queue and flying.get(link, 0) < IN_FLIGHT:
                queue.sort()
                _, n, s = queue.pop(0)
                program.append(("start", n, s))
                flying[link] = flying.get(link, 0) + 1
                end = now
                for used, t in wire(n, s):
                    free[used] = max(now, free.get(used, 0.0)) + t
                    end = max(end, free[used])
                events.append((end + 1.8, 0, n, s))
    return program


def layer_kernel(trips, *refs):
    (
        hidden, segs, places, targets, query, doc_rows,
        bias_q, bias_v, bias_o, gain1, shift1, bias_up, bias_down, gain2, shift2,
        qkv_hbm, out_hbm, up_hbm, down_hbm, vocab_hbm,
        block_out, loss_out, grad_in, grad_query, mats_out, wide_out, vec_out,
        wqkv, wout, wup, wdown, wvoc,
        qb, kb, vb, mixed, first_norm, first_low, acc,
        x4, x4t, kvb, kv4, sp, sp_send, qm, qm_send,
        picks, tsend, trecv, target_rows, usend, urecv, ssend, srecv, logits,
        qexp, probs, probs_low,
        hints, hints_in, joint, joint_in,
        left0, left0_y, left1, left1_y, a1, a1_y, at, at_y, second_b, inner_b, rest_b, g1, g1_y, g2,
        vecs, up_bias_s,
        block_v, grad_v, load_sem, store_sem, send, recv, *trip_bufs,
    ) = refs
    bias_q, bias_v, bias_o, gain1, shift1, bias_up, bias_down, gain2, shift2 = (
        b[...].reshape(1, -1) for b in (bias_q, bias_v, bias_o, gain1, shift1, bias_up, bias_down, gain2, shift2)
    )
    left0, left1, a1, at, g1 = (left0, left0_y), (left1, left1_y), (a1, a1_y), (at, at_y), (g1, g1_y)
    spot = Spot()
    batch, doc = spot.at["batch"], spot.at["doc"]
    nb, nd = lax.axis_size("batch"), lax.axis_size("doc")
    core, x = spot.mine(("doc", 0)), spot.mine(("doc", 1))
    z0 = spot.mine(("batch", 1))
    rows, width = hidden.shape
    pairs, slots = places.shape
    n_pick = pairs * slots
    heads = width // HEAD_DIM
    share = width // nb
    net = Net(send, recv)

    loads = [
        pltpu.make_async_copy(qkv_hbm.at[:, pl.ds(width, 2 * width)], wqkv.at[:, pl.ds(width, 2 * width)], load_sem.at[0]),
        pltpu.make_async_copy(vocab_hbm, wvoc, load_sem.at[1]),
        pltpu.make_async_copy(qkv_hbm.at[:, pl.ds(0, width)], wqkv.at[:, pl.ds(0, width)], load_sem.at[2]),
        pltpu.make_async_copy(out_hbm, wout, load_sem.at[3]),
        pltpu.make_async_copy(up_hbm, wup, load_sem.at[4]),
        pltpu.make_async_copy(down_hbm, wdown, load_sem.at[5]),
    ]
    for load in loads:
        load.start()

    batch_peers = [(lax.rem(batch + j, nb), doc) for j in range(1, nb)]
    doc_peers = [(batch, lax.rem(doc + j, nd)) for j in range(1, nd)]

    def side_peer(dx, dz, to_core, key):
        tx = lax.rem(x + dx, 2)
        mine = spot.mine(key)
        tz = lax.rem(mine + dz, 2)
        return (batch + (tz - mine) * (1 << key[1]), 2 * tx + to_core), tx, tz

    routes = [("batch", 1), ("batch", 0)]
    twin = spot.peer(("doc", 0))
    slots_of = [4 * spot.mine(key) + doc for key in routes]

    def fan(due, part_of, dst, lanes, to_core, dzs, route):
        slot = slots_of[route]
        sem = net.take()
        land = dst.at[slot, :, pl.ds(0, lanes)]
        always = 0
        for dz in dzs:
            for dx in range(2):
                peer, tx, tz = side_peer(dx, dz, to_core, routes[route])
                copy = net.copy(part_of(tx, tz), land, peer, sem)
                if dx or dz:
                    copy.start()
                    always += 1
                else:
                    pl.when(core != to_core)(copy.start)
        own = 0 in dzs

        def sized(n):
            view = dst.at[pl.ds(0, n), :, pl.ds(0, lanes)]
            return net.copy(view, view, twin, sem)

        def sent():
            if own:
                pl.when(core != to_core)(sized(always + 1).wait_send)
                pl.when(core == to_core)(sized(always).wait_send)
            else:
                sized(always).wait_send()

        net.open.append(sent)
        net.expect(due, lambda: pl.when(core == to_core)(sized(4 * len(dzs) - own).wait_recv))

    far = [
        side_peer(dx, 1, lax.rem(core + dc, 2), key)[0] for key in routes for dx, dc in ((1, 0), (1, 1), (0, 1))
    ]
    everyone = batch_peers + doc_peers + far
    barrier = pltpu.get_barrier_semaphore()
    for peer in everyone:
        pl.semaphore_signal(barrier, inc=1, device_id=peer, device_id_type=MESH)

    place_col = column_of(places[...])
    pick_bool = iota((n_pick, rows), 1) == place_col
    pick = pick_bool.astype(BF16)
    pick_f32 = pick_bool.astype(F32)
    tokens = hidden[...]
    loads[0].wait()
    kb[...] = mm(tokens, wqkv[:, width : 2 * width]).astype(BF16)
    vb[...] = (mm(tokens, wqkv[:, 2 * width :]) + bias_v).astype(BF16)
    tokens_p = mm(pick, tokens).astype(BF16)

    pl.semaphore_wait(barrier, len(everyone))
    own_part = query.shape[1]
    spread_lanes = (iota((own_part, own_part * nd), 0) + own_part * doc == iota((own_part, own_part * nd), 1)).astype(F32)
    hints[0:pairs, :] = mm_exact(query[...], spread_lanes)
    hints[8 : 8 + pairs, :] = doc_rows[...]
    hints_in[doc, 0:pairs, :] = hints[0:pairs, :]
    hints_in[doc, 8 : 8 + pairs, :] = hints[8 : 8 + pairs, :]
    net.group("hint", [(hints, hints_in.at[doc], peer) for peer in doc_peers], lambda n: hints_in.at[pl.ds(0, n)])
    beside = spot.peer(("doc", 1))
    net.group("tokens", [(hidden, x4.at[doc], beside)], lambda n: x4.at[pl.ds(0, n)])
    net.group("all tokens", [(hidden, x4.at[doc], twin)], lambda n: x4.at[pl.ds(0, n)])
    x4[doc] = hidden[...]

    loads[1].wait()
    entries = wvoc.shape[0]
    target_col = jnp.concatenate([column_of(targets[j]) for j in range(nb)], 0) - batch * entries
    all_rows = nb * n_pick
    is_target = iota((all_rows, entries), 1) == target_col
    tsend[...] = mm(is_target.astype(BF16), wvoc[...]).astype(BF16).reshape(nb, nd, n_pick // nd, width)
    trecv[batch] = tsend[batch, doc]
    net.group("part", [(tsend.at[p[0], doc], trecv.at[batch], p) for p in batch_peers], lambda n: trecv.at[pl.ds(0, n)])

    loads[2].wait()
    query_p = (mm(tokens_p, wqkv[:, 0:width]) + bias_q).astype(BF16)

    tall = heads * n_pick
    own_head = iota((tall, width), 0) // n_pick == iota((tall, width), 1) // HEAD_DIM

    def expand(v):
        return jnp.where(own_head, jnp.concatenate([v] * heads, 0), jnp.zeros((), v.dtype))

    def fold(v):
        return jnp.sum(jnp.where(own_head, v, 0.0).reshape(heads, n_pick, width), 0)

    seg_row = segs[...]
    seg_pick = jnp.sum(jnp.where(pick_bool, jnp.broadcast_to(seg_row, (n_pick, rows)), 0), 1, keepdims=True)
    same_pick = seg_pick == seg_row
    scale = 1.0 / math.sqrt(HEAD_DIM)
    qexp[...] = expand(query_p)
    scores = mm_nt(qexp[...], kb[...]) * scale
    same_tall = jnp.concatenate([same_pick.astype(F32)] * heads, 0) > 0.5
    scores = jnp.where(same_tall, scores, -1e30)
    weights = jnp.exp(scores - jnp.max(scores, -1, keepdims=True))
    weights = weights / jnp.sum(weights, -1, keepdims=True)
    probs[...] = weights
    probs_low[...] = weights.astype(BF16)
    mixed_p = fold(mm(probs_low[...], vb[...])).astype(BF16)
    loads[3].wait()
    attended = mm(mixed_p, wout[...]) + bias_o
    hat1, rstd1 = normed(tokens_p.astype(F32) + attended)
    first_p = hat1 * gain1 + shift1
    first_low_p = first_p.astype(BF16)
    loads[4].wait()
    inner_p = mm(first_low_p, wup[...]) + bias_up
    active_p = gelu(inner_p).astype(BF16)
    loads[5].wait()
    second_p = mm(active_p, wdown[...]) + bias_down
    hat2, rstd2 = normed(first_p + second_p)
    picks[batch] = (hat2 * gain2 + shift2).astype(BF16)
    net.group("pick", [(picks.at[batch], picks.at[batch], p) for p in batch_peers], lambda n: picks.at[pl.ds(0, n)])

    ff = wup.shape[1]
    counts = [ALONG_Z, 4 - ALONG_Z]
    firsts = [0, ALONG_Z]
    quads = [(z1, other) for z1 in range(2) for other in range(2)]
    lanes0 = [4 * share * (counts[0] + 1), 4 * share * counts[1]]
    lanes1 = [8 * share, 4 * share]
    for route in range(2):
        wide_lanes = share * counts[route]
        for k in range(2):
            for n, (z1, other) in enumerate(quads):
                b = 4 * z1 + (2 * k + other if route == 0 else 2 * other + k)
                own = slice(b * share, (b + 1) * share)
                start = 4 * share * b + share * firsts[route]
                left0[route][k, :, n * wide_lanes : (n + 1) * wide_lanes] = active_p[:, start : start + wide_lanes]
                left1[route][k, :, n * share : (n + 1) * share] = first_low_p[:, own]
                if route == 0:
                    at0 = 4 * wide_lanes + n * share
                    left0[route][k, :, at0 : at0 + share] = mixed_p[:, own]
                    left1[route][k, :, (4 + n) * share : (5 + n) * share] = tokens_p[:, own]

    def keep_left(route, left, lanes):
        def keep():
            a1[route][slots_of[route], :, 0:lanes] = left[route][spot.mine(routes[route])]

        return keep

    for route in range(2):
        pl.when(core == 0)(keep_left(route, left0, lanes0[route]))
        pl.when(core == 1)(keep_left(route, left1, lanes1[route]))

    def send_left(dzs):
        for route in range(2):
            fan("left", lambda tx, tz: left0[route].at[tz], a1[route], lanes0[route], 0, dzs, route)
            fan("left", lambda tx, tz: left1[route].at[tz], a1[route], lanes1[route], 1, dzs, route)

    half_w, half_f = width // 2, ff // 2
    tall_half = tall // 2
    send_left([0])

    def half_heads(due, src, dst, to_core):
        sem = net.take()
        for dx in range(2):
            peer, tx, _ = side_peer(dx, 0, to_core, routes[0])
            copy = net.copy(src.at[tx], dst.at[doc], peer, sem)
            if dx:
                copy.start()
            else:
                pl.when(core != to_core)(copy.start)

        def keep():
            dst[doc] = src[x]

        def sized(n):
            view = dst.at[pl.ds(0, n)]
            return net.copy(view, view, twin, sem)

        def sent():
            pl.when(core != to_core)(sized(2).wait_send)
            pl.when(core == to_core)(sized(1).wait_send)

        pl.when(core == to_core)(keep)
        net.open.append(sent)
        net.expect(due, lambda: pl.when(core == to_core)(sized(3).wait_recv))

    def halves(dst, v):
        for s in range(2):
            dst[s] = v[:, s * half_w : (s + 1) * half_w]

    sp_send[1] = probs_low[...].reshape(2, tall_half, rows)
    half_heads("heads", sp_send.at[1], sp, 1)
    halves(qm_send.at[0], query_p)
    half_heads("heads", qm_send.at[0], qm, 0)

    seg_col = jnp.sum(
        jnp.where(iota((rows, rows), 0) == iota((rows, rows), 1), jnp.broadcast_to(seg_row, (rows, rows)), 0),
        1,
        keepdims=True,
    )
    qb[...] = (mm(tokens, wqkv[:, 0:width]) + bias_q).astype(BF16)

    def attend(i):
        lanes = pl.ds(pl.multiple_of(i * 128, 128), 128)
        q_s, k_s, v_s = qb[:, lanes], kb[:, lanes], vb[:, lanes]
        low = iota((rows, 128), 1) < HEAD_DIM
        same = seg_col == seg_row
        parts = []
        for side in (low, ~low):
            s = mm_nt(jnp.where(side, q_s, jnp.zeros((), BF16)), k_s) * scale
            s = jnp.where(same, s, -1e30)
            e = jnp.exp(s - jnp.max(s, -1, keepdims=True))
            p = (e / jnp.sum(e, -1, keepdims=True)).astype(BF16)
            parts.append(mm(p, v_s))
        mixed[:, lanes] = jnp.where(low, parts[0], parts[1]).astype(BF16)

    half_way = width // 256
    pl.loop(0, half_way)(attend)
    send_left([1])
    net.collect("tokens")
    net.group("all tokens", [(x4.at[beside[1]], x4.at[beside[1]], twin)], lambda n: x4.at[pl.ds(0, n)])
    net.collect("part")
    part = trecv[0].astype(F32)
    for j in range(1, nb):
        part += trecv[j].astype(F32)
    target_rows[doc] = part.astype(BF16)
    net.group("target", [(target_rows.at[doc], target_rows.at[doc], p) for p in doc_peers], lambda n: target_rows.at[pl.ds(0, n)])
    pl.loop(half_way, width // 128)(attend)

    net.collect("pick")
    logits[...] = mm_nt(picks[...].reshape(all_rows, width), wvoc[...])
    lg = logits[...]
    top = jnp.max(lg, 1, keepdims=True)
    chosen = jnp.sum(jnp.where(is_target, lg, 0.0), 1, keepdims=True)
    others = jnp.where(is_target, 0.0, jnp.exp(lg - top))
    total = jnp.sum(others, 1, keepdims=True)
    lane = iota((all_rows, 128), 1)
    stats = jnp.where(lane == 0, top, jnp.where(lane == 1, total, chosen)).T
    blank = jnp.zeros((8, 128 - n_pick), F32)
    for j in range(nb):
        ssend[j] = jnp.concatenate([stats[0:8, n_pick * j : n_pick * (j + 1)], blank], 1)
    srecv[batch] = ssend[batch]
    net.group("stats", [(ssend.at[p[0]], srecv.at[batch], p) for p in batch_peers], lambda n: srecv.at[pl.ds(0, n)])
    usend[...] = mm(others.astype(BF16), wvoc[...]).astype(BF16).reshape(nb, n_pick, width)
    urecv[batch] = usend[batch]
    net.group("back", [(usend.at[p[0]], urecv.at[batch], p) for p in batch_peers], lambda n: urecv.at[pl.ds(0, n)])

    tokens = hidden[...]
    hat, _ = normed(tokens.astype(F32) + mm(mixed[...], wout[...]) + bias_o)
    first_norm[...] = hat * gain1 + shift1
    first_low[...] = first_norm[...].astype(BF16)
    acc[...] = first_norm[...] + bias_down
    chunk = 512
    up_bias_s[...] = bias_up

    def feed(i):
        cols = pl.ds(pl.multiple_of(i * chunk, chunk), chunk)
        hid = mm(first_low[...], wup[:, cols]) + up_bias_s[:, cols]
        acc[...] += mm(gelu(hid).astype(BF16), wdown[cols, :])

    pl.loop(0, ff // chunk // 2)(feed)

    net.collect("stats")
    tops = [srecv[j][0:1, :] for j in range(nb)]
    peak = tops[0]
    for t in tops[1:]:
        peak = jnp.maximum(peak, t)
    factors = [jnp.exp(t - peak) for t in tops]
    rest = jnp.zeros_like(peak)
    chosen = jnp.zeros_like(peak)
    for j in range(nb):
        rest += factors[j] * srecv[j][1:2, :]
        chosen += srecv[j][2:3, :]
    whole = rest + jnp.exp(chosen - peak)
    logp = chosen - peak - jnp.log(whole)
    of_pair = iota((pairs, 128), 1) // slots == iota((pairs, 128), 0)
    reader = jnp.sum(jnp.where(of_pair, jnp.broadcast_to(logp, (pairs, 128)), 0.0), 1, keepdims=True) / slots
    joint[...] = jnp.zeros_like(joint)
    joint[0:pairs, :] = jnp.broadcast_to(reader, (pairs, 128))
    joint_in[doc] = joint[...]
    net.group("joint", [(joint, joint_in.at[doc], p) for p in doc_peers], lambda n: joint_in.at[pl.ds(0, n)])
    shares = jnp.concatenate([f / whole for f in factors] + [rest / whole] + [jnp.zeros_like(peak)] * (15 - nb), 0).T

    pl.loop(ff // chunk // 2, ff // chunk)(feed)
    hat, _ = normed(acc[...])
    block_v[...] = (hat * gain2 + shift2).astype(BF16)
    block_store = pltpu.make_async_copy(block_v, block_out, store_sem.at[8])
    block_store.start()
    net.collect("all tokens")
    x4t[...] = x4[...].reshape(nd * rows, width).T

    net.collect("hint")
    full_query = hints_in[0, 0:pairs, :]
    for j in range(1, nd):
        full_query += hints_in[j, 0:pairs, :]
    docs = [hints_in[j, 8 : 8 + pairs, :] for j in range(nd)]
    score = [jnp.broadcast_to(jnp.sum(full_query * d, 1, keepdims=True), (pairs, 128)) for d in docs]
    net.collect("joint")
    both = [s + joint_in[j, 0:pairs, :] for j, s in enumerate(score)]

    def soft(vals):
        high = vals[0]
        for v in vals[1:]:
            high = jnp.maximum(high, v)
        es = [jnp.exp(v - high) for v in vals]
        tot = es[0]
        for e in es[1:]:
            tot = tot + e
        return [e / tot for e in es], high + jnp.log(tot)

    w_score, total_score = soft(score)
    w_joint, total_joint = soft(both)
    eye = iota((pairs, 128), 0) == iota((pairs, 128), 1)
    loss_out[...] = jnp.sum(jnp.where(eye, total_score - total_joint, 0.0), 0, keepdims=True)
    query_grad = (w_score[0] - w_joint[0]) * docs[0]
    for j in range(1, nd):
        query_grad += (w_score[j] - w_joint[j]) * docs[j]
    grad_query[...] = mm_exact(query_grad, spread_lanes, NT)
    mine = w_joint[0]
    for j in range(1, nd):
        mine = jnp.where(doc == j, w_joint[j], mine)
    row_weight = jnp.broadcast_to(mine.reshape(pairs, 1, 128), (pairs, slots, 128)).reshape(n_pick, 128)[:, 0:1]

    net.collect("left")

    def turn(route, lanes):
        def go():
            at[route][0:lanes, :] = a1[route][:, :, 0:lanes].reshape(8 * n_pick, lanes).T

        return go

    for route in range(2):
        pl.when(core == 0)(turn(route, lanes0[route]))
        pl.when(core == 1)(turn(route, lanes1[route]))

    net.collect("back")
    row_grad = jnp.zeros((n_pick, width), F32)
    for j in range(nb):
        row_grad += shares[0:n_pick, j : j + 1] * urecv[j].astype(F32)
    net.collect("target")
    at_target = target_rows[...].astype(F32).reshape(n_pick, width)
    row_grad -= shares[0:n_pick, nb : nb + 1] * at_target
    final_grad = row_grad * (row_weight / slots)

    def send_right(due, src, every, first, cols, dst, to_core, route):
        def part(tx):
            return pl.ds(pl.multiple_of(tx * every + first, 128), cols)

        fan(due, lambda tx, tz: src.at[:, part(tx)], dst, cols, to_core, [0, 1], route)

        def keep():
            dst[slots_of[route], :, 0:cols] = src[:, part(x)]

        pl.when(core == to_core)(keep)

    vecs[...] = jnp.zeros_like(vecs)
    sum_grad = norm_back(final_grad, hat2, rstd2, gain2)
    vecs[6:7, :] = jnp.sum(final_grad * hat2, 0, keepdims=True)
    vecs[7:8, :] = jnp.sum(final_grad, 0, keepdims=True)
    vecs[5:6, :] = jnp.sum(sum_grad, 0, keepdims=True)
    second_low = sum_grad.astype(BF16)
    second_b[...] = second_low
    for route in range(2):
        send_right(("g1", route), second_b, half_w, 0, half_w, g1[route], 0, route)
    inner_grad = mm_nt(second_low, wdown[...]) * gelu_slope(inner_p)
    inner_low = inner_grad.astype(BF16)
    inner_b[...] = inner_low
    for route in range(2):
        first, cols = firsts[route] * half_w, counts[route] * half_w
        send_right(("g1", route), inner_b, half_f, first, cols, g1[route], 1, route)
    up_bias_grad = jnp.sum(inner_grad, 0, keepdims=True)
    for i in range(ff // width):
        vecs[8 + i : 9 + i, :] = up_bias_grad[:, i * width : (i + 1) * width]
    first_grad = sum_grad + mm_nt(inner_low, wup[...])
    resid_grad = norm_back(first_grad, hat1, rstd1, gain1)
    resid_low = resid_grad.astype(BF16)
    rest_b[0] = resid_low
    send_right("g2", rest_b.at[0], half_w, 0, half_w, g2, 0, 0)
    vecs[3:4, :] = jnp.sum(first_grad * hat1, 0, keepdims=True)
    vecs[4:5, :] = jnp.sum(first_grad, 0, keepdims=True)
    vecs[2:3, :] = jnp.sum(resid_grad, 0, keepdims=True)
    mixed_grad_p = mm_nt(resid_low, wout[...]).astype(BF16)
    halves(qm_send.at[1], mixed_grad_p)
    half_heads("heads", qm_send.at[1], qm, 1)
    mixed_grad = expand(mixed_grad_p)
    prob_grad = mm_nt(mixed_grad, vb[...])
    p = probs[...]
    score_low = (p * (prob_grad - jnp.sum(prob_grad * p, -1, keepdims=True)) * scale).astype(BF16)
    sp_send[0] = score_low.reshape(2, tall_half, rows)
    half_heads("heads", sp_send.at[0], sp, 0)
    query_grad_p = fold(mm(score_low, kb[...]))
    rest_b[1] = query_grad_p.astype(BF16)
    send_right("g2", rest_b.at[1], half_w, 0, half_w, g2, 1, 0)
    vecs[0:1, :] = jnp.sum(query_grad_p, 0, keepdims=True)
    value_grad = mm_tn(probs_low[...], mixed_grad)
    kvb[1] = value_grad.astype(BF16)
    vecs[1:2, :] = jnp.sum(value_grad, 0, keepdims=True)

    sems = [net.take_chain(len(t.steps)) for t in trips]
    groups, left_over = [], list(trip_bufs)
    for t in trips:
        k = len(t.buffers())
        groups.append(left_over[:k])
        left_over = left_over[k:]

    def tail(side, net):
        runs = [TripRun(t, groups[n], sems[n], net, spot) for n, t in enumerate(trips)]
        stores = []

        def store(src, dst, n):
            copy = pltpu.make_async_copy(src, dst, store_sem.at[n])
            copy.start()
            stores.append(copy)

        def make_wide():
            net.collect("heads")
            half_tall = iota((tall_half, half_w), 0) // n_pick == iota((tall_half, half_w), 1) // HEAD_DIM
            for d in range(nd):
                tiled = jnp.concatenate([qm[d]] * (heads // 2), 0)
                tiled = jnp.where(half_tall, tiled, jnp.zeros((), BF16))
                kv4[d] = mm_tn(sp[d], tiled).astype(BF16)
            right = kv4[...].reshape(nd * rows, half_w)
            for b in range(nb):
                out = mm(x4t[b * share : (b + 1) * share, :], right).astype(BF16)
                for n in range(3):
                    runs[5 + n].bufs[0][b // 4, b // 2 % 2, b % 2] = out[:, 128 * n : 128 * (n + 1)]

        def block(i, route, offsets, g, col):
            left = jnp.concatenate([at[route][pl.ds(pl.multiple_of(o, 32), share), :] for o in offsets], 0)
            right = g[:, :, pl.ds(col, half_w)].reshape(8 * n_pick, half_w)
            out = mm(left, right).astype(BF16)
            for n, (z1, other) in enumerate(quads):
                runs[i].bufs[0][z1, other] = out[n * share : (n + 1) * share]

        def make_blocks(route):
            net.collect(("g1", route))
            for i in range(counts[route]):
                offsets = [((1 - core) * (n * counts[route] + i) + core * n) * share for n in range(4)]
                block(firsts[route] + i, route, offsets, g1[route], pl.multiple_of(core * i * half_w, 128))

        def make_last():
            net.collect("g2")
            first_row = (1 - core) * 4 * share * counts[0] + core * 4 * share
            block(4, 0, [first_row + n * share for n in range(4)], g2, 0)

        def make_inward():
            kvb[0] = mm_tn(score_low, qexp[...]).astype(BF16)
            inward = mm_nt(kvb[0], wqkv[:, width : 2 * width]) + mm_nt(kvb[1], wqkv[:, 2 * width :])
            at_rows = resid_grad + mm_nt(rest_b[1], wqkv[:, 0:width])
            grad_v[...] = (inward + mm_exact(pick_f32, at_rows, TN)).astype(BF16)
            store(grad_v, grad_in, 9)

        def make_sums():
            runs[8].bufs[0][...] = vecs[...].astype(BF16)

        along_y = list(range(ALONG_Z, 4))
        along_z = list(range(ALONG_Z))
        stages = (
            [
                (0.0, [8], make_sums),
                (0.6, along_y, lambda: make_blocks(1)),
                (1.2, along_z, lambda: make_blocks(0)),
                (1.8, [4], make_last),
                (8.0, [5, 6, 7], make_wide),
                (12.0, [], make_inward),
            ]
            if side == 0
            else [
                (0.0, [8], make_sums),
                (2.5, [5, 6, 7], make_wide),
                (5.0, along_y, lambda: make_blocks(1)),
                (5.6, along_z, lambda: make_blocks(0)),
                (6.2, [4], make_last),
                (10.0, [], make_inward),
            ]
        )
        last = []
        for what, i, step in trip_program(trips, [(t, made) for t, made, _ in stages]):
            if what == "make":
                stages[i][2]()
            elif what == "start":
                runs[i].start(step)
            elif trips[i].steps[step][1] in (("doc", 0), None):
                last.append((i, step))
            else:
                runs[i].finish(step)
        for i, step in last:
            runs[i].finish(step)
            if i < 5:
                store(runs[i].final, mats_out.at[i], i)
            elif i < 8:
                store(runs[i].final, wide_out.at[i - 5], i)
            else:
                vec_out[...] = runs[i].final[...]
        for copy in stores:
            copy.wait()
        net.drain()

    for side in range(2):
        pl.when(core == side)(partial(tail, side, net.branch()))
    block_store.wait()


def finish_kernel(block, grad, loss, gq, mats, wide, vec, *outs):
    (o_block, o_loss, o_grad, o_gq, o_qkv, o_qb, o_vb, o_out, o_ob, o_g1, o_s1, o_up, o_ub, o_down, o_db, o_g2, o_s2) = outs
    batch = lax.axis_index("batch")
    nb = lax.axis_size("batch")
    width = vec.shape[1]
    share, half = width // nb, width // 2
    o_block[...] = block[...]
    o_grad[...] = grad[...]
    o_loss[...] = loss[:, 0 : o_loss.shape[1]]
    o_gq[...] = gq[...]
    for s in range(2):
        cols = slice(s * half, (s + 1) * half)
        o_out[:, cols] = mats[4, s].astype(F32)
        o_qkv[:, cols] = mats[4, 2 + s].astype(F32)
        for i in range(4):
            o_down[i * share : (i + 1) * share, cols] = mats[i, s].astype(F32)
            o_up[:, (4 * s + i) * half : (4 * s + i + 1) * half] = mats[i, 2 + s].astype(F32)
        for c in range(2):
            for j in range(3):
                start = (1 + c) * width + s * half + 128 * j
                o_qkv[:, start : start + 128] = wide[j, 2 * c + s].astype(F32)
    v = vec[...].astype(F32)
    take = (iota((width, share), 0) == iota((width, share), 1) + batch * share).astype(F32)
    got = mm_exact(v, take)
    for i, o in enumerate((o_qb, o_vb, o_ob, o_g1, o_s1, o_db, o_g2, o_s2)):
        o[...] = got[i : i + 1, :]
    side = jnp.where(lax.rem(batch, 2) == 0, v[8:12, 0:half], v[8:12, half:])
    o_ub[...] = jnp.sum(jnp.where(iota((4, half), 0) == batch // 2, side, 0.0), 0)


def paired_local(*args):
    (
        hidden_in, segments, mask_pos, target_ids, query_emb, doc_emb,
        qkv_weight, query_bias, value_bias, out_weight, out_bias, gain_one, shift_one,
        up_weight, up_bias, down_weight, down_bias, gain_two, shift_two, vocab,
    ) = args
    rows, width = hidden_in.shape[2:]
    pairs, slots = mask_pos.shape[2:]
    n_pick = pairs * slots
    ff = up_weight.shape[1]
    entries = vocab.shape[0]
    nb, nd = lax.axis_size("batch"), lax.axis_size("doc")
    share = width // nb
    heads = width // HEAD_DIM
    trips = layer_trips(share)
    lanes_z, lanes_y = 4 * share * (ALONG_Z + 1), 4 * share * (4 - ALONG_Z)
    n_sems = sum(len(t.steps) for t in trips) + 28
    n_sends = len(trips) + 28
    vm, hbm = pl.BlockSpec(memory_space=pltpu.VMEM), pl.BlockSpec(memory_space=pl.ANY)

    def v(shape, dtype=BF16):
        return pltpu.VMEM(shape, dtype)

    dma = pltpu.SemaphoreType.DMA
    scratch = [
        v(qkv_weight.shape), v(out_weight.shape), v(up_weight.shape), v(down_weight.shape), v(vocab.shape),
        v((rows, width)), v((rows, width)), v((rows, width)), v((rows, width)),
        v((rows, width), F32), v((rows, width)), v((rows, width), F32),
        v((nd, rows, width)), v((width, nd * rows)), v((2, rows, width)), v((nd, rows, width // 2)),
        v((nd, heads * n_pick // 2, rows)), v((2, 2, heads * n_pick // 2, rows)),
        v((nd, n_pick, width // 2)), v((2, 2, n_pick, width // 2)),
        v((nb, n_pick, width)), v((nb, nd, n_pick // nd, width)), v((nb, n_pick // nd, width)),
        v((nd, n_pick // nd, width)), v((nb, n_pick, width)),
        v((nb, n_pick, width)), v((nb, 8, 128), F32), v((nb, 8, 128), F32), v((nb * n_pick, entries), F32),
        v((heads * n_pick, width)), v((heads * n_pick, rows), F32), v((heads * n_pick, rows)),
        v((16, 128), F32), v((nd, 16, 128), F32), v((8, 128), F32), v((nd, 8, 128), F32),
        v((2, n_pick, lanes_z)), v((2, n_pick, lanes_y)), v((2, n_pick, width)), v((2, n_pick, width // 2)),
        v((8, n_pick, lanes_z)), v((8, n_pick, max(lanes_y, width // 2))), v((lanes_z, 8 * n_pick)),
        v((max(lanes_y, width // 2), 8 * n_pick)),
        v((n_pick, width)), v((n_pick, ff)), v((2, n_pick, width)),
        v((8, n_pick, ALONG_Z * width // 2)), v((8, n_pick, (4 - ALONG_Z) * width // 2)), v((8, n_pick, width // 2)),
        v((16, width), F32), v((1, ff), F32),
        v((rows, width)), v((rows, width)), dma((6,)), dma((10,)), dma((n_sends,)), dma((n_sems,)),
    ]
    for t in trips:
        scratch += [v(shape) for shape in t.buffers()]
    sds = jax.ShapeDtypeStruct
    first = pl.pallas_call(
        partial(layer_kernel, trips),
        out_shape=[
            sds((rows, width), BF16),
            sds((1, 128), F32),
            sds((rows, width), BF16),
            sds((pairs, query_emb.shape[2]), F32),
            sds((5, 4, share, 384), BF16),
            sds((3, 4, share, 128), BF16),
            sds((16, width), BF16),
        ],
        in_specs=[vm] * 15 + [hbm] * 5,
        out_specs=[hbm, vm, hbm, vm, hbm, hbm, vm],
        scratch_shapes=scratch,
        compiler_params=pltpu.CompilerParams(
            collective_id=0, has_side_effects=True, vmem_limit_bytes=VMEM_BYTES
        ),
        name="layer",
    )
    biases = (query_bias, value_bias, out_bias, gain_one, shift_one, up_bias, down_bias, gain_two, shift_two)
    block, loss, grad, gq, mats, wide, vec = first(
        hidden_in.reshape(rows, width),
        segments.reshape(1, rows),
        mask_pos.reshape(pairs, slots),
        target_ids,
        query_emb.reshape(pairs, -1),
        doc_emb.reshape(pairs, -1),
        *biases,
        qkv_weight,
        out_weight,
        up_weight,
        down_weight,
        vocab,
    )
    small = sds((1, share), F32)
    outs = pl.pallas_call(
        finish_kernel,
        out_shape=[
            sds((rows, width), BF16), sds((1, pairs), F32), sds((rows, width), BF16), sds(gq.shape, F32),
            sds((share, 3 * width), F32), small, small, sds((share, width), F32), small, small, small,
            sds((share, ff), F32), sds((ff // nb,), F32), sds((ff // nb, width), F32), small, small, small,
        ],
        in_specs=[vm] * 7,
        out_specs=[vm] * 17,
        compiler_params=pltpu.CompilerParams(vmem_limit_bytes=VMEM_BYTES),
        name="finish",
    )(block, grad, loss, gq, mats, wide, vec)
    shapes = [hidden_in.shape, (1, pairs), hidden_in.shape, query_emb.shape]
    fixed = [o.reshape(s) for o, s in zip(outs[:4], shapes)]
    return tuple(fixed + [o.reshape(-1) if o.shape == (1, share) else o for o in outs[4:]])


def combined_all(x, axis, combine):
    everything = jax.tree.map(lambda part: lax.all_gather(part, axis), x)
    leading = jax.tree.map(lambda part: part[0], everything)

    def hop(k, so_far):
        return combine(so_far, jax.tree.map(lambda part: part[k], everything))

    return lax.fori_loop(1, lax.axis_size(axis), hop, leading)


def norm_rows(values, gain, shift):
    centre = jnp.mean(values, -1, keepdims=True)
    centred = values - centre
    spread = jnp.mean(centred * centred, -1, keepdims=True)
    return centred * lax.rsqrt(spread + 1e-06) * gain + shift


def lse_pair(earlier, later):
    maxima = jnp.maximum(earlier[0], later[0])
    totals = earlier[1] * jnp.exp(earlier[0] - maxima) + later[1] * jnp.exp(later[0] - maxima)
    return (maxima, totals)


def vocab_pair(earlier, later):
    return lse_pair(earlier[:2], later[:2]) + (earlier[2] + later[2],)


def place_rows(places, grads, seq_len):
    return jnp.zeros((seq_len, grads.shape[-1]), jnp.float32).at[places].add(grads)


def local(
    hidden_in,
    segments,
    mask_pos,
    target_ids,
    query_emb,
    doc_emb,
    qkv_weight,
    query_bias,
    value_bias,
    out_weight,
    out_bias,
    gain_one,
    shift_one,
    up_weight,
    up_bias,
    down_weight,
    down_bias,
    gain_two,
    shift_two,
    vocab,
):
    f32 = jnp.float32
    bf16 = jnp.bfloat16
    seq_count, _, seq_len, model_width = hidden_in.shape
    pair_count = mask_pos.shape[2]
    mask_count = mask_pos.shape[3]
    head_count = model_width // HEAD_DIM
    score_scale = 1.0 / math.sqrt(HEAD_DIM)
    split_shape = (seq_count, seq_len, head_count, HEAD_DIM)
    tokens = hidden_in.reshape(seq_count, seq_len, model_width)
    segs = segments.reshape(seq_count, seq_len)
    packed = jnp.einsum("nld,de->nle", tokens, qkv_weight, preferred_element_type=f32)
    queries = (packed[..., :model_width] + query_bias).astype(bf16).reshape(split_shape)
    key_rows = packed[..., model_width : 2 * model_width].astype(bf16).reshape(split_shape)
    value_rows = (packed[..., 2 * model_width :] + value_bias).astype(bf16).reshape(split_shape)
    same_seg = (segs[:, :, None] == segs[:, None, :])[:, None]
    raw_scores = jnp.einsum("nlhe,nmhe->nhlm", queries, key_rows, preferred_element_type=f32)

    def attend(scores_in):
        return jax.nn.softmax(jnp.where(same_seg, scores_in * score_scale, -1e30), axis=-1)

    probs, soft_back = jax.vjp(attend, raw_scores)
    probs_low = probs.astype(bf16)
    mixed_heads = jnp.einsum("nhlm,nmhe->nlhe", probs_low, value_rows, preferred_element_type=f32)
    mixed_low = mixed_heads.reshape(seq_count, seq_len, model_width).astype(bf16)
    attended = (
        jnp.einsum("nld,de->nle", mixed_low, out_weight, preferred_element_type=f32) + out_bias
    )
    first_norm, norm_back_one = jax.vjp(
        norm_rows, tokens.astype(f32) + attended, gain_one, shift_one
    )
    first_low = first_norm.astype(bf16)
    inner_act = (
        jnp.einsum("nld,df->nlf", first_low, up_weight, preferred_element_type=f32) + up_bias
    )
    active, gelu_back = jax.vjp(partial(jax.nn.gelu, approximate=False), inner_act)
    active_low = active.astype(bf16)
    second = (
        jnp.einsum("nlf,fd->nld", active_low, down_weight, preferred_element_type=f32) + down_bias
    )
    final_rows, norm_back_two = jax.vjp(norm_rows, first_norm + second, gain_two, shift_two)
    per_seq = pair_count * mask_count
    rows_dev = seq_count * per_seq
    flat_places = mask_pos.reshape(seq_count, per_seq)
    picked = jnp.take_along_axis(final_rows, flat_places[:, :, None], axis=1)
    picked_low = picked.reshape(rows_dev, model_width).astype(bf16)
    logits = lax.dot_general(
        lax.all_gather(picked_low, "batch", axis=0, tiled=True),
        vocab,
        (((1,), (1,)), ((), ())),
        preferred_element_type=f32,
    )
    shard_size = vocab.shape[0]
    vocab_ids = lax.axis_index("batch") * shard_size + lax.iota(jnp.int32, shard_size)
    is_target = target_ids.reshape(-1)[:, None] == vocab_ids[None, :]
    maxima = jnp.max(logits, 1)
    totals = jnp.sum(jnp.exp(logits - maxima[:, None]), 1)
    chosen = jnp.sum(jnp.where(is_target, logits, 0.0), 1)
    maxima, totals, chosen = combined_all((maxima, totals, chosen), "batch", vocab_pair)
    log_total = maxima + jnp.log(totals)
    first_own = lax.axis_index("batch") * rows_dev
    own_logp = lax.dynamic_slice_in_dim(chosen - log_total, first_own, rows_dev)
    reader = jnp.mean(own_logp.reshape(seq_count, pair_count, mask_count), -1)
    gathered_query = lax.all_gather(query_emb, "doc", axis=2, tiled=True)
    doc_rows = doc_emb.reshape(seq_count, pair_count, doc_emb.shape[-1])
    score = jnp.sum(gathered_query * doc_rows, -1)
    joint = score + reader
    unit_terms = jnp.ones_like(score)
    score_top, score_sum = combined_all((score, unit_terms), "doc", lse_pair)
    score_total = score_top + jnp.log(score_sum)
    shifted = joint - score_total
    joint_top, joint_sum = combined_all((shifted, unit_terms), "doc", lse_pair)
    joint_total = joint_top + jnp.log(joint_sum)
    loss = -joint_total
    weight_joint = jnp.exp(shifted - joint_total)
    weight_score = jnp.exp(score - score_total)
    score_grad = weight_score - weight_joint
    grad_query = lax.psum_scatter(
        score_grad[..., None] * doc_rows, "doc", scatter_dimension=2, tiled=True
    )
    row_scale = jnp.broadcast_to(
        (weight_joint / mask_count)[..., None], (seq_count, pair_count, mask_count)
    ).reshape(rows_dev)
    all_scale = lax.all_gather(row_scale, "batch", axis=0, tiled=True)
    vocab_probs = jnp.exp(logits - log_total[:, None])
    logit_grad = (all_scale[:, None] * (vocab_probs - is_target.astype(f32))).astype(bf16)
    picked_grad = lax.psum_scatter(
        jnp.dot(logit_grad, vocab, preferred_element_type=f32).astype(jnp.bfloat16),
        "batch",
        scatter_dimension=0,
        tiled=True,
    ).astype(jnp.float32)
    final_grad = jax.vmap(partial(place_rows, seq_len=seq_len))(
        flat_places, picked_grad.reshape(seq_count, per_seq, model_width)
    )
    sum_grad, grad_gain_two, grad_shift_two = norm_back_two(final_grad)
    grad_down_bias = jnp.sum(sum_grad, (0, 1))
    second_low = sum_grad.astype(bf16)
    grad_down_weight = jnp.einsum("nlf,nld->fd", active_low, second_low, preferred_element_type=f32)
    active_grad = jnp.einsum("nld,fd->nlf", second_low, down_weight, preferred_element_type=f32)
    (inner_grad,) = gelu_back(active_grad)
    grad_up_bias = jnp.sum(inner_grad, (0, 1))
    inner_low = inner_grad.astype(bf16)
    grad_up_weight = jnp.einsum("nld,nlf->df", first_low, inner_low, preferred_element_type=f32)
    first_grad = sum_grad + jnp.einsum(
        "nlf,df->nld", inner_low, up_weight, preferred_element_type=f32
    )
    resid_grad, grad_gain_one, grad_shift_one = norm_back_one(first_grad)
    grad_out_bias = jnp.sum(resid_grad, (0, 1))
    resid_low = resid_grad.astype(bf16)
    grad_out_weight = jnp.einsum("nld,nle->de", mixed_low, resid_low, preferred_element_type=f32)
    mixed_grad = (
        jnp.einsum("nle,de->nld", resid_low, out_weight, preferred_element_type=f32)
        .astype(bf16)
        .reshape(split_shape)
    )
    value_grad = jnp.einsum("nhlm,nlhe->nmhe", probs_low, mixed_grad, preferred_element_type=f32)
    prob_grad = jnp.einsum("nlhe,nmhe->nhlm", mixed_grad, value_rows, preferred_element_type=f32)
    (score_back,) = soft_back(prob_grad)
    score_low = score_back.astype(bf16)
    query_grad = jnp.einsum("nhlm,nmhe->nlhe", score_low, key_rows, preferred_element_type=f32)
    key_grad = jnp.einsum("nhlm,nlhe->nmhe", score_low, queries, preferred_element_type=f32)
    flat_shape = (seq_count, seq_len, model_width)
    query_grad = query_grad.reshape(flat_shape)
    key_grad = key_grad.reshape(flat_shape)
    value_grad = value_grad.reshape(flat_shape)
    grad_query_bias = jnp.sum(query_grad, (0, 1))
    grad_value_bias = jnp.sum(value_grad, (0, 1))
    packed_grad = jnp.concatenate([query_grad, key_grad, value_grad], -1).astype(bf16)
    grad_qkv_weight = jnp.einsum("nld,nle->de", tokens, packed_grad, preferred_element_type=f32)
    input_grad = resid_grad + jnp.einsum(
        "nle,de->nld", packed_grad, qkv_weight, preferred_element_type=f32
    )
    vectors = jnp.concatenate(
        [
            jnp.stack(
                [
                    grad_query_bias,
                    grad_value_bias,
                    grad_out_bias,
                    grad_gain_one,
                    grad_shift_one,
                    grad_down_bias,
                    grad_gain_two,
                    grad_shift_two,
                ]
            ),
            grad_up_bias.reshape(-1, model_width),
        ]
    )
    vectors = jnp.pad(vectors, ((0, -vectors.shape[0] % 16), (0, 0)))
    mats = (grad_down_weight, grad_up_weight, grad_out_weight, grad_qkv_weight)
    down_sum, up_sum, out_sum, qkv_sum, vector_sum = reduce_params(
        [m.astype(bf16) for m in mats], vectors, lax.axis_size("batch"), lax.axis_size("doc")
    )
    nb = lax.axis_size("batch")
    slot = lax.axis_index("batch")

    def share(v):
        return lax.dynamic_slice_in_dim(v, slot * (v.shape[0] // nb), v.shape[0] // nb)

    up_bias_sum = vector_sum[8 : 8 + grad_up_bias.shape[0] // model_width].reshape(-1)
    results = (
        qkv_sum.astype(f32),
        share(vector_sum[0]),
        share(vector_sum[1]),
        out_sum.astype(f32),
        share(vector_sum[2]),
        share(vector_sum[3]),
        share(vector_sum[4]),
        up_sum.astype(f32),
        share(up_bias_sum),
        down_sum.astype(f32),
        share(vector_sum[5]),
        share(vector_sum[6]),
        share(vector_sum[7]),
    )
    block_out = final_rows.astype(bf16).reshape(hidden_in.shape)
    grad_in = input_grad.astype(bf16).reshape(hidden_in.shape)
    return (
        block_out,
        loss,
        grad_in,
        grad_query,
        results[0],
        results[1],
        results[2],
        results[3],
        results[4],
        results[5],
        results[6],
        results[7],
        results[8],
        results[9],
        results[10],
        results[11],
        results[12],
    )


def solution(mesh):
    in_specs = (
        P("batch", "doc", None, None),
        P("batch", "doc", None),
        P("batch", "doc", None, None),
        P(),
        P("batch", None, "doc"),
        P("batch", "doc", None, None),
        P(),
        P(),
        P(),
        P(),
        P(),
        P(),
        P(),
        P(),
        P(),
        P(),
        P(),
        P(),
        P(),
        P("batch", None),
    )
    out_specs = (
        P("batch", "doc", None, None),
        P("batch", None),
        P("batch", "doc", None, None),
        P("batch", None, "doc"),
        P("batch", None),
        P("batch"),
        P("batch"),
        P("batch", None),
        P("batch"),
        P("batch"),
        P("batch"),
        P("batch", None),
        P("batch"),
        P("batch", None),
        P("batch"),
        P("batch"),
        P("batch"),
    )
    paired = dict(mesh.shape) == {"batch": 8, "doc": 4}
    return jax.shard_map(paired_local if paired else local, mesh=mesh, in_specs=in_specs, out_specs=out_specs, check_vma=False)
```
